32 devices in a mesh: img: 16 (over z, y, x), mlp: 2 (over core).
Axes of the slice: x: 2, y: 2, z: 4, core: 2. Of those that a mesh axis runs over, the one named last changes fastest.
Arguments:
- images: bfloat16 [160, 197, 768], P(('img', 'mlp')), may hold values from -13 to 13
- keep_mask: int32 [160, 197], P(('img', 'mlp')), may hold values from 0 to 1, as said below
- ln1_gain: float32 [768], replicated, may hold values from 0.5 to 1.5
- ln1_bias: float32 [768], replicated, may hold values from -3 to 3
- w_qkv: bfloat16 [768, 2304], replicated, may hold values from -0.21875 to 0.21875
- bias_q: bfloat16 [768], replicated, may hold values from -4 to 4
- bias_v: bfloat16 [768], replicated, may hold values from -0.75 to 0.75
- w_proj: bfloat16 [768, 768], replicated, may hold values from -1.5 to 1.5
- b_proj: bfloat16 [768], replicated, may hold values from -4 to 4
- ln2_gain: float32 [768], replicated, may hold values from 0.5 to 1.5
- ln2_bias: float32 [768], replicated, may hold values from -3 to 3
- w_fc1: bfloat16 [768, 3072], P(None, 'mlp'), may hold values from -0.21875 to 0.21875
- b_fc1: bfloat16 [3072], P('mlp'), may hold values from -4 to 4
- w_fc2: bfloat16 [3072, 768], P('mlp'), may hold values from -0.109375 to 0.109375
- b_fc2: bfloat16 [768], replicated, may hold values from -4 to 4
- cotangent: bfloat16 [160, 197, 768], P(('img', 'mlp')), may hold values from -6 to 6
Outputs:
- layer_out: bfloat16 [160, 197, 768], P(('img', 'mlp'))
- grad_images: float32 [160, 197, 768], P(('img', 'mlp'))
- grad_ln1_gain: float32 [768], replicated
- grad_ln1_bias: float32 [768], replicated
- grad_w_qkv: float32 [768, 2304], replicated
- grad_bias_q: float32 [768], replicated
- grad_bias_v: float32 [768], replicated
- grad_w_proj: float32 [768, 768], replicated
- grad_b_proj: float32 [768], replicated
- grad_ln2_gain: float32 [768], replicated
- grad_ln2_bias: float32 [768], replicated
- grad_w_fc1: float32 [768, 3072], P(None, 'mlp')
- grad_b_fc1: float32 [3072], P('mlp')
- grad_w_fc2: float32 [3072, 768], P('mlp')
- grad_b_fc2: float32 [768], replicated
- root_means: float32 [3], replicated
The draws below stay inside these ranges and needn't reach their ends.
Inputs may be any that keep to these rules, and one draw needn't show every extreme that they name: `keep_mask`: each image keeps between (201) // 5 and 157 of its patches, and both counts occur.
All inputs are finite; a program needn't handle non-finite values.
Results may differ from the reference program's by a relative error of at most 0.015.
Values may be sent and summed in bfloat16 or wider, within the bound.
A program may use at most 192 MiB of HBM per device.

```python
import jax
import jax.numpy as jnp
from jax import lax

D = 768
HEADS = 12
HEAD_DIM = 64
FF = 3072
PATCHES = 197
IMAGES = 160


def draw_images(key, part):
    place = jnp.arange(IMAGES, dtype=jnp.float32) / max(IMAGES - 1, 1)
    values = jax.random.truncated_normal(key, -5.0, 5.0, (IMAGES, PATCHES, D), jnp.float32)
    factor = 0.5 * jnp.exp(place * jnp.log(5.0))
    return (values * factor[:, None, None]).astype(jnp.bfloat16)


def draw_keep_mask(key, part):
    low_count = (PATCHES + 4) // 5
    high_count = 4 * PATCHES // 5
    spread = (high_count - low_count) // 8
    key_counts, key_order = jax.random.split(key)
    image_index = jnp.arange(IMAGES, dtype=jnp.int32)
    base_count = low_count + (high_count - low_count) * image_index // (IMAGES - 1)
    jitter = jax.random.randint(key_counts, (IMAGES,), -spread, spread + 1)
    counts = jnp.clip(base_count + jitter, low_count, high_count)
    counts = counts.at[0].set(low_count).at[IMAGES - 1].set(high_count)
    scores = jax.random.randint(key_order, (IMAGES, PATCHES), 0, 1 << 20)
    scores = scores * PATCHES + jnp.arange(PATCHES, dtype=jnp.int32)[None, :]
    rank_order = jnp.argsort(jnp.argsort(scores, axis=1), axis=1)
    return (rank_order < counts[:, None]).astype(jnp.int32)


def block_levels(key, shape, cuts, smallest, largest):
    loudness, own = 1.0, jax.random.fold_in(key, 6)
    for axis_at, blocks in cuts:
        draws = jnp.exp(jax.random.uniform(jax.random.fold_in(own, axis_at), (blocks,), jnp.float32, smallest / len(cuts), largest / len(cuts)))
        loudness = loudness * jnp.repeat(draws, shape[axis_at] // blocks).reshape([-1 if axis == axis_at else 1 for axis in range(len(shape))])
    return loudness


def bell_draw(rng, extent, width, reach, pieces=(), held_as=jnp.bfloat16):
    factor_of = block_levels(rng, extent, pieces, -0.22, 0.18) if pieces else 1.0
    values = jax.random.normal(rng, extent, jnp.float32) * width * factor_of
    return jnp.minimum(jnp.maximum(values, -reach), reach).astype(held_as)


def setup_inputs(seed: int = 0) -> dict:
    arg_keys = jax.random.split(jax.random.key(seed), 17)
    images = draw_images(jax.random.fold_in(arg_keys[16], 71), 0)
    keep_mask = draw_keep_mask(jax.random.fold_in(arg_keys[16], 71), 0)
    ln1_gain = jnp.clip(1.0 + 0.1 * jax.random.normal(arg_keys[2], (D,), jnp.float32), 0.5, 1.5)
    ln1_bias = bell_draw(arg_keys[3], (D,), 0.2, 3.0, (), jnp.float32)
    w_qkv = bell_draw(arg_keys[4], (D, 3 * D), D ** -0.5, 0.21875)
    bias_q = bell_draw(arg_keys[5], (D,), 0.3, 4.0)
    bias_v = bell_draw(arg_keys[6], (D,), 0.05, 0.75)
    w_proj = bell_draw(arg_keys[7], (D, D), (D // 48) ** -0.5, 1.5)
    b_proj = bell_draw(arg_keys[8], (D,), 0.3, 4.0)
    ln2_gain = jnp.clip(1.0 + 0.1 * jax.random.normal(arg_keys[9], (D,), jnp.float32), 0.5, 1.5)
    ln2_bias = bell_draw(arg_keys[10], (D,), 0.2, 3.0, (), jnp.float32)
    w_fc1 = bell_draw(arg_keys[11], (D, FF), D ** -0.5, 0.21875, ((1, 2),))
    b_fc1 = bell_draw(arg_keys[12], (FF,), 0.3, 4.0, ((0, 2),))
    w_fc2 = bell_draw(arg_keys[13], (FF, D), FF ** -0.5, 0.109375, ((0, 2),))
    b_fc2 = bell_draw(arg_keys[14], (D,), 0.3, 4.0)
    cotangent = bell_draw(arg_keys[15], (IMAGES, PATCHES, D), 1.0, 6.0, ((0, 32),))
    return dict(images=images, keep_mask=keep_mask, ln1_gain=ln1_gain, ln1_bias=ln1_bias, w_qkv=w_qkv, bias_q=bias_q, bias_v=bias_v, w_proj=w_proj, b_proj=b_proj, ln2_gain=ln2_gain, ln2_bias=ln2_bias, w_fc1=w_fc1, b_fc1=b_fc1, w_fc2=w_fc2, b_fc2=b_fc2, cotangent=cotangent)


@jax.custom_vjp
def low(v):
    return lax.optimization_barrier(v.astype(jnp.bfloat16)).astype(jnp.float32)

@jax.custom_vjp
def low_back(v):
    return v

def low_keep(v):
    return (low(v), None)

def low_pass(kept, grad):
    return (grad,)

def back_keep(v):
    return (v, None)

def back_low(kept, grad):
    return (low(grad),)
low.defvjp(low_keep, low_pass)
low_back.defvjp(back_keep, back_low)
NORM_EPS = 1e-06

def product(left_side, right_side):
    return jnp.dot(left_side, right_side, precision=lax.Precision.HIGHEST)

def layer_norm(input_rows, norm_gain, norm_shift):
    center = input_rows - lax.optimization_barrier(jnp.mean(input_rows, axis=1, keepdims=True))
    variance = lax.optimization_barrier(jnp.mean(center * center, axis=1, keepdims=True))
    return center * lax.rsqrt(variance + NORM_EPS) * norm_gain + norm_shift

def block_forward(params, pictures, keep_rows):
    ln1_gain, ln1_bias, w_qkv, bias_q, bias_v, w_proj, b_proj, ln2_gain, ln2_bias, w_fc1, b_fc1, w_fc2, b_fc2 = params
    image_count = pictures.shape[0]
    total_rows = image_count * PATCHES
    input_rows = pictures.reshape(total_rows, D)
    keep_column = keep_rows.reshape(total_rows, 1)
    normed = low(layer_norm(input_rows, ln1_gain, ln1_bias))
    projected = product(normed, w_qkv)
    head_shape = (image_count, PATCHES, HEADS, HEAD_DIM)
    query_heads = low(low_back(projected[:, :D] + bias_q)).reshape(head_shape)
    key_heads = low(low_back(projected[:, D:2 * D])).reshape(head_shape)
    value_heads = low(low_back(projected[:, 2 * D:] + bias_v)).reshape(head_shape)
    raw_scores = jnp.einsum('gqhe,gkhe->ghqk', query_heads, key_heads, precision=lax.Precision.HIGHEST)
    scores = low_back(raw_scores * HEAD_DIM ** (-0.5))
    scores = jnp.where(keep_rows[:, None, None, :] > 0, scores, -1e+30)
    row_peak = lax.optimization_barrier(jnp.max(scores, axis=3, keepdims=True))
    raised = jnp.exp(scores - row_peak)
    softmax_weights = low(low_back(raised / lax.optimization_barrier(jnp.sum(raised, axis=3, keepdims=True))))
    attended = jnp.einsum('ghqk,gkhe->gqhe', softmax_weights, value_heads, precision=lax.Precision.HIGHEST)
    attended = low(low_back(attended.reshape(total_rows, D)))
    attn_out = product(attended, w_proj) + b_proj
    middle = input_rows + keep_column * low_back(attn_out)
    hidden_in = low(layer_norm(middle, ln2_gain, ln2_bias))
    pre_act = low_back(product(hidden_in, w_fc1) + b_fc1)
    activation = low(low_back(jax.nn.gelu(pre_act, approximate=False)))
    mlp_out = product(activation, w_fc2) + b_fc2
    block_output = middle + keep_column * low_back(mlp_out)
    stat_sums = jnp.stack([jnp.sum(keep_column * block_output * block_output), jnp.sum(keep_column * attn_out * attn_out), jnp.sum(keep_column * mlp_out * mlp_out), jnp.sum(keep_column)])
    return (block_output.reshape(image_count, PATCHES, D), stat_sums)

def reference(images, keep_mask, ln1_gain, ln1_bias, w_qkv, bias_q, bias_v, w_proj, b_proj, ln2_gain, ln2_bias, w_fc1, b_fc1, w_fc2, b_fc2, cotangent):
    params = tuple((weight.astype(jnp.float32) for weight in (ln1_gain, ln1_bias, w_qkv, bias_q, bias_v, w_proj, b_proj, ln2_gain, ln2_bias, w_fc1, b_fc1, w_fc2, b_fc2)))
    group_size = max((candidate for candidate in range(1, 21) if IMAGES % candidate == 0))
    block_count = IMAGES // group_size
    image_blocks = images.astype(jnp.float32).reshape(block_count, group_size, PATCHES, D)
    keep_blocks = keep_mask.astype(jnp.float32).reshape(block_count, group_size, PATCHES)
    cot_blocks = cotangent.astype(jnp.float32).reshape(block_count, group_size, PATCHES, D)

    def advance(totals, inputs):
        block_images, block_keep, block_cot = inputs

        def forward(weights, pictures):
            return block_forward(weights, pictures, block_keep)
        block_output, pullback, stat_sums = jax.vjp(forward, params, block_images, has_aux=True)
        grad_weights, grad_pictures = pullback(block_cot)
        grad_totals, stat_totals = totals
        updated = (jax.tree.map(jnp.add, grad_totals, grad_weights), stat_totals + stat_sums)
        return (updated, (block_output, grad_pictures))
    initial = (jax.tree.map(jnp.zeros_like, params), jnp.zeros((4,), jnp.float32))
    (grad_totals, stat_totals), (outputs, grad_blocks) = lax.scan(advance, initial, (image_blocks, keep_blocks, cot_blocks))
    layer_out = outputs.reshape(IMAGES, PATCHES, D).astype(jnp.bfloat16)
    grad_images = grad_blocks.reshape(IMAGES, PATCHES, D)
    root_means = jnp.sqrt(stat_totals[:3] / (stat_totals[3] * D))
    g_ln1_gain, g_ln1_bias, g_w_qkv, g_bias_q, g_bias_v, g_w_proj, g_b_proj, g_ln2_gain, g_ln2_bias, g_w_fc1, g_b_fc1, g_w_fc2, g_b_fc2 = grad_totals
    return (layer_out, grad_images, g_ln1_gain, g_ln1_bias, g_w_qkv, g_bias_q, g_bias_v, g_w_proj, g_b_proj, g_ln2_gain, g_ln2_bias, g_w_fc1, g_b_fc1, g_w_fc2, g_b_fc2, root_means)
```

```python
import functools

import jax
import jax.numpy as jnp
from jax import lax
from jax.experimental import pallas as pl
from jax.experimental.pallas import tpu as pltpu
from jax.sharding import PartitionSpec as P

HEAD_DIM = 64
NORM_EPS = 1e-06
F32 = jnp.float32
BF16 = jnp.bfloat16
ERFC_POLY = (
    -0.05792342897865154,
    0.27982426175045266,
    -0.47905523971588865,
    0.27061712140601424,
    -0.022718349995155727,
    0.2015184791612061,
    0.24328701077158832,
    0.2823637910445855,
    0.2820864086305586,
)


def dot(a, b):
    return jnp.dot(a, b, preferred_element_type=F32)


def dot_t(a, b):
    return lax.dot_general(a, b, (((1,), (1,)), ((), ())), preferred_element_type=F32)


def t_dot(a, b):
    return lax.dot_general(a, b, (((0,), (0,)), ((), ())), preferred_element_type=F32)


def slots_of(patches):
    most = 4 * patches // 5
    return -(-most // 16) * 16


def norm_rows(rows):
    center = rows - jnp.mean(rows, axis=1, keepdims=True)
    inverse = lax.rsqrt(jnp.mean(center * center, axis=1, keepdims=True) + NORM_EPS)
    return center * inverse, inverse


def norm_back(weighted, scaled, inverse):
    return inverse * (
        weighted
        - jnp.mean(weighted, axis=1, keepdims=True)
        - scaled * jnp.mean(weighted * scaled, axis=1, keepdims=True)
    )


def gelu_pair(values):
    reach = jnp.abs(values) * 0.7071067811865476
    inv = 1.0 / (1.0 + 0.5 * reach)
    decay = jnp.exp(-0.5 * (values * values))
    poly = jnp.full_like(values, ERFC_POLY[0])
    for coefficient in ERFC_POLY[1:]:
        poly = poly * inv + coefficient
    tail = (0.5 * inv) * poly * decay
    share = jnp.where(values > 0, 1.0 - tail, tail)
    return values * share, share + values * (decay * 0.3989422804014327)


def forward_kernel(
    slots,
    keep_ref, img_ref, cot_ref, g1_ref, b1_ref, wqkv_ref, bq_ref, bv_ref, wproj_ref, bproj_ref, g2_ref, b2_ref,
    sel_ref, x_ref, normed_ref, qkv_ref, probs_ref, att_ref, mid_ref, hid_ref, gm_ref, sums_ref,
):
    patches, width = img_ref.shape[1:]
    heads = width // HEAD_DIM
    keep = keep_ref[0].astype(F32)
    upto = lax.broadcasted_iota(jnp.int32, (patches, patches), 0) <= lax.broadcasted_iota(
        jnp.int32, (patches, patches), 1
    )
    keep8 = jnp.broadcast_to(keep, (8, patches)).astype(BF16)
    rank = dot(keep8, upto.astype(F32).astype(BF16))[0:1]
    count = jnp.sum(keep, axis=1, keepdims=True)
    slot = lax.broadcasted_iota(jnp.int32, (slots, patches), 0).astype(F32)
    sel = jnp.where((slot == rank - 1.0) & (keep > 0), 1.0, 0.0).astype(BF16)
    sel_ref[0] = sel
    gm_ref[...] = dot(sel, cot_ref[0]).astype(BF16)
    rows = dot(sel, img_ref[0])
    x_ref[...] = rows.astype(BF16)
    scaled, _ = norm_rows(rows)
    normed = (scaled * g1_ref[...] + b1_ref[...]).astype(BF16)
    normed_ref[...] = normed
    for part in range(3):
        cols = slice(part * width, (part + 1) * width)
        block = dot(normed, wqkv_ref[:, cols])
        if part == 0:
            block = block + bq_ref[...].astype(F32)
        if part == 2:
            block = block + bv_ref[...].astype(F32)
        qkv_ref[:, cols] = block.astype(BF16)
    closed = jnp.where(
        lax.broadcasted_iota(jnp.int32, (1, slots), 1).astype(F32) < count, 0.0, -1e30
    )
    first = lax.broadcasted_iota(jnp.int32, (1, 2 * HEAD_DIM), 1) < HEAD_DIM
    zero = jnp.zeros((), BF16)
    for pair in range(heads // 2):
        lanes = slice(pair * 128, pair * 128 + 128)
        query = qkv_ref[:, lanes] * jnp.asarray(HEAD_DIM ** -0.5, BF16)
        key = qkv_ref[:, width + pair * 128 : width + pair * 128 + 128]
        value = qkv_ref[:, 2 * width + pair * 128 : 2 * width + pair * 128 + 128]
        total = None
        for half in range(2):
            mine = first if half == 0 else jnp.logical_not(first)
            scores = dot_t(query, jnp.where(mine, key, zero)) + closed
            raised = jnp.exp(scores - jnp.max(scores, axis=1, keepdims=True))
            probs = (raised * (1.0 / jnp.sum(raised, axis=1, keepdims=True))).astype(BF16)
            probs_ref[0, 2 * pair + half] = probs
            term = dot(probs, jnp.where(mine, value, zero))
            total = term if total is None else total + term
        att_ref[:, lanes] = total.astype(BF16)
    attn_out = dot(att_ref[...], wproj_ref[...]) + bproj_ref[...].astype(F32)
    valid = lax.broadcasted_iota(jnp.int32, (slots, 1), 0).astype(F32) < count
    attn_kept = jnp.where(valid, attn_out, 0.0)
    middle = rows + attn_kept
    mid_ref[...] = middle
    sums_ref[0, 0:1] = jnp.sum(attn_kept * attn_kept, axis=0, keepdims=True)
    sums_ref[0, 1:2] = jnp.broadcast_to(count, (1, width))
    scaled, _ = norm_rows(middle)
    hid_ref[...] = (scaled * g2_ref[...] + b2_ref[...]).astype(BF16)


def mlp_kernel(hid_ref, gm_ref, w1_ref, b1_ref, w2_ref, out_ref, gh_ref, dw1_ref, dw2_ref, db1_ref):
    step = pl.program_id(0)
    hid, gm = hid_ref[...], gm_ref[...]
    w1, w2 = w1_ref[0], w2_ref[0]
    pre = dot(hid, w1) + b1_ref[0].astype(F32)
    act, slope = gelu_pair(pre)
    act = act.astype(BF16)
    grad_act = dot_t(gm, w2).astype(BF16).astype(F32)
    grad_pre_f = grad_act * slope
    grad_pre = grad_pre_f.astype(BF16)
    dw2_ref[0] = t_dot(act, gm).astype(BF16)
    dw1_ref[0] = t_dot(hid, grad_pre).astype(BF16)
    db1_ref[0] = jnp.sum(grad_pre.astype(F32), axis=0, keepdims=True)

    @pl.when(step == 0)
    def _():
        out_ref[...] = dot(act, w2)
        gh_ref[...] = dot_t(grad_pre, w1)

    @pl.when(step > 0)
    def _():
        out_ref[...] += dot(act, w2)
        gh_ref[...] += dot_t(grad_pre, w1)


def backward_kernel(
    images, slots, groups,
    sel_ref, x_ref, normed_ref, qkv_ref, probs_ref, att_ref, mid_ref, gm_ref, gh_ref, mlp_ref, valid_ref,
    g1_ref, g2_ref, bfc2_ref, wqkv_ref, wproj_ref, img_ref, cot_ref,
    lo_ref, gi_ref, dwp_ref, dwq_ref, vec_ref,
    gmid_ref, gatt_ref, gq_ref, gk_ref, gv_ref, gn_ref,
):
    step = pl.program_id(0)
    rows, width = x_ref.shape

    @pl.when(step == 0)
    def _():
        middle = mid_ref[...]
        valid = valid_ref[...] > 0
        mlp_out = jnp.where(valid, mlp_ref[...] + bfc2_ref[...].astype(F32), 0.0)
        block = middle + mlp_out
        kept = jnp.where(valid, block, 0.0)
        vec_ref[8:9] = jnp.sum(kept * kept, axis=0, keepdims=True)
        vec_ref[9:10] = jnp.sum(mlp_out * mlp_out, axis=0, keepdims=True)
        low = block.astype(BF16)
        for i in range(images):
            put = t_dot(sel_ref[i], low[i * slots : (i + 1) * slots])
            here = jnp.sum(sel_ref[i].astype(F32), axis=0, keepdims=True)
            lo_ref[i] = put.astype(BF16)
        scaled, inverse = norm_rows(middle)
        grad_hidden = gh_ref[...]
        vec_ref[0:1] = jnp.sum(grad_hidden * scaled, axis=0, keepdims=True)
        vec_ref[1:2] = jnp.sum(grad_hidden, axis=0, keepdims=True)
        gm = gm_ref[...].astype(F32)
        vec_ref[2:3] = jnp.sum(gm, axis=0, keepdims=True)
        grad_middle = gm + norm_back(grad_hidden * g2_ref[...], scaled, inverse)
        gmid_ref[...] = grad_middle
        grad_attn = grad_middle.astype(BF16)
        vec_ref[3:4] = jnp.sum(grad_attn.astype(F32), axis=0, keepdims=True)
        dwp_ref[...] = t_dot(att_ref[...], grad_attn).astype(BF16)
        gatt_ref[...] = dot_t(grad_attn, wproj_ref[...]).astype(BF16)
        gn_ref[...] = jnp.zeros_like(gn_ref)

    first = lax.broadcasted_iota(jnp.int32, (1, 2 * HEAD_DIM), 1) < HEAD_DIM
    zero = jnp.zeros((), BF16)
    scale = jnp.asarray(HEAD_DIM ** -0.5, BF16)
    pairs = width // 128 // groups
    for group in range(groups):

        @pl.when(step == group + 1)
        def _():
            base = group * pairs * 128

            @pl.loop(0, images)
            def _(i):
                here = pl.ds(pl.multiple_of(i * slots, 16), slots)
                for pair in range(pairs):
                    at = base + pair * 128
                    own = slice(pair * 128, pair * 128 + 128)
                    query = qkv_ref[here, at : at + 128]
                    key = qkv_ref[here, width + at : width + at + 128]
                    value = qkv_ref[here, 2 * width + at : 2 * width + at + 128]
                    grad_att = gatt_ref[here, at : at + 128]
                    gq = gk = gv = None
                    for half in range(2):
                        mine = first if half == 0 else jnp.logical_not(first)
                        low = probs_ref[i, 2 * (base // 128 + pair) + half]
                        probs = low.astype(F32)
                        g_mine = jnp.where(mine, grad_att, zero)
                        grad_probs = dot_t(g_mine, value).astype(BF16).astype(F32)
                        inner = jnp.sum(probs * grad_probs, axis=1, keepdims=True)
                        grad_scores = (probs * (grad_probs - inner)).astype(BF16) * scale
                        tv = t_dot(low, g_mine)
                        tq = dot(grad_scores, jnp.where(mine, key, zero))
                        tk = t_dot(grad_scores, jnp.where(mine, query, zero))
                        gq = tq if gq is None else gq + tq
                        gk = tk if gk is None else gk + tk
                        gv = tv if gv is None else gv + tv
                    gq_ref[here, own] = gq.astype(BF16)
                    gk_ref[here, own] = gk.astype(BF16)
                    gv_ref[here, own] = gv.astype(BF16)

            span = pairs * 128
            vec_ref[4:5, base : base + span] = jnp.sum(gq_ref[...].astype(F32), axis=0, keepdims=True)
            vec_ref[5:6, base : base + span] = jnp.sum(gv_ref[...].astype(F32), axis=0, keepdims=True)
            for part, ref in enumerate((gq_ref, gk_ref, gv_ref)):
                cols = slice(part * width + base, part * width + base + span)
                dwq_ref[:, cols] = t_dot(normed_ref[...], ref[...]).astype(BF16)
                gn_ref[...] += dot_t(ref[...], wqkv_ref[:, cols])

    @pl.when(step == groups + 1)
    def _():
        scaled, inverse = norm_rows(x_ref[...].astype(F32))
        grad_normed = gn_ref[...]
        vec_ref[6:7] = jnp.sum(grad_normed * scaled, axis=0, keepdims=True)
        vec_ref[7:8] = jnp.sum(grad_normed, axis=0, keepdims=True)
        change = gmid_ref[...] + norm_back(grad_normed * g1_ref[...], scaled, inverse)
        high = change.astype(BF16)
        rest = (change - high.astype(F32)).astype(BF16)
        for i in range(images):
            here = slice(i * slots, (i + 1) * slots)
            gi_ref[i] = t_dot(sel_ref[i], high[here]) + t_dot(sel_ref[i], rest[here])


def whole(shape):
    return pl.BlockSpec(shape, lambda *_: (0,) * len(shape), pipeline_mode=pl.Buffered(1))


def on_device(
    images, keep_mask, ln1_gain, ln1_bias, w_qkv, bias_q, bias_v, w_proj, b_proj,
    ln2_gain, ln2_bias, w_fc1, b_fc1, w_fc2, b_fc2, cotangent,
):
    count, patches, width = images.shape
    slots = slots_of(patches)
    rows = count * slots
    heads = width // HEAD_DIM
    shard = w_fc1.shape[1]
    row = lambda v: v.reshape(1, -1)
    whole_w1 = lax.all_gather(w_fc1, "mlp")
    whole_w2 = lax.all_gather(w_fc2, "mlp")
    whole_b1 = lax.all_gather(b_fc1, "mlp").reshape(2, 1, shard)
    shape = jax.ShapeDtypeStruct
    limit = pltpu.CompilerParams(vmem_limit_bytes=60 * 2**20)
    per_image = lambda *tail: pl.BlockSpec((1,) + tail, lambda i: (i,) + (0,) * len(tail))
    per_rows = lambda cols: pl.BlockSpec((slots, cols), lambda i: (i, 0))
    sel, x, normed, qkv, probs, att, mid, hid, gm, sums = pl.pallas_call(
        functools.partial(forward_kernel, slots),
        grid=(count,),
        out_shape=(
            shape((count, slots, patches), BF16),
            shape((rows, width), BF16),
            shape((rows, width), BF16),
            shape((rows, 3 * width), BF16),
            shape((count, heads, slots, slots), BF16),
            shape((rows, width), BF16),
            shape((rows, width), F32),
            shape((rows, width), BF16),
            shape((rows, width), BF16),
            shape((count, 8, width), F32),
        ),
        in_specs=[
            per_image(1, patches), per_image(patches, width), per_image(patches, width),
            whole((1, width)), whole((1, width)), whole((width, 3 * width)), whole((1, width)), whole((1, width)),
            whole((width, width)), whole((1, width)), whole((1, width)), whole((1, width)),
        ],
        out_specs=(
            per_image(slots, patches), per_rows(width), per_rows(width), per_rows(3 * width),
            per_image(heads, slots, slots), per_rows(width), per_rows(width), per_rows(width), per_rows(width),
            per_image(8, width),
        ),
        compiler_params=limit,
        name="attention_forward",
    )(
        keep_mask.reshape(count, 1, patches), images, cotangent, row(ln1_gain), row(ln1_bias), w_qkv,
        row(bias_q), row(bias_v), w_proj, row(b_proj), row(ln2_gain), row(ln2_bias),
    )
    chunk = 512 if shard % 512 == 0 else 256
    each = shard // chunk
    mlp_out, grad_hidden, dw1, dw2, db1 = pl.pallas_call(
        mlp_kernel,
        grid=(2 * each,),
        out_shape=(
            shape((rows, width), F32), shape((rows, width), F32),
            shape((2, width, shard), BF16), shape((2, shard, width), BF16), shape((2, 1, shard), F32),
        ),
        in_specs=[
            whole((rows, width)), whole((rows, width)),
            pl.BlockSpec((1, width, chunk), lambda c: (c // each, 0, c % each)),
            pl.BlockSpec((1, 1, chunk), lambda c: (c // each, 0, c % each)),
            pl.BlockSpec((1, chunk, width), lambda c: (c // each, c % each, 0)),
        ],
        out_specs=(
            whole((rows, width)), whole((rows, width)),
            pl.BlockSpec((1, width, chunk), lambda c: (c // each, 0, c % each)),
            pl.BlockSpec((1, chunk, width), lambda c: (c // each, c % each, 0)),
            pl.BlockSpec((1, 1, chunk), lambda c: (c // each, 0, c % each)),
        ),
        compiler_params=limit,
        name="mlp_both_ways",
    )(hid, gm, whole_w1, whole_b1, whole_w2)
    kept = jnp.sum(keep_mask, axis=1, keepdims=True)
    valid = (jnp.arange(slots, dtype=jnp.int32)[None, :] < kept).astype(F32).reshape(rows, 1)
    groups = 3
    span = width // groups
    low, put, dwp, dwq, vec = pl.pallas_call(
        functools.partial(backward_kernel, count, slots, groups),
        grid=(groups + 2,),
        out_shape=(
            shape((count, patches, width), BF16), shape((count, patches, width), F32),
            shape((width, width), BF16), shape((width, 3 * width), BF16), shape((16, width), F32),
        ),
        in_specs=[
            whole((count, slots, patches)), whole((rows, width)), whole((rows, width)), whole((rows, 3 * width)),
            whole((count, heads, slots, slots)), whole((rows, width)), whole((rows, width)), whole((rows, width)),
            whole((rows, width)), whole((rows, width)), whole((rows, 1)),
            whole((1, width)), whole((1, width)), whole((1, width)), whole((width, 3 * width)), whole((width, width)),
            pl.BlockSpec(memory_space=pl.ANY), pl.BlockSpec(memory_space=pl.ANY),
        ],
        out_specs=(
            whole((count, patches, width)), whole((count, patches, width)),
            whole((width, width)), whole((width, 3 * width)), whole((16, width)),
        ),
        scratch_shapes=[
            pltpu.VMEM((rows, width), F32), pltpu.VMEM((rows, width), BF16),
            pltpu.VMEM((rows, span), BF16), pltpu.VMEM((rows, span), BF16), pltpu.VMEM((rows, span), BF16),
            pltpu.VMEM((rows, width), F32),
        ],
        compiler_params=limit,
        name="attention_backward",
    )(
        sel, x, normed, qkv, probs, att, mid, gm, grad_hidden, mlp_out, valid,
        row(ln1_gain), row(ln2_gain), row(b_fc2), w_qkv, w_proj, images, cotangent,
    )
    kept_at = (keep_mask > 0)[:, :, None]
    layer_out = jnp.where(kept_at, low, images)
    grad_images = jnp.where(kept_at, put, cotangent.astype(F32))
    both = ("img", "mlp")
    place = lax.axis_index("mlp")
    dw1s = lax.psum_scatter(dw1.reshape(2 * width, shard), "mlp", scatter_dimension=0, tiled=True)
    dw2s = lax.psum_scatter(dw2.reshape(2 * shard, width), "mlp", scatter_dimension=0, tiled=True)
    s_w1, s_w2 = lax.psum((dw1s, dw2s), "img")
    s_wq, s_wp = lax.psum((dwq, dwp), both)
    vec, sums, s_b1 = lax.psum((vec, jnp.sum(sums, axis=0), db1.reshape(2, shard)), both)
    s_b1 = lax.dynamic_index_in_dim(s_b1, place, 0, keepdims=False)
    stream_sq, mlp_sq, attn_sq = jnp.sum(vec[8]), jnp.sum(vec[9]), jnp.sum(sums[0])
    root_means = jnp.sqrt(jnp.stack([stream_sq, attn_sq, mlp_sq]) / (sums[1, 0] * width))
    f = lambda v: v.astype(F32)
    return (
        layer_out, grad_images, vec[6], vec[7], f(s_wq), vec[4], vec[5], f(s_wp), vec[3], vec[0], vec[1],
        f(s_w1), s_b1, f(s_w2), vec[2], root_means,
    )


def solution(mesh):
    rows, line = P(("img", "mlp"), None, None), P(("img", "mlp"), None)
    return jax.shard_map(
        on_device,
        mesh=mesh,
        in_specs=(
            rows, line, P(), P(), P(), P(), P(), P(), P(), P(), P(),
            P(None, "mlp"), P("mlp"), P("mlp", None), P(), rows,
        ),
        out_specs=(
            rows, rows, P(), P(), P(), P(), P(), P(), P(), P(), P(),
            P(None, "mlp"), P("mlp"), P("mlp", None), P(), P(),
        ),
        check_vma=False,
    )
```

```python
import functools

import jax
import jax.numpy as jnp
from jax import lax
from jax.experimental import pallas as pl
from jax.experimental.pallas import tpu as pltpu
from jax.sharding import PartitionSpec as P

HEAD_DIM = 64
NORM_EPS = 1e-06
F32 = jnp.float32
BF16 = jnp.bfloat16
MESH = pl.DeviceIdType.MESH
ERFC_POLY = (
    -0.05792342897865154,
    0.27982426175045266,
    -0.47905523971588865,
    0.27061712140601424,
    -0.022718349995155727,
    0.2015184791612061,
    0.24328701077158832,
    0.2823637910445855,
    0.2820864086305586,
)


def dot(a, b):
    return jnp.dot(a, b, preferred_element_type=F32)


def dot_t(a, b):
    return lax.dot_general(a, b, (((1,), (1,)), ((), ())), preferred_element_type=F32)


def t_dot(a, b):
    return lax.dot_general(a, b, (((0,), (0,)), ((), ())), preferred_element_type=F32)


def slots_of(patches):
    most = 4 * patches // 5
    return -(-most // 16) * 16


def norm_rows(rows):
    center = rows - jnp.mean(rows, axis=1, keepdims=True)
    inverse = lax.rsqrt(jnp.mean(center * center, axis=1, keepdims=True) + NORM_EPS)
    return center * inverse, inverse


def norm_back(weighted, scaled, inverse):
    return inverse * (
        weighted
        - jnp.mean(weighted, axis=1, keepdims=True)
        - scaled * jnp.mean(weighted * scaled, axis=1, keepdims=True)
    )


def gelu_pair(values):
    reach = jnp.abs(values) * 0.7071067811865476
    inv = 1.0 / (1.0 + 0.5 * reach)
    decay = jnp.exp(-0.5 * (values * values))
    poly = jnp.full_like(values, ERFC_POLY[0])
    for coefficient in ERFC_POLY[1:]:
        poly = poly * inv + coefficient
    tail = (0.5 * inv) * poly * decay
    share = jnp.where(values > 0, 1.0 - tail, tail)
    return values * share, share + values * (decay * 0.3989422804014327)


def swap_weights(ours, theirs, send_sem, recv_sem):
    other = {"mlp": 1 - lax.axis_index("mlp")}
    copies = [
        pltpu.make_async_remote_copy(
            src_ref=ours[j], dst_ref=theirs[j], send_sem=send_sem.at[j], recv_sem=recv_sem.at[j],
            device_id=other, device_id_type=MESH,
        )
        for j in range(len(ours))
    ]

    def trade(begin):
        @pl.when(pl.program_id(0) == (0 if begin else pl.num_programs(0) - 1))
        def _():
            if begin:
                barrier = pltpu.get_barrier_semaphore()
                pl.semaphore_signal(barrier, inc=1, device_id=other, device_id_type=MESH)
                pl.semaphore_wait(barrier, 1)
            for copy in copies:
                if begin:
                    copy.start()
                else:
                    copy.wait()

    return trade


def forward_kernel(
    slots, exchange,
    keep_ref, img_ref, cot_ref, g1_ref, b1_ref, wqkv_ref, bq_ref, bv_ref, wproj_ref, bproj_ref, g2_ref, b2_ref,
    *refs,
):
    if exchange:
        ours, refs, (send_sem, recv_sem) = refs[:3], refs[3:-2], refs[-2:]
        theirs, refs = refs[-3:], refs[:-3]
        trade = swap_weights(ours, theirs, send_sem, recv_sem)
        trade(True)
    sel_ref, x_ref, normed_ref, qkv_ref, probs_ref, att_ref, mid_ref, hid_ref, gm_ref, sums_ref = refs
    patches, width = img_ref.shape[1:]
    heads = width // HEAD_DIM
    keep = keep_ref[0].astype(F32)
    upto = lax.broadcasted_iota(jnp.int32, (patches, patches), 0) <= lax.broadcasted_iota(
        jnp.int32, (patches, patches), 1
    )
    keep8 = jnp.broadcast_to(keep, (8, patches)).astype(BF16)
    rank = dot(keep8, upto.astype(F32).astype(BF16))[0:1]
    count = jnp.sum(keep, axis=1, keepdims=True)
    slot = lax.broadcasted_iota(jnp.int32, (slots, patches), 0).astype(F32)
    sel = jnp.where((slot == rank - 1.0) & (keep > 0), 1.0, 0.0).astype(BF16)
    sel_ref[0] = sel
    gm_ref[...] = dot(sel, cot_ref[0]).astype(BF16)
    rows = dot(sel, img_ref[0])
    x_ref[...] = rows.astype(BF16)
    scaled, _ = norm_rows(rows)
    normed = (scaled * g1_ref[...] + b1_ref[...]).astype(BF16)
    normed_ref[...] = normed
    for part in range(3):
        cols = slice(part * width, (part + 1) * width)
        block = dot(normed, wqkv_ref[:, cols])
        if part == 0:
            block = block + bq_ref[...].astype(F32)
        if part == 2:
            block = block + bv_ref[...].astype(F32)
        qkv_ref[:, cols] = block.astype(BF16)
    closed = jnp.where(
        lax.broadcasted_iota(jnp.int32, (1, slots), 1).astype(F32) < count, 0.0, -1e30
    )
    first = lax.broadcasted_iota(jnp.int32, (1, 2 * HEAD_DIM), 1) < HEAD_DIM
    zero = jnp.zeros((), BF16)
    for pair in range(heads // 2):
        lanes = slice(pair * 128, pair * 128 + 128)
        query = qkv_ref[:, lanes] * jnp.asarray(HEAD_DIM ** -0.5, BF16)
        key = qkv_ref[:, width + pair * 128 : width + pair * 128 + 128]
        value = qkv_ref[:, 2 * width + pair * 128 : 2 * width + pair * 128 + 128]
        total = None
        for half in range(2):
            mine = first if half == 0 else jnp.logical_not(first)
            scores = dot_t(query, jnp.where(mine, key, zero)) + closed
            raised = jnp.exp(scores - jnp.max(scores, axis=1, keepdims=True))
            probs = (raised * (1.0 / jnp.sum(raised, axis=1, keepdims=True))).astype(BF16)
            probs_ref[0, 2 * pair + half] = probs
            term = dot(probs, jnp.where(mine, value, zero))
            total = term if total is None else total + term
        att_ref[:, lanes] = total.astype(BF16)
    attn_out = dot(att_ref[...], wproj_ref[...]) + bproj_ref[...].astype(F32)
    valid = lax.broadcasted_iota(jnp.int32, (slots, 1), 0).astype(F32) < count
    attn_kept = jnp.where(valid, attn_out, 0.0)
    middle = rows + attn_kept
    mid_ref[...] = middle
    sums_ref[0, 0:1] = jnp.sum(attn_kept * attn_kept, axis=0, keepdims=True)
    sums_ref[0, 1:2] = jnp.broadcast_to(count, (1, width))
    scaled, _ = norm_rows(middle)
    hid_ref[...] = (scaled * g2_ref[...] + b2_ref[...]).astype(BF16)
    if exchange:
        trade(False)


def mlp_kernel(hid_ref, gm_ref, w1_ref, b1_ref, w2_ref, out_ref, gh_ref, dw1_ref, dw2_ref, db1_ref):
    step = pl.program_id(0)
    hid, gm = hid_ref[...], gm_ref[...]
    w1, w2 = w1_ref[0], w2_ref[0]
    pre = dot(hid, w1) + b1_ref[0].astype(F32)
    act, slope = gelu_pair(pre)
    act = act.astype(BF16)
    grad_act = dot_t(gm, w2).astype(BF16).astype(F32)
    grad_pre_f = grad_act * slope
    grad_pre = grad_pre_f.astype(BF16)
    dw2_ref[0] = t_dot(act, gm).astype(BF16)
    dw1_ref[0] = t_dot(hid, grad_pre).astype(BF16)
    db1_ref[0] = jnp.sum(grad_pre.astype(F32), axis=0, keepdims=True)

    @pl.when(step == 0)
    def _():
        out_ref[...] = dot(act, w2)
        gh_ref[...] = dot_t(grad_pre, w1)

    @pl.when(step > 0)
    def _():
        out_ref[...] += dot(act, w2)
        gh_ref[...] += dot_t(grad_pre, w1)


def backward_kernel(
    images, slots, groups,
    sel_ref, x_ref, normed_ref, qkv_ref, probs_ref, att_ref, mid_ref, gm_ref, gh_ref, mlp_ref, valid_ref,
    g1_ref, g2_ref, bfc2_ref, wqkv_ref, wproj_ref, img_ref, cot_ref,
    lo_ref, gi_ref, dwp_ref, dwq_ref, vec_ref,
    gmid_ref, gatt_ref, gq_ref, gk_ref, gv_ref, gn_ref,
):
    step = pl.program_id(0)
    rows, width = x_ref.shape

    @pl.when(step == 0)
    def _():
        middle = mid_ref[...]
        valid = valid_ref[...] > 0
        mlp_out = jnp.where(valid, mlp_ref[...] + bfc2_ref[...].astype(F32), 0.0)
        block = middle + mlp_out
        kept = jnp.where(valid, block, 0.0)
        vec_ref[8:9] = jnp.sum(kept * kept, axis=0, keepdims=True)
        vec_ref[9:10] = jnp.sum(mlp_out * mlp_out, axis=0, keepdims=True)
        low = block.astype(BF16)
        for i in range(images):
            put = t_dot(sel_ref[i], low[i * slots : (i + 1) * slots])
            here = jnp.sum(sel_ref[i].astype(F32), axis=0, keepdims=True)
            lo_ref[i] = put.astype(BF16)
        scaled, inverse = norm_rows(middle)
        grad_hidden = gh_ref[...]
        vec_ref[0:1] = jnp.sum(grad_hidden * scaled, axis=0, keepdims=True)
        vec_ref[1:2] = jnp.sum(grad_hidden, axis=0, keepdims=True)
        gm = gm_ref[...].astype(F32)
        vec_ref[2:3] = jnp.sum(gm, axis=0, keepdims=True)
        grad_middle = gm + norm_back(grad_hidden * g2_ref[...], scaled, inverse)
        gmid_ref[...] = grad_middle
        grad_attn = grad_middle.astype(BF16)
        vec_ref[3:4] = jnp.sum(grad_attn.astype(F32), axis=0, keepdims=True)
        dwp_ref[...] = t_dot(att_ref[...], grad_attn).astype(BF16)
        gatt_ref[...] = dot_t(grad_attn, wproj_ref[...]).astype(BF16)
        gn_ref[...] = jnp.zeros_like(gn_ref)

    first = lax.broadcasted_iota(jnp.int32, (1, 2 * HEAD_DIM), 1) < HEAD_DIM
    zero = jnp.zeros((), BF16)
    scale = jnp.asarray(HEAD_DIM ** -0.5, BF16)
    pairs = width // 128 // groups
    for group in range(groups):

        @pl.when(step == group + 1)
        def _():
            base = group * pairs * 128

            @pl.loop(0, images)
            def _(i):
                here = pl.ds(pl.multiple_of(i * slots, 16), slots)
                for pair in range(pairs):
                    at = base + pair * 128
                    own = slice(pair * 128, pair * 128 + 128)
                    query = qkv_ref[here, at : at + 128]
                    key = qkv_ref[here, width + at : width + at + 128]
                    value = qkv_ref[here, 2 * width + at : 2 * width + at + 128]
                    grad_att = gatt_ref[here, at : at + 128]
                    gq = gk = gv = None
                    for half in range(2):
                        mine = first if half == 0 else jnp.logical_not(first)
                        low = probs_ref[i, 2 * (base // 128 + pair) + half]
                        probs = low.astype(F32)
                        g_mine = jnp.where(mine, grad_att, zero)
                        grad_probs = dot_t(g_mine, value).astype(BF16).astype(F32)
                        inner = jnp.sum(probs * grad_probs, axis=1, keepdims=True)
                        grad_scores = (probs * (grad_probs - inner)).astype(BF16) * scale
                        tv = t_dot(low, g_mine)
                        tq = dot(grad_scores, jnp.where(mine, key, zero))
                        tk = t_dot(grad_scores, jnp.where(mine, query, zero))
                        gq = tq if gq is None else gq + tq
                        gk = tk if gk is None else gk + tk
                        gv = tv if gv is None else gv + tv
                    gq_ref[here, own] = gq.astype(BF16)
                    gk_ref[here, own] = gk.astype(BF16)
                    gv_ref[here, own] = gv.astype(BF16)

            span = pairs * 128
            vec_ref[4:5, base : base + span] = jnp.sum(gq_ref[...].astype(F32), axis=0, keepdims=True)
            vec_ref[5:6, base : base + span] = jnp.sum(gv_ref[...].astype(F32), axis=0, keepdims=True)
            for part, ref in enumerate((gq_ref, gk_ref, gv_ref)):
                cols = slice(part * width + base, part * width + base + span)
                dwq_ref[:, cols] = t_dot(normed_ref[...], ref[...]).astype(BF16)
                gn_ref[...] += dot_t(ref[...], wqkv_ref[:, cols])

    @pl.when(step == groups + 1)
    def _():
        scaled, inverse = norm_rows(x_ref[...].astype(F32))
        grad_normed = gn_ref[...]
        vec_ref[6:7] = jnp.sum(grad_normed * scaled, axis=0, keepdims=True)
        vec_ref[7:8] = jnp.sum(grad_normed, axis=0, keepdims=True)
        change = gmid_ref[...] + norm_back(grad_normed * g1_ref[...], scaled, inverse)
        high = change.astype(BF16)
        rest = (change - high.astype(F32)).astype(BF16)
        for i in range(images):
            here = slice(i * slots, (i + 1) * slots)
            gi_ref[i] = t_dot(sel_ref[i], high[here]) + t_dot(sel_ref[i], rest[here])


def whole(shape):
    return pl.BlockSpec(shape, lambda *_: (0,) * len(shape), pipeline_mode=pl.Buffered(1))


def plain_device(
    images, keep_mask, ln1_gain, ln1_bias, w_qkv, bias_q, bias_v, w_proj, b_proj,
    ln2_gain, ln2_bias, w_fc1, b_fc1, w_fc2, b_fc2, cotangent,
):
    count, patches, width = images.shape
    slots = slots_of(patches)
    rows = count * slots
    heads = width // HEAD_DIM
    shard = w_fc1.shape[1]
    row = lambda v: v.reshape(1, -1)
    whole_w1 = lax.all_gather(w_fc1, "mlp")
    whole_w2 = lax.all_gather(w_fc2, "mlp")
    whole_b1 = lax.all_gather(b_fc1, "mlp").reshape(2, 1, shard)
    shape = jax.ShapeDtypeStruct
    limit = pltpu.CompilerParams(vmem_limit_bytes=60 * 2**20)
    per_image = lambda *tail: pl.BlockSpec((1,) + tail, lambda i: (i,) + (0,) * len(tail))
    per_rows = lambda cols: pl.BlockSpec((slots, cols), lambda i: (i, 0))
    sel, x, normed, qkv, probs, att, mid, hid, gm, sums = pl.pallas_call(
        functools.partial(forward_kernel, slots, False),
        grid=(count,),
        out_shape=(
            shape((count, slots, patches), BF16),
            shape((rows, width), BF16),
            shape((rows, width), BF16),
            shape((rows, 3 * width), BF16),
            shape((count, heads, slots, slots), BF16),
            shape((rows, width), BF16),
            shape((rows, width), F32),
            shape((rows, width), BF16),
            shape((rows, width), BF16),
            shape((count, 8, width), F32),
        ),
        in_specs=[
            per_image(1, patches), per_image(patches, width), per_image(patches, width),
            whole((1, width)), whole((1, width)), whole((width, 3 * width)), whole((1, width)), whole((1, width)),
            whole((width, width)), whole((1, width)), whole((1, width)), whole((1, width)),
        ],
        out_specs=(
            per_image(slots, patches), per_rows(width), per_rows(width), per_rows(3 * width),
            per_image(heads, slots, slots), per_rows(width), per_rows(width), per_rows(width), per_rows(width),
            per_image(8, width),
        ),
        compiler_params=limit,
        name="attention_forward",
    )(
        keep_mask.reshape(count, 1, patches), images, cotangent, row(ln1_gain), row(ln1_bias), w_qkv,
        row(bias_q), row(bias_v), w_proj, row(b_proj), row(ln2_gain), row(ln2_bias),
    )
    chunk = 512 if shard % 512 == 0 else 256
    each = shard // chunk
    mlp_out, grad_hidden, dw1, dw2, db1 = pl.pallas_call(
        mlp_kernel,
        grid=(2 * each,),
        out_shape=(
            shape((rows, width), F32), shape((rows, width), F32),
            shape((2, width, shard), BF16), shape((2, shard, width), BF16), shape((2, 1, shard), F32),
        ),
        in_specs=[
            whole((rows, width)), whole((rows, width)),
            pl.BlockSpec((1, width, chunk), lambda c: (c // each, 0, c % each)),
            pl.BlockSpec((1, 1, chunk), lambda c: (c // each, 0, c % each)),
            pl.BlockSpec((1, chunk, width), lambda c: (c // each, c % each, 0)),
        ],
        out_specs=(
            whole((rows, width)), whole((rows, width)),
            pl.BlockSpec((1, width, chunk), lambda c: (c // each, 0, c % each)),
            pl.BlockSpec((1, chunk, width), lambda c: (c // each, c % each, 0)),
            pl.BlockSpec((1, 1, chunk), lambda c: (c // each, 0, c % each)),
        ),
        compiler_params=limit,
        name="mlp_both_ways",
    )(hid, gm, whole_w1, whole_b1, whole_w2)
    kept = jnp.sum(keep_mask, axis=1, keepdims=True)
    valid = (jnp.arange(slots, dtype=jnp.int32)[None, :] < kept).astype(F32).reshape(rows, 1)
    groups = 3
    span = width // groups
    low, put, dwp, dwq, vec = pl.pallas_call(
        functools.partial(backward_kernel, count, slots, groups),
        grid=(groups + 2,),
        out_shape=(
            shape((count, patches, width), BF16), shape((count, patches, width), F32),
            shape((width, width), BF16), shape((width, 3 * width), BF16), shape((16, width), F32),
        ),
        in_specs=[
            whole((count, slots, patches)), whole((rows, width)), whole((rows, width)), whole((rows, 3 * width)),
            whole((count, heads, slots, slots)), whole((rows, width)), whole((rows, width)), whole((rows, width)),
            whole((rows, width)), whole((rows, width)), whole((rows, 1)),
            whole((1, width)), whole((1, width)), whole((1, width)), whole((width, 3 * width)), whole((width, width)),
            pl.BlockSpec(memory_space=pl.ANY), pl.BlockSpec(memory_space=pl.ANY),
        ],
        out_specs=(
            whole((count, patches, width)), whole((count, patches, width)),
            whole((width, width)), whole((width, 3 * width)), whole((16, width)),
        ),
        scratch_shapes=[
            pltpu.VMEM((rows, width), F32), pltpu.VMEM((rows, width), BF16),
            pltpu.VMEM((rows, span), BF16), pltpu.VMEM((rows, span), BF16), pltpu.VMEM((rows, span), BF16),
            pltpu.VMEM((rows, width), F32),
        ],
        compiler_params=limit,
        name="attention_backward",
    )(
        sel, x, normed, qkv, probs, att, mid, gm, grad_hidden, mlp_out, valid,
        row(ln1_gain), row(ln2_gain), row(b_fc2), w_qkv, w_proj, images, cotangent,
    )
    kept_at = (keep_mask > 0)[:, :, None]
    layer_out = jnp.where(kept_at, low, images)
    grad_images = jnp.where(kept_at, put, cotangent.astype(F32))
    both = ("img", "mlp")
    place = lax.axis_index("mlp")
    dw1s = lax.psum_scatter(dw1.reshape(2 * width, shard), "mlp", scatter_dimension=0, tiled=True)
    dw2s = lax.psum_scatter(dw2.reshape(2 * shard, width), "mlp", scatter_dimension=0, tiled=True)
    s_w1, s_w2 = lax.psum((dw1s, dw2s), "img")
    s_wq, s_wp = lax.psum((dwq, dwp), both)
    vec, sums, s_b1 = lax.psum((vec, jnp.sum(sums, axis=0), db1.reshape(2, shard)), both)
    s_b1 = lax.dynamic_index_in_dim(s_b1, place, 0, keepdims=False)
    stream_sq, mlp_sq, attn_sq = jnp.sum(vec[8]), jnp.sum(vec[9]), jnp.sum(sums[0])
    root_means = jnp.sqrt(jnp.stack([stream_sq, attn_sq, mlp_sq]) / (sums[1, 0] * width))
    f = lambda v: v.astype(F32)
    return (
        layer_out, grad_images, vec[6], vec[7], f(s_wq), vec[4], vec[5], f(s_wp), vec[3], vec[0], vec[1],
        f(s_w1), s_b1, f(s_w2), vec[2], root_means,
    )


class Place:
    def __init__(self, deep, width):
        spot, self.core = lax.axis_index("img"), lax.axis_index("mlp")
        x, y, self.z = spot % 2, (spot // 2) % 2, spot // 4
        core = self.core
        self.bit1 = x * (1 - core) + y * core
        self.bit2 = y * (1 - core) + x * core
        step_x, step_y = 1 - 2 * x, 2 - 4 * y
        self.deep = deep
        self.other = {"mlp": 1 - core}
        self.peer1 = {"img": spot + step_x * (1 - core) + step_y * core}
        self.peer2 = {"img": spot + step_y * (1 - core) + step_x * core}
        self.peer_z = [{"img": ((self.z + k) % deep) * 4 + spot % 4} for k in range(1, deep)]
        self.half, self.quarter = width // 2, width // 4
        self.piece = width // 4 // deep
        self.half_at = self.bit1 * self.half
        self.half_off = (1 - self.bit1) * self.half
        self.quarter_at = self.half_at + self.bit2 * self.quarter
        self.quarter_off = self.half_at + (1 - self.bit2) * self.quarter

    def piece_at(self, z):
        return self.quarter_at + z * self.piece

    def everyone(self):
        return [self.other, self.peer1, self.peer2] + self.peer_z

    def greet(self):
        for peer in self.everyone():
            pl.semaphore_signal(pltpu.get_barrier_semaphore(), inc=1, device_id=peer, device_id_type=MESH)

    def all_here(self):
        pl.semaphore_wait(pltpu.get_barrier_semaphore(), len(self.everyone()))


def span(start, size):
    return pl.ds(pl.multiple_of(start, 16), size)


def remote(source, target, send_sem, recv_sem, peer):
    return pltpu.make_async_remote_copy(
        src_ref=source, dst_ref=target, send_sem=send_sem, recv_sem=recv_sem, device_id=peer, device_id_type=MESH
    )


def added(left, right):
    return (left.astype(F32) + right.astype(F32)).astype(BF16)


class Reduce:
    def __init__(self, place, partial, sending, total, got_core, got1, got2, got_z, send, recv, send_z, recv_z):
        self.place, self.partial, self.sending, self.total = place, partial, sending, total
        self.got_core, self.got1, self.got2, self.got_z = got_core, got1, got2, got_z
        self.send, self.recv, self.send_z, self.recv_z = send, recv, send_z, recv_z

    def copies(self, c, stage):
        p = self.place
        if stage == 0:
            return [remote(self.sending(c), self.got_core.at[c], self.send.at[c, 0], self.recv.at[c, 0], p.other)]
        total = self.total(c)
        if stage == 1:
            part = total.at[:, span(p.half_off, p.half), :]
            return [remote(part, self.got1.at[c], self.send.at[c, 1], self.recv.at[c, 1], p.peer1)]
        if stage == 2:
            part = total.at[:, span(p.quarter_off, p.quarter), :]
            return [remote(part, self.got2.at[c], self.send.at[c, 2], self.recv.at[c, 2], p.peer2)]
        made = []
        for k, peer in enumerate(p.peer_z):
            part = total.at[:, span(p.piece_at((p.z + k + 1) % p.deep), p.piece), :]
            made.append(remote(part, self.got_z.at[c, k], self.send_z.at[c, k], self.recv_z.at[c, k], peer))
        return made

    def begin(self, c, stage):
        for copy in self.copies(c, stage):
            copy.start()

    def arrive(self, c, stage):
        for copy in self.copies(c, stage):
            copy.wait_recv()

    def sent(self, c):
        for stage in range(4):
            for copy in self.copies(c, stage):
                copy.wait_send()

    def plane1(self, c):
        self.arrive(c, 0)
        total, partial, got = self.total(c), self.partial(c), self.got_core.at[c]
        total[...] = added(partial[...], got[...])
        self.begin(c, 1)

    def plane2(self, c):
        p = self.place
        self.arrive(c, 1)
        rows = span(p.half_at, p.half)
        total = self.total(c)
        total[:, rows, :] = added(total[:, rows, :], self.got1[c])
        self.begin(c, 2)

    def along_z(self, c):
        p = self.place
        self.arrive(c, 2)
        rows = span(p.quarter_at, p.quarter)
        total = self.total(c)
        total[:, rows, :] = added(total[:, rows, :], self.got2[c])
        self.begin(c, 3)

    def finish(self, c):
        p = self.place
        self.arrive(c, 3)
        rows = span(p.piece_at(p.z), p.piece)
        value = self.total(c)[:, rows, :].astype(F32)
        for k in range(p.deep - 1):
            value = value + self.got_z[c, k].astype(F32)
        return value.astype(BF16)


class Gather:
    def __init__(self, place, piece, result, mirror, local, send, recv, send_z, recv_z):
        self.place, self.piece, self.result, self.mirror, self.local = place, piece, result, mirror, local
        self.send, self.recv, self.send_z, self.recv_z = send, recv, send_z, recv_z

    def kept(self, c):
        p = self.place
        return pltpu.make_async_copy(
            self.piece(c), self.result(c).at[:, span(p.piece_at(p.z), p.piece), :], self.local.at[c]
        )

    def copies(self, c, stage, landing=False):
        p, result = self.place, self.result(c)
        if stage == 0:
            made = []
            for k, peer in enumerate(p.peer_z):
                z = (p.z - k - 1 + p.deep) % p.deep if landing else p.z
                target = result.at[:, span(p.piece_at(z), p.piece), :]
                made.append(remote(self.piece(c), target, self.send_z.at[c, k], self.recv_z.at[c, k], peer))
            return made
        if stage == 1:
            source = result.at[:, span(p.quarter_at, p.quarter), :]
            target = result.at[:, span(p.quarter_off if landing else p.quarter_at, p.quarter), :]
            return [remote(source, target, self.send.at[c, 0], self.recv.at[c, 0], p.peer2)]
        if stage == 2:
            source = result.at[:, span(p.half_at, p.half), :]
            target = result.at[:, span(p.half_off if landing else p.half_at, p.half), :]
            return [remote(source, target, self.send.at[c, 1], self.recv.at[c, 1], p.peer1)]
        return [remote(result, self.mirror(c) if landing else result, self.send.at[c, 2], self.recv.at[c, 2], p.other)]

    def begin(self, c, stage):
        for copy in self.copies(c, stage):
            copy.start()

    def arrive(self, c, stage):
        for copy in self.copies(c, stage, landing=True):
            copy.wait_recv()

    def along_z(self, c):
        self.kept(c).start()
        self.begin(c, 0)

    def plane2(self, c):
        self.kept(c).wait()
        self.arrive(c, 0)
        self.begin(c, 1)

    def plane1(self, c):
        self.arrive(c, 1)
        self.begin(c, 2)

    def across(self, c):
        self.arrive(c, 2)
        self.begin(c, 3)

    def sent(self, c):
        for stage in range(3 if self.mirror is None else 4):
            for copy in self.copies(c, stage):
                copy.wait_send()


def vec_slot(slot, width):
    return slice(slot // 2, slot // 2 + 1), slice(slot % 2 * width, slot % 2 * width + width)


def mlp_staged_kernel(
    deep, images, slots, ticks,
    hid_ref, gm_ref, att_ref, mid_ref, sel_ref, sums_ref, w1a_ref, w1b_ref, b1a_ref, b1b_ref, w2a_ref, w2b_ref,
    wproj_ref, g2_ref, bfc2_ref,
    red_ref, gmid_ref, gatt_ref, dwp_ref, lo_ref, vec_ref,
    out_ref, gh_ref, give_ref, own_ref, got_core, got1, got2, got_z, send, recv, send_z, recv_z,
):
    step = pl.program_id(0)
    rows, width = hid_ref.shape
    place = Place(deep, width)
    panels = 4
    reduce = Reduce(
        place, lambda c: own_ref.at[c], lambda c: give_ref.at[c], lambda c: own_ref.at[c],
        got_core, got1, got2, got_z, send, recv, send_z, recv_z,
    )

    def put_red(c):
        red_ref[pl.ds(c * panels, panels)] = reduce.finish(c)

    def half(w1_ref, b1_ref, w2_ref, target, db_row):
        hid, gm = hid_ref[...], gm_ref[...]
        w1, w2 = w1_ref[...], w2_ref[...]
        chunk = w1.shape[1]
        pre = dot(hid, w1) + b1_ref[...].astype(F32)
        act, slope = gelu_pair(pre)
        act = act.astype(BF16)
        grad_act = dot_t(gm, w2).astype(BF16).astype(F32)
        grad_pre = (grad_act * slope).astype(BF16)
        d2 = t_dot(act, gm).astype(BF16)
        for j in range(width // 128):
            at = j % 3 * chunk
            target[2 + j // 3, at : at + chunk, :] = d2[:, j * 128 : j * 128 + 128]
        d1 = t_dot(hid, grad_pre).astype(BF16)
        target[0] = d1[:, :128]
        target[1] = d1[:, 128:]
        cols = pl.ds(pl.multiple_of(step * chunk, chunk), chunk)
        vec_ref[pl.ds(db_row, 1), cols] = jnp.sum(grad_pre.astype(F32), axis=0, keepdims=True)
        out_ref[...] += dot(act, w2)
        gh_ref[...] += dot_t(grad_pre, w1)

    @pl.when(step == 0)
    def _():
        place.greet()
        out_ref[...] = jnp.zeros_like(out_ref)
        gh_ref[...] = jnp.zeros_like(gh_ref)
        place.all_here()

    @pl.when((step >= 1) & (step <= ticks))
    def _():
        reduce.plane1(step - 1)

    @pl.when((step >= 2) & (step <= ticks))
    def _():
        reduce.plane2(step - 2)

    @pl.when((step >= 3) & (step <= ticks))
    def _():
        reduce.along_z(step - 3)

    @pl.when((step >= 4) & (step <= ticks))
    def _():
        put_red(step - 4)

    @pl.when(step < ticks)
    def _():
        half(w1b_ref, b1b_ref, w2b_ref, give_ref.at[step], 7 - place.core)

    @pl.when(step < ticks)
    def _():
        reduce.begin(step, 0)
        half(w1a_ref, b1a_ref, w2a_ref, own_ref.at[step], 6 + place.core)

    def note(slot, value):
        at_row, at_col = vec_slot(slot, width)
        vec_ref[at_row, at_col] = value

    def column_sum(value):
        return jnp.sum(value, axis=0, keepdims=True)

    @pl.when(step == ticks)
    def _():
        stream = mlp_sq = jnp.zeros((1, width), F32)
        gain = shift = b_two = b_proj = jnp.zeros((1, width), F32)
        for i in range(images):
            here = slice(i * slots, i * slots + slots)
            sel = sel_ref[i]
            middle = mid_ref[here]
            valid = jnp.sum(sel.astype(F32), axis=1, keepdims=True) > 0
            mlp_out = jnp.where(valid, out_ref[here] + bfc2_ref[...].astype(F32), 0.0)
            block = middle + mlp_out
            kept = jnp.where(valid, block, 0.0)
            stream = stream + column_sum(kept * kept)
            mlp_sq = mlp_sq + column_sum(mlp_out * mlp_out)
            lo_ref[i] = t_dot(sel, block.astype(BF16)).astype(BF16)
            scaled, inverse = norm_rows(middle)
            grad_hidden = gh_ref[here]
            gain = gain + column_sum(grad_hidden * scaled)
            shift = shift + column_sum(grad_hidden)
            gm = gm_ref[here].astype(F32)
            b_two = b_two + column_sum(gm)
            grad_middle = gm + norm_back(grad_hidden * g2_ref[...], scaled, inverse)
            gmid_ref[here] = grad_middle
            grad_attn = grad_middle.astype(BF16)
            b_proj = b_proj + column_sum(grad_attn.astype(F32))
            hid_ref_out = grad_attn
            gatt_ref[here] = grad_attn
        for slot, value in enumerate((gain, shift, b_two, b_proj)):
            note(slot, value)
        note(8, stream)
        note(9, mlp_sq)
        note(10, sum(sums_ref[i, 0:1] for i in range(images)))
        note(11, sum(sums_ref[i, 1:2] for i in range(images)))
        reduce.plane2(ticks - 1)
        reduce.along_z(ticks - 2)
        put_red(ticks - 3)
        grad_attn = gatt_ref[...]
        for part in range(3):
            cols = slice(part * width // 3, (part + 1) * width // 3)
            d = t_dot(att_ref[...], grad_attn[:, cols]).astype(BF16)
            dwp_ref[0, part] = d[:, :128]
            dwp_ref[1, part] = d[:, 128:]
        reduce.along_z(ticks - 1)
        put_red(ticks - 2)
        gatt_ref[...] = dot_t(grad_attn, wproj_ref[...]).astype(BF16)
        put_red(ticks - 1)

        @pl.loop(0, ticks)
        def _(c):
            reduce.sent(c)


def attention_staged_kernel(
    deep, images, slots, groups, ticks,
    q_ref, k_ref, v_ref, probs_ref, gatt_ref, wq_ref, wk_ref, wv_ref, normed_ref, x_ref, gmid_ref, sel_ref, g1_ref,
    dwp_ref, red_ref, vecin_ref,
    mlp_ref, attn_ref, gi_ref, vec_ref,
    gq_ref, gk_ref, gv_ref, gn_ref, stage_ref, total_ref, piece_ref, got_core, got1, got2, got_z,
    vsum_ref, vgot_ref, vz_ref,
    send, recv, send_z, recv_z, m_local, m_send, m_recv, m_send_z, m_recv_z,
    a_local, a_send, a_recv, a_send_z, a_recv_z, v_send, v_recv, v_send_z, v_recv_z,
):
    step = pl.program_id(0)
    rows, width = x_ref.shape
    place = Place(deep, width)
    core = place.core
    polls = images + 2

    def partial_of(owner):
        def pick(c):
            if isinstance(c, int) and c == 0:
                return dwp_ref.at[owner]
            return stage_ref.at[c - 1, owner]

        return pick

    reduce = Reduce(
        place, partial_of(core), partial_of(1 - core), lambda c: total_ref.at[c],
        got_core, got1, got2, got_z, send, recv, send_z, recv_z,
    )
    back = Gather(
        place, lambda c: piece_ref.at[c], lambda c: attn_ref.at[core, pl.ds(3 * c, 3)],
        lambda c: attn_ref.at[1 - core, pl.ds(3 * c, 3)], a_local, a_send, a_recv, a_send_z, a_recv_z,
    )
    mlp = Gather(
        place, lambda c: red_ref.at[pl.ds(4 * c, 4)], lambda c: mlp_ref.at[pl.ds(4 * c, 4)], None,
        m_local, m_send, m_recv, m_send_z, m_recv_z,
    )

    def turn(c):
        piece_ref[c] = reduce.finish(c)
        back.along_z(c)

    def do(name, c):
        return {
            "X": reduce.plane1, "Y": reduce.plane2, "Z": reduce.along_z, "R": turn,
            "ay": back.plane2, "ax": back.plane1, "ac": back.across,
            "my": mlp.plane2, "mx": mlp.plane1,
        }[name](c)

    plan = {}
    for at, name, c in (
        (1, "X", 0), (3, "my", 0), (4, "Y", 0), (6, "mx", 0), (6, "Z", 0),
        (7, "my", 1), (8, "X", 1), (9, "R", 0), (10, "mx", 1), (11, "Y", 1), (11, "my", 2), (12, "ay", 0),
        (13, "Z", 1), (14, "mx", 2), (15, "X", 2), (15, "ax", 0), (16, "R", 1), (16, "my", 3), (18, "Y", 2),
        (18, "mx", 3), (19, "ay", 1), (20, "Z", 2),
    ):
        plan.setdefault(at, []).append((name, c))

    def run(at, now):
        for moment, jobs in sorted(plan.items()):
            if at(moment % polls):

                @pl.when(now == moment)
                def _(jobs=jobs):
                    for name, c in jobs:
                        do(name, c)

    first = lax.broadcasted_iota(jnp.int32, (1, 2 * HEAD_DIM), 1) < HEAD_DIM
    zero = jnp.zeros((), BF16)
    scale = jnp.asarray(HEAD_DIM ** -0.5, BF16)
    pairs = width // 128 // groups
    wide = pairs * 128

    @pl.when(step == 0)
    def _():
        place.greet()
        gn_ref[...] = jnp.zeros_like(gn_ref)
        vsum_ref[0] = vecin_ref[...]
        place.all_here()
        reduce.begin(0, 0)
        for c in range(ticks):
            mlp.along_z(c)

    @pl.when(step < groups)
    def _():
        @pl.loop(0, images)
        def _(i):
            run(lambda at: at < images, step * polls + i)
            here = pl.ds(pl.multiple_of(i * slots, 16), slots)
            for pair in range(pairs):
                own = slice(pair * 128, pair * 128 + 128)
                query, key, value = q_ref[here, own], k_ref[here, own], v_ref[here, own]
                grad_att = gatt_ref[here, own]
                gq = gk = gv = None
                for half in range(2):
                    mine = first if half == 0 else jnp.logical_not(first)
                    low = probs_ref[i, 2 * pair + half]
                    probs = low.astype(F32)
                    g_mine = jnp.where(mine, grad_att, zero)
                    grad_probs = dot_t(g_mine, value).astype(BF16).astype(F32)
                    inner = jnp.sum(probs * grad_probs, axis=1, keepdims=True)
                    grad_scores = (probs * (grad_probs - inner)).astype(BF16) * scale
                    tv = t_dot(low, g_mine)
                    tq = dot(grad_scores, jnp.where(mine, key, zero))
                    tk = t_dot(grad_scores, jnp.where(mine, query, zero))
                    gq = tq if gq is None else gq + tq
                    gk = tk if gk is None else gk + tk
                    gv = tv if gv is None else gv + tv
                gq_ref[here, own] = gq.astype(BF16)
                gk_ref[here, own] = gk.astype(BF16)
                gv_ref[here, own] = gv.astype(BF16)

        run(lambda at: at == images, step * polls + images)
        cols = pl.ds(pl.multiple_of(step * wide, wide), wide)
        shifted = pl.ds(pl.multiple_of(width + step * wide, wide), wide)
        vsum_ref[0, 2:3, cols] = jnp.sum(gq_ref[...].astype(F32), axis=0, keepdims=True)
        vsum_ref[0, 2:3, shifted] = jnp.sum(gv_ref[...].astype(F32), axis=0, keepdims=True)
        for part, (ref, w_ref) in enumerate(((gq_ref, wq_ref), (gk_ref, wk_ref), (gv_ref, wv_ref))):
            d = t_dot(normed_ref[...], ref[...]).astype(BF16)
            stage_ref[step, 0, part] = d[:, :128]
            stage_ref[step, 1, part] = d[:, 128:]
            gn_ref[...] += dot_t(ref[...], w_ref[...])
        reduce.begin(step + 1, 0)
        run(lambda at: at == images + 1, step * polls + images + 1)

    def vec_copies(stage):
        if stage < 3:
            peer = (place.other, place.peer1, place.peer2)[stage]
            return [remote(vsum_ref.at[stage], vgot_ref.at[stage], v_send.at[stage], v_recv.at[stage], peer)]
        return [
            remote(vsum_ref.at[3], vz_ref.at[k], v_send_z.at[k], v_recv_z.at[k], peer)
            for k, peer in enumerate(place.peer_z)
        ]

    def vec_begin(stage):
        for copy in vec_copies(stage):
            copy.start()

    def vec_next(stage):
        for copy in vec_copies(stage):
            copy.wait_recv()
        if stage < 3:
            vsum_ref[stage + 1] = vsum_ref[stage] + vgot_ref[stage]
            vec_begin(stage + 1)

    @pl.when(step == groups)
    def _():
        last = groups
        do("X", last)
        gain = shift = jnp.zeros((1, width), F32)
        for i in range(images):
            here = slice(i * slots, i * slots + slots)
            sel = sel_ref[i]
            scaled, inverse = norm_rows(x_ref[here].astype(F32))
            grad_normed = gn_ref[here]
            gain = gain + jnp.sum(grad_normed * scaled, axis=0, keepdims=True)
            shift = shift + jnp.sum(grad_normed, axis=0, keepdims=True)
            change = gmid_ref[here] + norm_back(grad_normed * g1_ref[...], scaled, inverse)
            high = change.astype(BF16)
            rest = (change - high.astype(F32)).astype(BF16)
            gi_ref[i] = t_dot(sel, high) + t_dot(sel, rest)
            if i == 1:
                do("R", 2)
                do("ax", 1)
                do("my", 4)
            if i == 3:
                do("Y", last)
                do("mx", 4)
                do("ac", 0)
        at_row, at_col = vec_slot(6, width)
        vsum_ref[0, at_row, at_col] = gain
        at_row, at_col = vec_slot(7, width)
        vsum_ref[0, at_row, at_col] = shift
        vec_begin(0)
        do("Z", last)
        do("ay", 2)
        vec_next(0)
        do("my", 5)
        do("R", last)
        vec_next(1)
        do("ax", 2)
        do("ac", 1)
        do("ay", last)
        vec_next(2)
        do("mx", 5)
        do("ax", last)
        vec_next(3)
        value = None
        for z in range(deep):
            mine = vsum_ref[3]
            from_k = [vz_ref[k] for k in range(deep - 1)]
            term = mine
            for k in range(deep - 1):
                term = jnp.where((place.z - k - 1 + deep) % deep == z, from_k[k], term)
            value = term if value is None else value + term
        vec_ref[...] = value
        do("ac", 2)
        do("ac", last)
        for c in range(ticks):
            mlp.arrive(c, 2)
            mlp.sent(c)
        for c in range(groups + 1):
            back.arrive(c, 3)
            back.sent(c)
            reduce.sent(c)
        for stage in range(4):
            for copy in vec_copies(stage):
                copy.wait_send()


def staged_device(
    deep, images, keep_mask, ln1_gain, ln1_bias, w_qkv, bias_q, bias_v, w_proj, b_proj,
    ln2_gain, ln2_bias, w_fc1, b_fc1, w_fc2, b_fc2, cotangent,
):
    count, patches, width = images.shape
    slots = slots_of(patches)
    rows = count * slots
    heads = width // HEAD_DIM
    shard = w_fc1.shape[1]
    row = lambda v: v.reshape(1, -1)
    shape = jax.ShapeDtypeStruct
    limit = 62 * 2**20
    any_space = pl.BlockSpec(memory_space=pl.ANY)
    per_image = lambda *tail: pl.BlockSpec((1,) + tail, lambda i: (i,) + (0,) * len(tail))
    per_rows = lambda cols: pl.BlockSpec((slots, cols), lambda i: (i, 0))
    dma = pltpu.SemaphoreType.DMA
    sel, x, normed, qkv, probs, att, mid, hid, gm, sums, far_w1, far_b1, far_w2 = pl.pallas_call(
        functools.partial(forward_kernel, slots, True),
        grid=(count,),
        out_shape=(
            shape((count, slots, patches), BF16),
            shape((rows, width), BF16),
            shape((rows, width), BF16),
            shape((rows, 3 * width), BF16),
            shape((count, heads, slots, slots), BF16),
            shape((rows, width), BF16),
            shape((rows, width), F32),
            shape((rows, width), BF16),
            shape((rows, width), BF16),
            shape((count, 8, width), F32),
            shape((width, shard), BF16), shape((1, shard), BF16), shape((shard, width), BF16),
        ),
        in_specs=[
            per_image(1, patches), per_image(patches, width), per_image(patches, width),
            whole((1, width)), whole((1, width)), whole((width, 3 * width)), whole((1, width)), whole((1, width)),
            whole((width, width)), whole((1, width)), whole((1, width)), whole((1, width)),
            any_space, any_space, any_space,
        ],
        out_specs=(
            per_image(slots, patches), per_rows(width), per_rows(width), per_rows(3 * width),
            per_image(heads, slots, slots), per_rows(width), per_rows(width), per_rows(width), per_rows(width),
            per_image(8, width), any_space, any_space, any_space,
        ),
        scratch_shapes=[dma((3,)), dma((3,))],
        compiler_params=pltpu.CompilerParams(vmem_limit_bytes=limit, collective_id=0, has_side_effects=True),
        name="attention_forward",
    )(
        keep_mask.reshape(count, 1, patches), images, cotangent, row(ln1_gain), row(ln1_bias), w_qkv,
        row(bias_q), row(bias_v), w_proj, row(b_proj), row(ln2_gain), row(ln2_bias),
        w_fc1, row(b_fc1), w_fc2,
    )
    chunk = 256
    ticks = shard // chunk
    groups = 3
    piece = width // 4 // deep
    by_cols = lambda *lead: pl.BlockSpec(lead + (chunk,), lambda c: (0, c - c // ticks))
    by_rows = pl.BlockSpec((chunk, width), lambda c: (c - c // ticks, 0))
    red, gmid, gatt, dwp, low, vec = pl.pallas_call(
        functools.partial(mlp_staged_kernel, deep, count, slots, ticks),
        grid=(ticks + 1,),
        out_shape=(
            shape((4 * ticks, piece, 128), BF16), shape((rows, width), F32), shape((rows, width), BF16),
            shape((2, 3, width, 128), BF16), shape((count, patches, width), BF16), shape((8, 2 * width), F32),
        ),
        in_specs=[
            whole((rows, width)), whole((rows, width)), whole((rows, width)), whole((rows, width)),
            whole((count, slots, patches)), whole((count, 8, width)),
            by_cols(width), by_cols(width), by_cols(1), by_cols(1), by_rows, by_rows,
            whole((width, width)), whole((1, width)), whole((1, width)),
        ],
        out_specs=(
            whole((4 * ticks, piece, 128)), whole((rows, width)), whole((rows, width)),
            whole((2, 3, width, 128)), whole((count, patches, width)), whole((8, 2 * width)),
        ),
        scratch_shapes=[
            pltpu.VMEM((rows, width), F32), pltpu.VMEM((rows, width), F32),
            pltpu.VMEM((ticks, 4, width, 128), BF16), pltpu.VMEM((ticks, 4, width, 128), BF16),
            pltpu.VMEM((ticks, 4, width, 128), BF16), pltpu.VMEM((ticks, 4, width // 2, 128), BF16),
            pltpu.VMEM((ticks, 4, width // 4, 128), BF16), pltpu.VMEM((ticks, deep - 1, 4, piece, 128), BF16),
            dma((ticks, 3)), dma((ticks, 3)), dma((ticks, deep - 1)), dma((ticks, deep - 1)),
        ],
        compiler_params=pltpu.CompilerParams(vmem_limit_bytes=limit, collective_id=1, has_side_effects=True),
        name="mlp_both_ways",
    )(
        hid, gm, att, mid, sel, sums, w_fc1, far_w1, row(b_fc1), far_b1, w_fc2, far_w2, w_proj, row(ln2_gain), row(b_fc2),
    )
    wide = width // groups
    chunks = groups + 1
    now = lambda g: g - g // groups
    third = lambda lead, part: pl.BlockSpec((lead, wide), lambda g: (0, part * groups + now(g)))
    big, attn, put, vec = pl.pallas_call(
        functools.partial(attention_staged_kernel, deep, count, slots, groups, ticks),
        grid=(groups + 1,),
        out_shape=(
            shape((4 * ticks, width, 128), BF16), shape((2, 3 * chunks, width, 128), BF16),
            shape((count, patches, width), F32), shape((8, 2 * width), F32),
        ),
        in_specs=[
            third(rows, 0), third(rows, 1), third(rows, 2),
            pl.BlockSpec((count, heads // groups, slots, slots), lambda g: (0, now(g), 0, 0)),
            third(rows, 0), third(width, 0), third(width, 1), third(width, 2),
            whole((rows, width)), whole((rows, width)), whole((rows, width)), whole((count, slots, patches)),
            whole((1, width)), whole((2, 3, width, 128)), whole((4 * ticks, piece, 128)), whole((8, 2 * width)),
        ],
        out_specs=(any_space, any_space, whole((count, patches, width)), whole((8, 2 * width))),
        scratch_shapes=[
            pltpu.VMEM((rows, wide), BF16), pltpu.VMEM((rows, wide), BF16), pltpu.VMEM((rows, wide), BF16),
            pltpu.VMEM((rows, width), F32),
            pltpu.VMEM((groups, 2, 3, width, 128), BF16), pltpu.VMEM((chunks, 3, width, 128), BF16),
            pltpu.VMEM((chunks, 3, piece, 128), BF16), pltpu.VMEM((chunks, 3, width, 128), BF16),
            pltpu.VMEM((chunks, 3, width // 2, 128), BF16), pltpu.VMEM((chunks, 3, width // 4, 128), BF16),
            pltpu.VMEM((chunks, deep - 1, 3, piece, 128), BF16),
            pltpu.VMEM((4, 8, 2 * width), F32), pltpu.VMEM((3, 8, 2 * width), F32),
            pltpu.VMEM((deep - 1, 8, 2 * width), F32),
            dma((chunks, 3)), dma((chunks, 3)), dma((chunks, deep - 1)), dma((chunks, deep - 1)),
            dma((ticks,)), dma((ticks, 2)), dma((ticks, 2)), dma((ticks, deep - 1)), dma((ticks, deep - 1)),
            dma((chunks,)), dma((chunks, 3)), dma((chunks, 3)), dma((chunks, deep - 1)), dma((chunks, deep - 1)),
            dma((3,)), dma((3,)), dma((deep - 1,)), dma((deep - 1,)),
        ],
        compiler_params=pltpu.CompilerParams(vmem_limit_bytes=limit, collective_id=2, has_side_effects=True),
        name="attention_backward",
    )(
        qkv, qkv, qkv, probs, gatt, w_qkv, w_qkv, w_qkv, normed, x, gmid, sel, row(ln1_gain), dwp, red, vec,
    )
    kept_at = (keep_mask > 0)[:, :, None]
    layer_out = jnp.where(kept_at, low, images)
    grad_images = jnp.where(kept_at, put, cotangent.astype(F32))
    big = big.reshape(ticks, 4, width, 128)
    s_w1 = big[:, :2].transpose(2, 0, 1, 3).reshape(width, shard).astype(F32)
    s_w2 = big[:, 2:].reshape(ticks, 2, 3, chunk, 128).transpose(0, 3, 1, 2, 4).reshape(shard, width).astype(F32)
    s_wp = attn[:, :3].transpose(2, 1, 0, 3).reshape(width, width).astype(F32)
    s_wq = (
        attn[:, 3:].reshape(2, groups, 3, width, 128).transpose(3, 2, 1, 0, 4).reshape(width, 3 * width).astype(F32)
    )
    flat = vec[:6].reshape(12, width)
    root_means = jnp.sqrt(
        jnp.stack([jnp.sum(flat[8]), jnp.sum(flat[10]), jnp.sum(flat[9])]) / (flat[11, 0] * width)
    )
    s_b1 = lax.dynamic_index_in_dim(vec[6:8], lax.axis_index("mlp"), 0, keepdims=False)
    return (
        layer_out, grad_images, flat[6], flat[7], s_wq, flat[4], flat[5], s_wp, flat[3], flat[0], flat[1],
        s_w1, s_b1, s_w2, flat[2], root_means,
    )


def solution(mesh):
    rows, line = P(("img", "mlp"), None, None), P(("img", "mlp"), None)
    deep = mesh.shape["img"] // 4
    staged = mesh.shape["img"] == 4 * deep and mesh.shape["mlp"] == 2 and 1 < deep <= 4
    return jax.shard_map(
        functools.partial(staged_device, deep) if staged else plain_device,
        mesh=mesh,
        in_specs=(
            rows, line, P(), P(), P(), P(), P(), P(), P(), P(), P(),
            P(None, "mlp"), P("mlp"), P("mlp", None), P(), rows,
        ),
        out_specs=(
            rows, rows, P(), P(), P(), P(), P(), P(), P(), P(), P(),
            P(None, "mlp"), P("mlp"), P("mlp", None), P(), P(),
        ),
        check_vma=False,
    )
```

```python
import functools

import jax
import jax.numpy as jnp
from jax import lax
from jax.experimental import pallas as pl
from jax.experimental.pallas import tpu as pltpu
from jax.sharding import PartitionSpec as P

HEAD_DIM = 64
NORM_EPS = 1e-06
F32 = jnp.float32
BF16 = jnp.bfloat16
MESH = pl.DeviceIdType.MESH
ERFC_POLY = (
    -0.05792342897865154,
    0.27982426175045266,
    -0.47905523971588865,
    0.27061712140601424,
    -0.022718349995155727,
    0.2015184791612061,
    0.24328701077158832,
    0.2823637910445855,
    0.2820864086305586,
)


def dot(a, b):
    return jnp.dot(a, b, preferred_element_type=F32)


def dot_t(a, b):
    return lax.dot_general(a, b, (((1,), (1,)), ((), ())), preferred_element_type=F32)


def t_dot(a, b):
    return lax.dot_general(a, b, (((0,), (0,)), ((), ())), preferred_element_type=F32)


def slots_of(patches):
    most = 4 * patches // 5
    return -(-most // 16) * 16


def norm_rows(rows):
    center = rows - jnp.mean(rows, axis=1, keepdims=True)
    inverse = lax.rsqrt(jnp.mean(center * center, axis=1, keepdims=True) + NORM_EPS)
    return center * inverse, inverse


def norm_back(weighted, scaled, inverse):
    return inverse * (
        weighted
        - jnp.mean(weighted, axis=1, keepdims=True)
        - scaled * jnp.mean(weighted * scaled, axis=1, keepdims=True)
    )


def gelu_pair(values):
    reach = jnp.abs(values) * 0.7071067811865476
    inv = 1.0 / (1.0 + 0.5 * reach)
    decay = jnp.exp(-0.5 * (values * values))
    poly = jnp.full_like(values, ERFC_POLY[0])
    for coefficient in ERFC_POLY[1:]:
        poly = poly * inv + coefficient
    tail = (0.5 * inv) * poly * decay
    share = jnp.where(values > 0, 1.0 - tail, tail)
    return values * share, share + values * (decay * 0.3989422804014327)


def swap_weights(ours, theirs, send_sem, recv_sem):
    other = {"mlp": 1 - lax.axis_index("mlp")}
    copies = [
        pltpu.make_async_remote_copy(
            src_ref=ours[j], dst_ref=theirs[j], send_sem=send_sem.at[j], recv_sem=recv_sem.at[j],
            device_id=other, device_id_type=MESH,
        )
        for j in range(len(ours))
    ]

    def trade(begin):
        @pl.when(pl.program_id(0) == (0 if begin else pl.num_programs(0) - 1))
        def _():
            if begin:
                barrier = pltpu.get_barrier_semaphore()
                pl.semaphore_signal(barrier, inc=1, device_id=other, device_id_type=MESH)
                pl.semaphore_wait(barrier, 1)
            for copy in copies:
                if begin:
                    copy.start()
                else:
                    copy.wait()

    return trade


def as_row(ref):
    return ref[...].astype(F32).reshape(1, -1)


def forward_kernel(
    slots, exchange,
    keep_ref, img_ref, cot_ref, g1_ref, b1_ref, wqkv_ref, bq_ref, bv_ref, wproj_ref, bproj_ref, g2_ref, b2_ref,
    *refs,
):
    if exchange:
        ours, refs, (send_sem, recv_sem) = refs[:3], refs[3:-2], refs[-2:]
        theirs, refs = refs[-3:], refs[:-3]
        trade = swap_weights(ours, theirs, send_sem, recv_sem)
        trade(True)
    sel_ref, x_ref, normed_ref, qkv_ref, probs_ref, att_ref, mid_ref, hid_ref, gm_ref, sums_ref = refs
    patches, width = img_ref.shape[1:]
    heads = width // HEAD_DIM
    keep = keep_ref[pl.ds(pl.program_id(0), 1)].astype(F32)
    upto = lax.broadcasted_iota(jnp.int32, (patches, patches), 0) <= lax.broadcasted_iota(
        jnp.int32, (patches, patches), 1
    )
    keep8 = jnp.broadcast_to(keep, (8, patches)).astype(BF16)
    rank = dot(keep8, upto.astype(F32).astype(BF16))[0:1]
    count = jnp.sum(keep, axis=1, keepdims=True)
    slot = lax.broadcasted_iota(jnp.int32, (slots, patches), 0).astype(F32)
    sel = jnp.where((slot == rank - 1.0) & (keep > 0), 1.0, 0.0).astype(BF16)
    sel_ref[0] = sel
    gm_ref[...] = dot(sel, cot_ref[0]).astype(BF16)
    rows = dot(sel, img_ref[0])
    x_ref[...] = rows.astype(BF16)
    scaled, _ = norm_rows(rows)
    normed = (scaled * as_row(g1_ref) + as_row(b1_ref)).astype(BF16)
    normed_ref[...] = normed
    for part in range(3):
        cols = slice(part * width, (part + 1) * width)
        block = dot(normed, wqkv_ref[:, cols])
        if part == 0:
            block = block + as_row(bq_ref)
        if part == 2:
            block = block + as_row(bv_ref)
        qkv_ref[:, cols] = block.astype(BF16)
    closed = jnp.where(
        lax.broadcasted_iota(jnp.int32, (1, slots), 1).astype(F32) < count, 0.0, -1e30
    )
    first = lax.broadcasted_iota(jnp.int32, (1, 2 * HEAD_DIM), 1) < HEAD_DIM
    zero = jnp.zeros((), BF16)
    for pair in range(heads // 2):
        lanes = slice(pair * 128, pair * 128 + 128)
        query = qkv_ref[:, lanes] * jnp.asarray(HEAD_DIM ** -0.5, BF16)
        key = qkv_ref[:, width + pair * 128 : width + pair * 128 + 128]
        value = qkv_ref[:, 2 * width + pair * 128 : 2 * width + pair * 128 + 128]
        total = None
        for half in range(2):
            mine = first if half == 0 else jnp.logical_not(first)
            scores = dot_t(query, jnp.where(mine, key, zero)) + closed
            raised = jnp.exp(scores - jnp.max(scores, axis=1, keepdims=True))
            probs = (raised * (1.0 / jnp.sum(raised, axis=1, keepdims=True))).astype(BF16)
            probs_ref[0, 2 * pair + half] = probs
            term = dot(probs, jnp.where(mine, value, zero))
            total = term if total is None else total + term
        att_ref[:, lanes] = total.astype(BF16)
    attn_out = dot(att_ref[...], wproj_ref[...]) + as_row(bproj_ref)
    valid = lax.broadcasted_iota(jnp.int32, (slots, 1), 0).astype(F32) < count
    attn_kept = jnp.where(valid, attn_out, 0.0)
    middle = rows + attn_kept
    mid_ref[...] = middle
    sums_ref[0, 0:1] = jnp.sum(attn_kept * attn_kept, axis=0, keepdims=True)
    sums_ref[0, 1:2] = jnp.broadcast_to(count, (1, width))
    scaled, _ = norm_rows(middle)
    hid_ref[...] = (scaled * as_row(g2_ref) + as_row(b2_ref)).astype(BF16)
    if exchange:
        trade(False)


def mlp_kernel(hid_ref, gm_ref, w1_ref, b1_ref, w2_ref, out_ref, gh_ref, dw1_ref, dw2_ref, db1_ref):
    step = pl.program_id(0)
    hid, gm = hid_ref[...], gm_ref[...]
    w1, w2 = w1_ref[0], w2_ref[0]
    pre = dot(hid, w1) + b1_ref[0].astype(F32)
    act, slope = gelu_pair(pre)
    act = act.astype(BF16)
    grad_act = dot_t(gm, w2).astype(BF16).astype(F32)
    grad_pre_f = grad_act * slope
    grad_pre = grad_pre_f.astype(BF16)
    dw2_ref[0] = t_dot(act, gm).astype(BF16)
    dw1_ref[0] = t_dot(hid, grad_pre).astype(BF16)
    db1_ref[0] = jnp.sum(grad_pre.astype(F32), axis=0, keepdims=True)

    @pl.when(step == 0)
    def _():
        out_ref[...] = dot(act, w2)
        gh_ref[...] = dot_t(grad_pre, w1)

    @pl.when(step > 0)
    def _():
        out_ref[...] += dot(act, w2)
        gh_ref[...] += dot_t(grad_pre, w1)


def backward_kernel(
    images, slots, groups,
    sel_ref, x_ref, normed_ref, qkv_ref, probs_ref, att_ref, mid_ref, gm_ref, gh_ref, mlp_ref, valid_ref,
    g1_ref, g2_ref, bfc2_ref, wqkv_ref, wproj_ref, img_ref, cot_ref,
    lo_ref, gi_ref, dwp_ref, dwq_ref, vec_ref,
    gmid_ref, gatt_ref, gq_ref, gk_ref, gv_ref, gn_ref,
):
    step = pl.program_id(0)
    rows, width = x_ref.shape

    @pl.when(step == 0)
    def _():
        middle = mid_ref[...]
        valid = valid_ref[...] > 0
        mlp_out = jnp.where(valid, mlp_ref[...] + bfc2_ref[...].astype(F32), 0.0)
        block = middle + mlp_out
        kept = jnp.where(valid, block, 0.0)
        vec_ref[8:9] = jnp.sum(kept * kept, axis=0, keepdims=True)
        vec_ref[9:10] = jnp.sum(mlp_out * mlp_out, axis=0, keepdims=True)
        low = block.astype(BF16)
        for i in range(images):
            put = t_dot(sel_ref[i], low[i * slots : (i + 1) * slots])
            here = jnp.sum(sel_ref[i].astype(F32), axis=0, keepdims=True)
            lo_ref[i] = put.astype(BF16)
        scaled, inverse = norm_rows(middle)
        grad_hidden = gh_ref[...]
        vec_ref[0:1] = jnp.sum(grad_hidden * scaled, axis=0, keepdims=True)
        vec_ref[1:2] = jnp.sum(grad_hidden, axis=0, keepdims=True)
        gm = gm_ref[...].astype(F32)
        vec_ref[2:3] = jnp.sum(gm, axis=0, keepdims=True)
        grad_middle = gm + norm_back(grad_hidden * g2_ref[...], scaled, inverse)
        gmid_ref[...] = grad_middle
        grad_attn = grad_middle.astype(BF16)
        vec_ref[3:4] = jnp.sum(grad_attn.astype(F32), axis=0, keepdims=True)
        dwp_ref[...] = t_dot(att_ref[...], grad_attn).astype(BF16)
        gatt_ref[...] = dot_t(grad_attn, wproj_ref[...]).astype(BF16)
        gn_ref[...] = jnp.zeros_like(gn_ref)

    first = lax.broadcasted_iota(jnp.int32, (1, 2 * HEAD_DIM), 1) < HEAD_DIM
    zero = jnp.zeros((), BF16)
    scale = jnp.asarray(HEAD_DIM ** -0.5, BF16)
    pairs = width // 128 // groups
    for group in range(groups):

        @pl.when(step == group + 1)
        def _():
            base = group * pairs * 128

            @pl.loop(0, images)
            def _(i):
                here = pl.ds(pl.multiple_of(i * slots, 16), slots)
                for pair in range(pairs):
                    at = base + pair * 128
                    own = slice(pair * 128, pair * 128 + 128)
                    query = qkv_ref[here, at : at + 128]
                    key = qkv_ref[here, width + at : width + at + 128]
                    value = qkv_ref[here, 2 * width + at : 2 * width + at + 128]
                    grad_att = gatt_ref[here, at : at + 128]
                    gq = gk = gv = None
                    for half in range(2):
                        mine = first if half == 0 else jnp.logical_not(first)
                        low = probs_ref[i, 2 * (base // 128 + pair) + half]
                        probs = low.astype(F32)
                        g_mine = jnp.where(mine, grad_att, zero)
                        grad_probs = dot_t(g_mine, value).astype(BF16).astype(F32)
                        inner = jnp.sum(probs * grad_probs, axis=1, keepdims=True)
                        grad_scores = (probs * (grad_probs - inner)).astype(BF16) * scale
                        tv = t_dot(low, g_mine)
                        tq = dot(grad_scores, jnp.where(mine, key, zero))
                        tk = t_dot(grad_scores, jnp.where(mine, query, zero))
                        gq = tq if gq is None else gq + tq
                        gk = tk if gk is None else gk + tk
                        gv = tv if gv is None else gv + tv
                    gq_ref[here, own] = gq.astype(BF16)
                    gk_ref[here, own] = gk.astype(BF16)
                    gv_ref[here, own] = gv.astype(BF16)

            span = pairs * 128
            vec_ref[4:5, base : base + span] = jnp.sum(gq_ref[...].astype(F32), axis=0, keepdims=True)
            vec_ref[5:6, base : base + span] = jnp.sum(gv_ref[...].astype(F32), axis=0, keepdims=True)
            for part, ref in enumerate((gq_ref, gk_ref, gv_ref)):
                cols = slice(part * width + base, part * width + base + span)
                dwq_ref[:, cols] = t_dot(normed_ref[...], ref[...]).astype(BF16)
                gn_ref[...] += dot_t(ref[...], wqkv_ref[:, cols])

    @pl.when(step == groups + 1)
    def _():
        scaled, inverse = norm_rows(x_ref[...].astype(F32))
        grad_normed = gn_ref[...]
        vec_ref[6:7] = jnp.sum(grad_normed * scaled, axis=0, keepdims=True)
        vec_ref[7:8] = jnp.sum(grad_normed, axis=0, keepdims=True)
        change = gmid_ref[...] + norm_back(grad_normed * g1_ref[...], scaled, inverse)
        high = change.astype(BF16)
        rest = (change - high.astype(F32)).astype(BF16)
        for i in range(images):
            here = slice(i * slots, (i + 1) * slots)
            gi_ref[i] = t_dot(sel_ref[i], high[here]) + t_dot(sel_ref[i], rest[here])


def whole(shape):
    return pl.BlockSpec(shape, lambda *_: (0,) * len(shape), pipeline_mode=pl.Buffered(1))


def plain_device(
    images, keep_mask, ln1_gain, ln1_bias, w_qkv, bias_q, bias_v, w_proj, b_proj,
    ln2_gain, ln2_bias, w_fc1, b_fc1, w_fc2, b_fc2, cotangent,
):
    count, patches, width = images.shape
    slots = slots_of(patches)
    rows = count * slots
    heads = width // HEAD_DIM
    shard = w_fc1.shape[1]
    row = lambda v: v.reshape(1, -1)
    whole_w1 = lax.all_gather(w_fc1, "mlp")
    whole_w2 = lax.all_gather(w_fc2, "mlp")
    whole_b1 = lax.all_gather(b_fc1, "mlp").reshape(2, 1, shard)
    shape = jax.ShapeDtypeStruct
    limit = pltpu.CompilerParams(vmem_limit_bytes=60 * 2**20)
    per_image = lambda *tail: pl.BlockSpec((1,) + tail, lambda i: (i,) + (0,) * len(tail))
    per_rows = lambda cols: pl.BlockSpec((slots, cols), lambda i: (i, 0))
    sel, x, normed, qkv, probs, att, mid, hid, gm, sums = pl.pallas_call(
        functools.partial(forward_kernel, slots, False),
        grid=(count,),
        out_shape=(
            shape((count, slots, patches), BF16),
            shape((rows, width), BF16),
            shape((rows, width), BF16),
            shape((rows, 3 * width), BF16),
            shape((count, heads, slots, slots), BF16),
            shape((rows, width), BF16),
            shape((rows, width), F32),
            shape((rows, width), BF16),
            shape((rows, width), BF16),
            shape((count, 8, width), F32),
        ),
        in_specs=[
            whole((count, patches)), per_image(patches, width), per_image(patches, width),
            whole((width,)), whole((width,)), whole((width, 3 * width)), whole((width,)), whole((width,)),
            whole((width, width)), whole((width,)), whole((width,)), whole((width,)),
        ],
        out_specs=(
            per_image(slots, patches), per_rows(width), per_rows(width), per_rows(3 * width),
            per_image(heads, slots, slots), per_rows(width), per_rows(width), per_rows(width), per_rows(width),
            per_image(8, width),
        ),
        compiler_params=limit,
        name="attention_forward",
    )(
        keep_mask, images, cotangent, ln1_gain, ln1_bias, w_qkv, bias_q, bias_v, w_proj, b_proj, ln2_gain, ln2_bias,
    )
    chunk = 512 if shard % 512 == 0 else 256
    each = shard // chunk
    mlp_out, grad_hidden, dw1, dw2, db1 = pl.pallas_call(
        mlp_kernel,
        grid=(2 * each,),
        out_shape=(
            shape((rows, width), F32), shape((rows, width), F32),
            shape((2, width, shard), BF16), shape((2, shard, width), BF16), shape((2, 1, shard), F32),
        ),
        in_specs=[
            whole((rows, width)), whole((rows, width)),
            pl.BlockSpec((1, width, chunk), lambda c: (c // each, 0, c % each)),
            pl.BlockSpec((1, 1, chunk), lambda c: (c // each, 0, c % each)),
            pl.BlockSpec((1, chunk, width), lambda c: (c // each, c % each, 0)),
        ],
        out_specs=(
            whole((rows, width)), whole((rows, width)),
            pl.BlockSpec((1, width, chunk), lambda c: (c // each, 0, c % each)),
            pl.BlockSpec((1, chunk, width), lambda c: (c // each, c % each, 0)),
            pl.BlockSpec((1, 1, chunk), lambda c: (c // each, 0, c % each)),
        ),
        compiler_params=limit,
        name="mlp_both_ways",
    )(hid, gm, whole_w1, whole_b1, whole_w2)
    kept = jnp.sum(keep_mask, axis=1, keepdims=True)
    valid = (jnp.arange(slots, dtype=jnp.int32)[None, :] < kept).astype(F32).reshape(rows, 1)
    groups = 3
    span = width // groups
    low, put, dwp, dwq, vec = pl.pallas_call(
        functools.partial(backward_kernel, count, slots, groups),
        grid=(groups + 2,),
        out_shape=(
            shape((count, patches, width), BF16), shape((count, patches, width), F32),
            shape((width, width), BF16), shape((width, 3 * width), BF16), shape((16, width), F32),
        ),
        in_specs=[
            whole((count, slots, patches)), whole((rows, width)), whole((rows, width)), whole((rows, 3 * width)),
            whole((count, heads, slots, slots)), whole((rows, width)), whole((rows, width)), whole((rows, width)),
            whole((rows, width)), whole((rows, width)), whole((rows, 1)),
            whole((1, width)), whole((1, width)), whole((1, width)), whole((width, 3 * width)), whole((width, width)),
            pl.BlockSpec(memory_space=pl.ANY), pl.BlockSpec(memory_space=pl.ANY),
        ],
        out_specs=(
            whole((count, patches, width)), whole((count, patches, width)),
            whole((width, width)), whole((width, 3 * width)), whole((16, width)),
        ),
        scratch_shapes=[
            pltpu.VMEM((rows, width), F32), pltpu.VMEM((rows, width), BF16),
            pltpu.VMEM((rows, span), BF16), pltpu.VMEM((rows, span), BF16), pltpu.VMEM((rows, span), BF16),
            pltpu.VMEM((rows, width), F32),
        ],
        compiler_params=limit,
        name="attention_backward",
    )(
        sel, x, normed, qkv, probs, att, mid, gm, grad_hidden, mlp_out, valid,
        row(ln1_gain), row(ln2_gain), row(b_fc2), w_qkv, w_proj, images, cotangent,
    )
    kept_at = (keep_mask > 0)[:, :, None]
    layer_out = jnp.where(kept_at, low, images)
    grad_images = jnp.where(kept_at, put, cotangent.astype(F32))
    both = ("img", "mlp")
    place = lax.axis_index("mlp")
    dw1s = lax.psum_scatter(dw1.reshape(2 * width, shard), "mlp", scatter_dimension=0, tiled=True)
    dw2s = lax.psum_scatter(dw2.reshape(2 * shard, width), "mlp", scatter_dimension=0, tiled=True)
    s_w1, s_w2 = lax.psum((dw1s, dw2s), "img")
    s_wq, s_wp = lax.psum((dwq, dwp), both)
    vec, sums, s_b1 = lax.psum((vec, jnp.sum(sums, axis=0), db1.reshape(2, shard)), both)
    s_b1 = lax.dynamic_index_in_dim(s_b1, place, 0, keepdims=False)
    stream_sq, mlp_sq, attn_sq = jnp.sum(vec[8]), jnp.sum(vec[9]), jnp.sum(sums[0])
    root_means = jnp.sqrt(jnp.stack([stream_sq, attn_sq, mlp_sq]) / (sums[1, 0] * width))
    f = lambda v: v.astype(F32)
    return (
        layer_out, grad_images, vec[6], vec[7], f(s_wq), vec[4], vec[5], f(s_wp), vec[3], vec[0], vec[1],
        f(s_w1), s_b1, f(s_w2), vec[2], root_means,
    )


class Place:
    def __init__(self, deep, width):
        spot, self.core = lax.axis_index("img"), lax.axis_index("mlp")
        x, y, self.z = spot % 2, (spot // 2) % 2, spot // 4
        core = self.core
        self.bit1 = x * (1 - core) + y * core
        self.bit2 = y * (1 - core) + x * core
        step_x, step_y = 1 - 2 * x, 2 - 4 * y
        self.deep = deep
        self.other = {"mlp": 1 - core}
        self.peer1 = {"img": spot + step_x * (1 - core) + step_y * core}
        self.peer2 = {"img": spot + step_y * (1 - core) + step_x * core}
        self.peer_z = [{"img": ((self.z + k) % deep) * 4 + spot % 4} for k in range(1, deep)]
        self.half, self.quarter = width // 2, width // 4
        self.piece = width // 4 // deep
        self.half_at = self.bit1 * self.half
        self.half_off = (1 - self.bit1) * self.half
        self.quarter_at = self.half_at + self.bit2 * self.quarter
        self.quarter_off = self.half_at + (1 - self.bit2) * self.quarter

    def piece_at(self, z):
        return self.quarter_at + z * self.piece

    def everyone(self):
        return [self.other, self.peer1, self.peer2] + self.peer_z

    def greet(self):
        for peer in self.everyone():
            pl.semaphore_signal(pltpu.get_barrier_semaphore(), inc=1, device_id=peer, device_id_type=MESH)

    def all_here(self):
        pl.semaphore_wait(pltpu.get_barrier_semaphore(), len(self.everyone()))


def span(start, size):
    return pl.ds(pl.multiple_of(start, 16), size)


def remote(source, target, send_sem, recv_sem, peer):
    return pltpu.make_async_remote_copy(
        src_ref=source, dst_ref=target, send_sem=send_sem, recv_sem=recv_sem, device_id=peer, device_id_type=MESH
    )


def added(left, right):
    return (left.astype(F32) + right.astype(F32)).astype(BF16)


class Reduce:
    def __init__(self, place, partial, sending, total, got_core, got1, got2, got_z, send, recv, send_z, recv_z):
        self.place, self.partial, self.sending, self.total = place, partial, sending, total
        self.got_core, self.got1, self.got2, self.got_z = got_core, got1, got2, got_z
        self.send, self.recv, self.send_z, self.recv_z = send, recv, send_z, recv_z

    def copies(self, c, stage):
        p = self.place
        if stage == 0:
            return [remote(self.sending(c), self.got_core.at[c], self.send.at[c, 0], self.recv.at[c, 0], p.other)]
        total = self.total(c)
        if stage == 1:
            part = total.at[:, span(p.half_off, p.half), :]
            return [remote(part, self.got1.at[c], self.send.at[c, 1], self.recv.at[c, 1], p.peer1)]
        if stage == 2:
            part = total.at[:, span(p.quarter_off, p.quarter), :]
            return [remote(part, self.got2.at[c], self.send.at[c, 2], self.recv.at[c, 2], p.peer2)]
        made = []
        for k, peer in enumerate(p.peer_z):
            part = total.at[:, span(p.piece_at((p.z + k + 1) % p.deep), p.piece), :]
            made.append(remote(part, self.got_z.at[c, k], self.send_z.at[c, k], self.recv_z.at[c, k], peer))
        return made

    def begin(self, c, stage):
        for copy in self.copies(c, stage):
            copy.start()

    def arrive(self, c, stage):
        for copy in self.copies(c, stage):
            copy.wait_recv()

    def sent(self, c):
        for stage in range(4):
            for copy in self.copies(c, stage):
                copy.wait_send()

    def plane1(self, c):
        self.arrive(c, 0)
        total, partial, got = self.total(c), self.partial(c), self.got_core.at[c]
        total[...] = added(partial[...], got[...])
        self.begin(c, 1)

    def plane2(self, c):
        p = self.place
        self.arrive(c, 1)
        rows = span(p.half_at, p.half)
        total = self.total(c)
        total[:, rows, :] = added(total[:, rows, :], self.got1[c])
        self.begin(c, 2)

    def along_z(self, c):
        p = self.place
        self.arrive(c, 2)
        rows = span(p.quarter_at, p.quarter)
        total = self.total(c)
        total[:, rows, :] = added(total[:, rows, :], self.got2[c])
        self.begin(c, 3)

    def finish(self, c):
        p = self.place
        self.arrive(c, 3)
        rows = span(p.piece_at(p.z), p.piece)
        value = self.total(c)[:, rows, :].astype(F32)
        for k in range(p.deep - 1):
            value = value + self.got_z[c, k].astype(F32)
        return value.astype(BF16)


class Gather:
    def __init__(self, place, piece, result, mirror, local, send, recv, send_z, recv_z):
        self.place, self.piece, self.result, self.mirror, self.local = place, piece, result, mirror, local
        self.send, self.recv, self.send_z, self.recv_z = send, recv, send_z, recv_z

    def kept(self, c):
        p = self.place
        return pltpu.make_async_copy(
            self.piece(c), self.result(c).at[:, span(p.piece_at(p.z), p.piece), :], self.local.at[c]
        )

    def copies(self, c, stage, landing=False):
        p, result = self.place, self.result(c)
        if stage == 0:
            made = []
            for k, peer in enumerate(p.peer_z):
                z = (p.z - k - 1 + p.deep) % p.deep if landing else p.z
                target = result.at[:, span(p.piece_at(z), p.piece), :]
                made.append(remote(self.piece(c), target, self.send_z.at[c, k], self.recv_z.at[c, k], peer))
            return made
        if stage == 1:
            source = result.at[:, span(p.quarter_at, p.quarter), :]
            target = result.at[:, span(p.quarter_off if landing else p.quarter_at, p.quarter), :]
            return [remote(source, target, self.send.at[c, 0], self.recv.at[c, 0], p.peer2)]
        if stage == 2:
            source = result.at[:, span(p.half_at, p.half), :]
            target = result.at[:, span(p.half_off if landing else p.half_at, p.half), :]
            return [remote(source, target, self.send.at[c, 1], self.recv.at[c, 1], p.peer1)]
        return [remote(result, self.mirror(c) if landing else result, self.send.at[c, 2], self.recv.at[c, 2], p.other)]

    def begin(self, c, stage):
        for copy in self.copies(c, stage):
            copy.start()

    def arrive(self, c, stage):
        for copy in self.copies(c, stage, landing=True):
            copy.wait_recv()

    def along_z(self, c):
        self.kept(c).start()
        self.begin(c, 0)

    def plane2(self, c):
        self.kept(c).wait()
        self.arrive(c, 0)
        self.begin(c, 1)

    def plane1(self, c):
        self.arrive(c, 1)
        self.begin(c, 2)

    def across(self, c):
        self.arrive(c, 2)
        self.begin(c, 3)

    def sent(self, c):
        for stage in range(3 if self.mirror is None else 4):
            for copy in self.copies(c, stage):
                copy.wait_send()


def vec_slot(slot, width):
    return slice(slot // 2, slot // 2 + 1), slice(slot % 2 * width, slot % 2 * width + width)


def mlp_staged_kernel(
    deep, images, slots, ticks,
    hid_ref, gm_ref, att_ref, mid_ref, sel_ref, sums_ref, w1a_ref, w1b_ref, b1a_ref, b1b_ref, w2a_ref, w2b_ref,
    wproj_ref, g2_ref, bfc2_ref,
    red_ref, gmid_ref, gatt_ref, dwp_ref, lo_ref, vec_ref,
    out_ref, gh_ref, bias_ref, give_ref, own_ref, got_core, got1, got2, got_z, send, recv, send_z, recv_z,
):
    step = pl.program_id(0)
    rows, width = hid_ref.shape
    place = Place(deep, width)
    panels = 4
    chunk = w1a_ref.shape[1]
    reduce = Reduce(
        place, lambda c: own_ref.at[c], lambda c: give_ref.at[c], lambda c: own_ref.at[c],
        got_core, got1, got2, got_z, send, recv, send_z, recv_z,
    )

    def put_red(c):
        red_ref[pl.ds(c * panels, panels)] = reduce.finish(c)

    def half(w1_ref, b1, w2_ref, target, db_row):
        hid, gm = hid_ref[...], gm_ref[...]
        w1, w2 = w1_ref[...], w2_ref[...]
        pre = dot(hid, w1) + bias_ref[b1, pl.ds(step, 1)]
        act, slope = gelu_pair(pre)
        act = act.astype(BF16)
        grad_act = dot_t(gm, w2).astype(BF16).astype(F32)
        grad_pre = (grad_act * slope).astype(BF16)
        d2 = t_dot(act, gm).astype(BF16)
        for j in range(width // 128):
            at = j % 3 * chunk
            target[2 + j // 3, at : at + chunk, :] = d2[:, j * 128 : j * 128 + 128]
        d1 = t_dot(hid, grad_pre).astype(BF16)
        target[0] = d1[:, :128]
        target[1] = d1[:, 128:]
        cols = pl.ds(pl.multiple_of(step * chunk, chunk), chunk)
        vec_ref[pl.ds(db_row, 1), cols] = jnp.sum(grad_pre.astype(F32), axis=0, keepdims=True)
        out_ref[...] += dot(act, w2)
        gh_ref[...] += dot_t(grad_pre, w1)

    @pl.when(step == 0)
    def _():
        place.greet()
        out_ref[...] = jnp.zeros_like(out_ref)
        gh_ref[...] = jnp.zeros_like(gh_ref)
        for side, ref in enumerate((b1a_ref, b1b_ref)):
            line = as_row(ref)
            for c in range(ticks):
                bias_ref[side, c : c + 1] = line[:, c * chunk : (c + 1) * chunk]
        place.all_here()

    @pl.when((step >= 1) & (step <= ticks))
    def _():
        reduce.plane1(step - 1)

    @pl.when((step >= 2) & (step <= ticks))
    def _():
        reduce.plane2(step - 2)

    @pl.when((step >= 3) & (step <= ticks))
    def _():
        reduce.along_z(step - 3)

    @pl.when((step >= 4) & (step <= ticks))
    def _():
        put_red(step - 4)

    @pl.when(step < ticks)
    def _():
        half(w1b_ref, 1, w2b_ref, give_ref.at[step], 7 - place.core)

    @pl.when(step < ticks)
    def _():
        reduce.begin(step, 0)
        half(w1a_ref, 0, w2a_ref, own_ref.at[step], 6 + place.core)

    def note(slot, value):
        at_row, at_col = vec_slot(slot, width)
        vec_ref[at_row, at_col] = value

    def column_sum(value):
        return jnp.sum(value, axis=0, keepdims=True)

    @pl.when(step == ticks)
    def _():
        stream = mlp_sq = jnp.zeros((1, width), F32)
        gain = shift = b_two = b_proj = jnp.zeros((1, width), F32)
        for i in range(images):
            here = slice(i * slots, i * slots + slots)
            sel = sel_ref[i]
            middle = mid_ref[here]
            valid = jnp.sum(sel.astype(F32), axis=1, keepdims=True) > 0
            mlp_out = jnp.where(valid, out_ref[here] + as_row(bfc2_ref), 0.0)
            block = middle + mlp_out
            kept = jnp.where(valid, block, 0.0)
            stream = stream + column_sum(kept * kept)
            mlp_sq = mlp_sq + column_sum(mlp_out * mlp_out)
            lo_ref[i] = t_dot(sel, block.astype(BF16)).astype(BF16)
            scaled, inverse = norm_rows(middle)
            grad_hidden = gh_ref[here]
            gain = gain + column_sum(grad_hidden * scaled)
            shift = shift + column_sum(grad_hidden)
            gm = gm_ref[here].astype(F32)
            b_two = b_two + column_sum(gm)
            grad_middle = gm + norm_back(grad_hidden * as_row(g2_ref), scaled, inverse)
            gmid_ref[here] = grad_middle
            grad_attn = grad_middle.astype(BF16)
            b_proj = b_proj + column_sum(grad_attn.astype(F32))
            hid_ref_out = grad_attn
            gatt_ref[here] = grad_attn
        for slot, value in enumerate((gain, shift, b_two, b_proj)):
            note(slot, value)
        note(8, stream)
        note(9, mlp_sq)
        note(10, sum(sums_ref[i, 0:1] for i in range(images)))
        note(11, sum(sums_ref[i, 1:2] for i in range(images)))
        reduce.plane2(ticks - 1)
        reduce.along_z(ticks - 2)
        put_red(ticks - 3)
        grad_attn = gatt_ref[...]
        for part in range(3):
            cols = slice(part * width // 3, (part + 1) * width // 3)
            d = t_dot(att_ref[...], grad_attn[:, cols]).astype(BF16)
            dwp_ref[0, part] = d[:, :128]
            dwp_ref[1, part] = d[:, 128:]
        reduce.along_z(ticks - 1)
        put_red(ticks - 2)
        gatt_ref[...] = dot_t(grad_attn, wproj_ref[...]).astype(BF16)
        put_red(ticks - 1)

        @pl.loop(0, ticks)
        def _(c):
            reduce.sent(c)


def attention_staged_kernel(
    deep, images, slots, groups, ticks,
    q_ref, k_ref, v_ref, probs_ref, gatt_ref, wq_ref, wk_ref, wv_ref, normed_ref, x_ref, gmid_ref, sel_ref, g1_ref,
    dwp_ref, red_ref, vecin_ref,
    mlp_ref, attn_ref, gi_ref, vec_ref,
    gq_ref, gk_ref, gv_ref, gn_ref, stage_ref, total_ref, piece_ref, got_core, got1, got2, got_z,
    vsum_ref, vgot_ref, vz_ref,
    send, recv, send_z, recv_z, m_local, m_send, m_recv, m_send_z, m_recv_z,
    a_local, a_send, a_recv, a_send_z, a_recv_z, v_send, v_recv, v_send_z, v_recv_z,
):
    step = pl.program_id(0)
    rows, width = x_ref.shape
    place = Place(deep, width)
    core = place.core
    polls = images + 2

    def partial_of(owner):
        def pick(c):
            if isinstance(c, int) and c == 0:
                return dwp_ref.at[owner]
            return stage_ref.at[c - 1, owner]

        return pick

    reduce = Reduce(
        place, partial_of(core), partial_of(1 - core), lambda c: total_ref.at[c],
        got_core, got1, got2, got_z, send, recv, send_z, recv_z,
    )
    back = Gather(
        place, lambda c: piece_ref.at[c], lambda c: attn_ref.at[core, pl.ds(3 * c, 3)],
        lambda c: attn_ref.at[1 - core, pl.ds(3 * c, 3)], a_local, a_send, a_recv, a_send_z, a_recv_z,
    )
    mlp = Gather(
        place, lambda c: red_ref.at[pl.ds(4 * c, 4)], lambda c: mlp_ref.at[pl.ds(4 * c, 4)], None,
        m_local, m_send, m_recv, m_send_z, m_recv_z,
    )

    def turn(c):
        piece_ref[c] = reduce.finish(c)
        back.along_z(c)

    def do(name, c):
        return {
            "X": reduce.plane1, "Y": reduce.plane2, "Z": reduce.along_z, "R": turn,
            "ay": back.plane2, "ax": back.plane1, "ac": back.across,
            "my": mlp.plane2, "mx": mlp.plane1,
        }[name](c)

    plan = {}
    for at, name, c in (
        (1, "X", 0), (3, "my", 0), (4, "Y", 0), (6, "mx", 0), (6, "Z", 0),
        (7, "my", 1), (8, "X", 1), (9, "R", 0), (10, "mx", 1), (11, "Y", 1), (11, "my", 2), (12, "ay", 0),
        (13, "Z", 1), (14, "mx", 2), (15, "X", 2), (15, "ax", 0), (16, "R", 1), (16, "my", 3), (18, "Y", 2),
        (18, "mx", 3), (19, "ay", 1), (20, "Z", 2),
    ):
        plan.setdefault(at, []).append((name, c))

    def run(at, now):
        for moment, jobs in sorted(plan.items()):
            if at(moment % polls):

                @pl.when(now == moment)
                def _(jobs=jobs):
                    for name, c in jobs:
                        do(name, c)

    first = lax.broadcasted_iota(jnp.int32, (1, 2 * HEAD_DIM), 1) < HEAD_DIM
    zero = jnp.zeros((), BF16)
    scale = jnp.asarray(HEAD_DIM ** -0.5, BF16)
    pairs = width // 128 // groups
    wide = pairs * 128

    @pl.when(step == 0)
    def _():
        place.greet()
        gn_ref[...] = jnp.zeros_like(gn_ref)
        vsum_ref[0] = vecin_ref[...]
        place.all_here()
        reduce.begin(0, 0)
        for c in range(ticks):
            mlp.along_z(c)

    @pl.when(step < groups)
    def _():
        @pl.loop(0, images)
        def _(i):
            run(lambda at: at < images, step * polls + i)
            here = pl.ds(pl.multiple_of(i * slots, 16), slots)
            for pair in range(pairs):
                own = slice(pair * 128, pair * 128 + 128)
                query, key, value = q_ref[here, own], k_ref[here, own], v_ref[here, own]
                grad_att = gatt_ref[here, own]
                gq = gk = gv = None
                for half in range(2):
                    mine = first if half == 0 else jnp.logical_not(first)
                    low = probs_ref[i, 2 * pair + half]
                    probs = low.astype(F32)
                    g_mine = jnp.where(mine, grad_att, zero)
                    grad_probs = dot_t(g_mine, value).astype(BF16).astype(F32)
                    inner = jnp.sum(probs * grad_probs, axis=1, keepdims=True)
                    grad_scores = (probs * (grad_probs - inner)).astype(BF16) * scale
                    tv = t_dot(low, g_mine)
                    tq = dot(grad_scores, jnp.where(mine, key, zero))
                    tk = t_dot(grad_scores, jnp.where(mine, query, zero))
                    gq = tq if gq is None else gq + tq
                    gk = tk if gk is None else gk + tk
                    gv = tv if gv is None else gv + tv
                gq_ref[here, own] = gq.astype(BF16)
                gk_ref[here, own] = gk.astype(BF16)
                gv_ref[here, own] = gv.astype(BF16)

        run(lambda at: at == images, step * polls + images)
        cols = pl.ds(pl.multiple_of(step * wide, wide), wide)
        shifted = pl.ds(pl.multiple_of(width + step * wide, wide), wide)
        vsum_ref[0, 2:3, cols] = jnp.sum(gq_ref[...].astype(F32), axis=0, keepdims=True)
        vsum_ref[0, 2:3, shifted] = jnp.sum(gv_ref[...].astype(F32), axis=0, keepdims=True)
        for part, (ref, w_ref) in enumerate(((gq_ref, wq_ref), (gk_ref, wk_ref), (gv_ref, wv_ref))):
            d = t_dot(normed_ref[...], ref[...]).astype(BF16)
            stage_ref[step, 0, part] = d[:, :128]
            stage_ref[step, 1, part] = d[:, 128:]
            gn_ref[...] += dot_t(ref[...], w_ref[...])
        reduce.begin(step + 1, 0)
        run(lambda at: at == images + 1, step * polls + images + 1)

    def vec_copies(stage):
        if stage < 3:
            peer = (place.other, place.peer1, place.peer2)[stage]
            return [remote(vsum_ref.at[stage], vgot_ref.at[stage], v_send.at[stage], v_recv.at[stage], peer)]
        return [
            remote(vsum_ref.at[3], vz_ref.at[k], v_send_z.at[k], v_recv_z.at[k], peer)
            for k, peer in enumerate(place.peer_z)
        ]

    def vec_begin(stage):
        for copy in vec_copies(stage):
            copy.start()

    def vec_next(stage):
        for copy in vec_copies(stage):
            copy.wait_recv()
        if stage < 3:
            vsum_ref[stage + 1] = vsum_ref[stage] + vgot_ref[stage]
            vec_begin(stage + 1)

    @pl.when(step == groups)
    def _():
        last = groups
        do("X", last)
        gain = shift = jnp.zeros((1, width), F32)
        for i in range(images):
            here = slice(i * slots, i * slots + slots)
            sel = sel_ref[i]
            scaled, inverse = norm_rows(x_ref[here].astype(F32))
            grad_normed = gn_ref[here]
            gain = gain + jnp.sum(grad_normed * scaled, axis=0, keepdims=True)
            shift = shift + jnp.sum(grad_normed, axis=0, keepdims=True)
            change = gmid_ref[here] + norm_back(grad_normed * as_row(g1_ref), scaled, inverse)
            high = change.astype(BF16)
            rest = (change - high.astype(F32)).astype(BF16)
            gi_ref[i] = t_dot(sel, high) + t_dot(sel, rest)
            if i == 1:
                do("R", 2)
                do("ax", 1)
                do("my", 4)
            if i == 3:
                do("Y", last)
                do("mx", 4)
                do("ac", 0)
        at_row, at_col = vec_slot(6, width)
        vsum_ref[0, at_row, at_col] = gain
        at_row, at_col = vec_slot(7, width)
        vsum_ref[0, at_row, at_col] = shift
        vec_begin(0)
        do("Z", last)
        do("ay", 2)
        vec_next(0)
        do("my", 5)
        do("R", last)
        vec_next(1)
        do("ax", 2)
        do("ac", 1)
        do("ay", last)
        vec_next(2)
        do("mx", 5)
        do("ax", last)
        vec_next(3)
        value = None
        for z in range(deep):
            mine = vsum_ref[3]
            from_k = [vz_ref[k] for k in range(deep - 1)]
            term = mine
            for k in range(deep - 1):
                term = jnp.where((place.z - k - 1 + deep) % deep == z, from_k[k], term)
            value = term if value is None else value + term
        vec_ref[...] = value
        do("ac", 2)
        do("ac", last)
        for c in range(ticks):
            mlp.arrive(c, 2)
            mlp.sent(c)
        for c in range(groups + 1):
            back.arrive(c, 3)
            back.sent(c)
            reduce.sent(c)
        for stage in range(4):
            for copy in vec_copies(stage):
                copy.wait_send()


def finish_kernel(
    groups,
    big_ref, attn_ref, low_ref, put_ref, img_ref, cot_ref, keep_ref, vec_ref,
    lo_ref, gi_ref, wq_ref, wp_ref, w1_ref, w2_ref, b1_ref, root_ref, *small_refs,
):
    step = pl.program_id(0)
    width = low_ref.shape[2]
    chunk = w1_ref.shape[1]
    for j in range(chunk // 128):
        w1_ref[:, j * 128 : j * 128 + 128] = big_ref[j].astype(F32)
    for j in range(width // 128):
        at = j % 3 * chunk
        w2_ref[:, j * 128 : j * 128 + 128] = big_ref[2 + j // 3, at : at + chunk].astype(F32)
    for owner in range(2):
        for j in range(3):
            at = (2 * j + owner) * 128
            wp_ref[:, at : at + 128] = attn_ref[owner, j].astype(F32)
            for group in range(groups):
                at = j * width + (2 * group + owner) * 128
                wq_ref[:, at : at + 128] = attn_ref[owner, 3 + 3 * group + j].astype(F32)

    @pl.when(step < keep_ref.shape[0])
    def _():
        keep = keep_ref[pl.ds(step, 1)].astype(F32)
        eight = jnp.broadcast_to(keep, (8, keep.shape[1])).astype(BF16)
        once = jnp.where(lax.broadcasted_iota(jnp.int32, (8, 128), 0) == 0, 1.0, 0.0).astype(BF16)
        kept = t_dot(eight, once)[:, 0:1] > 0.5
        lo_ref[0] = jnp.where(kept, low_ref[0], img_ref[0])
        gi_ref[0] = jnp.where(kept, put_ref[0], cot_ref[0].astype(F32))

    @pl.when(step == 0)
    def _():
        def line(slot):
            at_row, at_col = vec_slot(slot, width)
            return vec_ref[at_row, at_col]

        for slot, ref in enumerate(small_refs):
            ref[...] = line(slot).reshape(width)
        b1_ref[...] = vec_ref[pl.ds(6 + lax.axis_index("mlp"), 1)].reshape(2 * width)
        count = line(11)[:, 0:1]
        lane = lax.broadcasted_iota(jnp.int32, (1, 128), 1)
        sums = jnp.where(lane == 0, jnp.sum(line(8)), jnp.where(lane == 1, jnp.sum(line(10)), jnp.sum(line(9))))
        root_ref[...] = jnp.sqrt(sums / (count * width)).reshape(128)[:3]


def staged_device(
    deep, images, keep_mask, ln1_gain, ln1_bias, w_qkv, bias_q, bias_v, w_proj, b_proj,
    ln2_gain, ln2_bias, w_fc1, b_fc1, w_fc2, b_fc2, cotangent,
):
    count, patches, width = images.shape
    slots = slots_of(patches)
    rows = count * slots
    heads = width // HEAD_DIM
    shard = w_fc1.shape[1]
    row = lambda v: v.reshape(1, -1)
    shape = jax.ShapeDtypeStruct
    limit = 62 * 2**20
    any_space = pl.BlockSpec(memory_space=pl.ANY)
    per_image = lambda *tail: pl.BlockSpec((1,) + tail, lambda i: (i,) + (0,) * len(tail))
    per_rows = lambda cols: pl.BlockSpec((slots, cols), lambda i: (i, 0))
    dma = pltpu.SemaphoreType.DMA
    sel, x, normed, qkv, probs, att, mid, hid, gm, sums, far_w1, far_b1, far_w2 = pl.pallas_call(
        functools.partial(forward_kernel, slots, True),
        grid=(count,),
        out_shape=(
            shape((count, slots, patches), BF16),
            shape((rows, width), BF16),
            shape((rows, width), BF16),
            shape((rows, 3 * width), BF16),
            shape((count, heads, slots, slots), BF16),
            shape((rows, width), BF16),
            shape((rows, width), F32),
            shape((rows, width), BF16),
            shape((rows, width), BF16),
            shape((count, 8, width), F32),
            shape((width, shard), BF16), shape((shard,), BF16), shape((shard, width), BF16),
        ),
        in_specs=[
            whole((count, patches)), per_image(patches, width), per_image(patches, width),
            whole((width,)), whole((width,)), whole((width, 3 * width)), whole((width,)), whole((width,)),
            whole((width, width)), whole((width,)), whole((width,)), whole((width,)),
            any_space, any_space, any_space,
        ],
        out_specs=(
            per_image(slots, patches), per_rows(width), per_rows(width), per_rows(3 * width),
            per_image(heads, slots, slots), per_rows(width), per_rows(width), per_rows(width), per_rows(width),
            per_image(8, width), any_space, any_space, any_space,
        ),
        scratch_shapes=[dma((3,)), dma((3,))],
        compiler_params=pltpu.CompilerParams(vmem_limit_bytes=limit, collective_id=0, has_side_effects=True),
        name="attention_forward",
    )(
        keep_mask, images, cotangent, ln1_gain, ln1_bias, w_qkv, bias_q, bias_v, w_proj, b_proj, ln2_gain, ln2_bias,
        w_fc1, b_fc1, w_fc2,
    )
    chunk = 256
    ticks = shard // chunk
    groups = 3
    piece = width // 4 // deep
    by_cols = lambda *lead: pl.BlockSpec(lead + (chunk,), lambda c: (0, c - c // ticks))
    by_rows = pl.BlockSpec((chunk, width), lambda c: (c - c // ticks, 0))
    red, gmid, gatt, dwp, low, vec = pl.pallas_call(
        functools.partial(mlp_staged_kernel, deep, count, slots, ticks),
        grid=(ticks + 1,),
        out_shape=(
            shape((4 * ticks, piece, 128), BF16), shape((rows, width), F32), shape((rows, width), BF16),
            shape((2, 3, width, 128), BF16), shape((count, patches, width), BF16), shape((8, 2 * width), F32),
        ),
        in_specs=[
            whole((rows, width)), whole((rows, width)), whole((rows, width)), whole((rows, width)),
            whole((count, slots, patches)), whole((count, 8, width)),
            by_cols(width), by_cols(width), whole((shard,)), whole((shard,)), by_rows, by_rows,
            whole((width, width)), whole((width,)), whole((width,)),
        ],
        out_specs=(
            whole((4 * ticks, piece, 128)), whole((rows, width)), whole((rows, width)),
            whole((2, 3, width, 128)), whole((count, patches, width)), whole((8, 2 * width)),
        ),
        scratch_shapes=[
            pltpu.VMEM((rows, width), F32), pltpu.VMEM((rows, width), F32), pltpu.VMEM((2, 8, chunk), F32),
            pltpu.VMEM((ticks, 4, width, 128), BF16), pltpu.VMEM((ticks, 4, width, 128), BF16),
            pltpu.VMEM((ticks, 4, width, 128), BF16), pltpu.VMEM((ticks, 4, width // 2, 128), BF16),
            pltpu.VMEM((ticks, 4, width // 4, 128), BF16), pltpu.VMEM((ticks, deep - 1, 4, piece, 128), BF16),
            dma((ticks, 3)), dma((ticks, 3)), dma((ticks, deep - 1)), dma((ticks, deep - 1)),
        ],
        compiler_params=pltpu.CompilerParams(vmem_limit_bytes=limit, collective_id=1, has_side_effects=True),
        name="mlp_both_ways",
    )(
        hid, gm, att, mid, sel, sums, w_fc1, far_w1, b_fc1, far_b1, w_fc2, far_w2, w_proj, ln2_gain, b_fc2,
    )
    wide = width // groups
    chunks = groups + 1
    now = lambda g: g - g // groups
    third = lambda lead, part: pl.BlockSpec((lead, wide), lambda g: (0, part * groups + now(g)))
    big, attn, put, vec = pl.pallas_call(
        functools.partial(attention_staged_kernel, deep, count, slots, groups, ticks),
        grid=(groups + 1,),
        out_shape=(
            shape((4 * ticks, width, 128), BF16), shape((2, 3 * chunks, width, 128), BF16),
            shape((count, patches, width), F32), shape((8, 2 * width), F32),
        ),
        in_specs=[
            third(rows, 0), third(rows, 1), third(rows, 2),
            pl.BlockSpec((count, heads // groups, slots, slots), lambda g: (0, now(g), 0, 0)),
            third(rows, 0), third(width, 0), third(width, 1), third(width, 2),
            whole((rows, width)), whole((rows, width)), whole((rows, width)), whole((count, slots, patches)),
            whole((width,)), whole((2, 3, width, 128)), whole((4 * ticks, piece, 128)), whole((8, 2 * width)),
        ],
        out_specs=(any_space, any_space, whole((count, patches, width)), whole((8, 2 * width))),
        scratch_shapes=[
            pltpu.VMEM((rows, wide), BF16), pltpu.VMEM((rows, wide), BF16), pltpu.VMEM((rows, wide), BF16),
            pltpu.VMEM((rows, width), F32),
            pltpu.VMEM((groups, 2, 3, width, 128), BF16), pltpu.VMEM((chunks, 3, width, 128), BF16),
            pltpu.VMEM((chunks, 3, piece, 128), BF16), pltpu.VMEM((chunks, 3, width, 128), BF16),
            pltpu.VMEM((chunks, 3, width // 2, 128), BF16), pltpu.VMEM((chunks, 3, width // 4, 128), BF16),
            pltpu.VMEM((chunks, deep - 1, 3, piece, 128), BF16),
            pltpu.VMEM((4, 8, 2 * width), F32), pltpu.VMEM((3, 8, 2 * width), F32),
            pltpu.VMEM((deep - 1, 8, 2 * width), F32),
            dma((chunks, 3)), dma((chunks, 3)), dma((chunks, deep - 1)), dma((chunks, deep - 1)),
            dma((ticks,)), dma((ticks, 2)), dma((ticks, 2)), dma((ticks, deep - 1)), dma((ticks, deep - 1)),
            dma((chunks,)), dma((chunks, 3)), dma((chunks, 3)), dma((chunks, deep - 1)), dma((chunks, deep - 1)),
            dma((3,)), dma((3,)), dma((deep - 1,)), dma((deep - 1,)),
        ],
        compiler_params=pltpu.CompilerParams(vmem_limit_bytes=limit, collective_id=2, has_side_effects=True),
        name="attention_backward",
    )(
        qkv, qkv, qkv, probs, gatt, w_qkv, w_qkv, w_qkv, normed, x, gmid, sel, ln1_gain, dwp, red, vec,
    )
    deal = width // ticks
    turn = lambda t: (t - t // count, 0, 0)
    layer_out, grad_images, s_wq, s_wp, s_w1, s_w2, s_b1, root_means, *small = pl.pallas_call(
        functools.partial(finish_kernel, groups),
        grid=(ticks,),
        out_shape=(
            shape((count, patches, width), BF16), shape((count, patches, width), F32),
            shape((width, 3 * width), F32), shape((width, width), F32), shape((width, shard), F32),
            shape((shard, width), F32), shape((shard,), F32), shape((3,), F32),
        ) + 8 * (shape((width,), F32),),
        in_specs=[
            pl.BlockSpec((4, width, 128), lambda t: (t, 0, 0)),
            pl.BlockSpec((2, 3 * chunks, deal, 128), lambda t: (0, 0, t, 0)),
            pl.BlockSpec((1, patches, width), turn), pl.BlockSpec((1, patches, width), turn),
            pl.BlockSpec((1, patches, width), turn), pl.BlockSpec((1, patches, width), turn),
            whole((count, patches)), whole((8, 2 * width)),
        ],
        out_specs=(
            pl.BlockSpec((1, patches, width), turn), pl.BlockSpec((1, patches, width), turn),
            pl.BlockSpec((deal, 3 * width), lambda t: (t, 0)), pl.BlockSpec((deal, width), lambda t: (t, 0)),
            pl.BlockSpec((width, chunk), lambda t: (0, t)), pl.BlockSpec((chunk, width), lambda t: (t, 0)),
            whole((shard,)), whole((3,)),
        ) + 8 * (whole((width,)),),
        compiler_params=pltpu.CompilerParams(vmem_limit_bytes=limit),
        name="results",
    )(big, attn, low, put, images, cotangent, keep_mask, vec)
    gain2, shift2, b_two, b_project, b_query, b_value, gain1, shift1 = small
    return (
        layer_out, grad_images, gain1, shift1, s_wq, b_query, b_value, s_wp, b_project, gain2, shift2,
        s_w1, s_b1, s_w2, b_two, root_means,
    )


def solution(mesh):
    rows, line = P(("img", "mlp"), None, None), P(("img", "mlp"), None)
    deep = mesh.shape["img"] // 4
    staged = mesh.shape["img"] == 4 * deep and mesh.shape["mlp"] == 2 and 1 < deep <= 4
    return jax.shard_map(
        functools.partial(staged_device, deep) if staged else plain_device,
        mesh=mesh,
        in_specs=(
            rows, line, P(), P(), P(), P(), P(), P(), P(), P(), P(),
            P(None, "mlp"), P("mlp"), P("mlp", None), P(), rows,
        ),
        out_specs=(
            rows, rows, P(), P(), P(), P(), P(), P(), P(), P(), P(),
            P(None, "mlp"), P("mlp"), P("mlp", None), P(), P(),
        ),
        check_vma=False,
    )
```

```python
import functools

import jax
import jax.numpy as jnp
from jax import lax
from jax.experimental import pallas as pl
from jax.experimental.pallas import tpu as pltpu
from jax.sharding import PartitionSpec as P

HEAD_DIM = 64
NORM_EPS = 1e-06
F32 = jnp.float32
BF16 = jnp.bfloat16
MESH = pl.DeviceIdType.MESH
ERFC_POLY = (
    -0.05792342897865154,
    0.27982426175045266,
    -0.47905523971588865,
    0.27061712140601424,
    -0.022718349995155727,
    0.2015184791612061,
    0.24328701077158832,
    0.2823637910445855,
    0.2820864086305586,
)


def dot(a, b):
    return jnp.dot(a, b, preferred_element_type=F32)


def dot_t(a, b):
    return lax.dot_general(a, b, (((1,), (1,)), ((), ())), preferred_element_type=F32)


def t_dot(a, b):
    return lax.dot_general(a, b, (((0,), (0,)), ((), ())), preferred_element_type=F32)


def slots_of(patches):
    most = 4 * patches // 5
    return -(-most // 16) * 16


def norm_rows(rows):
    center = rows - jnp.mean(rows, axis=1, keepdims=True)
    inverse = lax.rsqrt(jnp.mean(center * center, axis=1, keepdims=True) + NORM_EPS)
    return center * inverse, inverse


def norm_back(weighted, scaled, inverse):
    return inverse * (
        weighted
        - jnp.mean(weighted, axis=1, keepdims=True)
        - scaled * jnp.mean(weighted * scaled, axis=1, keepdims=True)
    )


def gelu_pair(values):
    reach = jnp.abs(values) * 0.7071067811865476
    inv = 1.0 / (1.0 + 0.5 * reach)
    decay = jnp.exp(-0.5 * (values * values))
    poly = jnp.full_like(values, ERFC_POLY[0])
    for coefficient in ERFC_POLY[1:]:
        poly = poly * inv + coefficient
    tail = (0.5 * inv) * poly * decay
    share = jnp.where(values > 0, 1.0 - tail, tail)
    return values * share, share + values * (decay * 0.3989422804014327)


def swap_weights(ours, theirs, send_sem, recv_sem):
    other = {"mlp": 1 - lax.axis_index("mlp")}
    copies = [
        pltpu.make_async_remote_copy(
            src_ref=ours[j], dst_ref=theirs[j], send_sem=send_sem.at[j], recv_sem=recv_sem.at[j],
            device_id=other, device_id_type=MESH,
        )
        for j in range(len(ours))
    ]

    def trade(begin):
        @pl.when(pl.program_id(0) == (0 if begin else pl.num_programs(0) - 1))
        def _():
            if begin:
                barrier = pltpu.get_barrier_semaphore()
                pl.semaphore_signal(barrier, inc=1, device_id=other, device_id_type=MESH)
                pl.semaphore_wait(barrier, 1)
            for copy in copies:
                if begin:
                    copy.start()
                else:
                    copy.wait()

    return trade


def as_row(ref):
    return ref[...].astype(F32).reshape(1, -1)


def forward_kernel(
    slots, exchange,
    keep_ref, img_ref, cot_ref, g1_ref, b1_ref, wqkv_ref, bq_ref, bv_ref, wproj_ref, bproj_ref, g2_ref, b2_ref,
    *refs,
):
    if exchange:
        ours, refs, (send_sem, recv_sem) = refs[:3], refs[3:-2], refs[-2:]
        theirs, refs = refs[-3:], refs[:-3]
        trade = swap_weights(ours, theirs, send_sem, recv_sem)
        trade(True)
    sel_ref, x_ref, normed_ref, qkv_ref, probs_ref, att_ref, mid_ref, hid_ref, gm_ref, sums_ref = refs
    patches, width = img_ref.shape[1:]
    heads = width // HEAD_DIM
    keep = keep_ref[pl.ds(pl.program_id(0), 1)].astype(F32)
    upto = lax.broadcasted_iota(jnp.int32, (patches, patches), 0) <= lax.broadcasted_iota(
        jnp.int32, (patches, patches), 1
    )
    keep8 = jnp.broadcast_to(keep, (8, patches)).astype(BF16)
    rank = dot(keep8, upto.astype(F32).astype(BF16))[0:1]
    count = jnp.sum(keep, axis=1, keepdims=True)
    slot = lax.broadcasted_iota(jnp.int32, (slots, patches), 0).astype(F32)
    sel = jnp.where((slot == rank - 1.0) & (keep > 0), 1.0, 0.0).astype(BF16)
    sel_ref[0] = sel
    gm_ref[...] = dot(sel, cot_ref[0]).astype(BF16)
    rows = dot(sel, img_ref[0])
    x_ref[...] = rows.astype(BF16)
    scaled, _ = norm_rows(rows)
    normed = (scaled * as_row(g1_ref) + as_row(b1_ref)).astype(BF16)
    normed_ref[...] = normed
    for part in range(3):
        cols = slice(part * width, (part + 1) * width)
        block = dot(normed, wqkv_ref[:, cols])
        if part == 0:
            block = block + as_row(bq_ref)
        if part == 2:
            block = block + as_row(bv_ref)
        qkv_ref[:, cols] = block.astype(BF16)
    closed = jnp.where(
        lax.broadcasted_iota(jnp.int32, (1, slots), 1).astype(F32) < count, 0.0, -1e30
    )
    first = lax.broadcasted_iota(jnp.int32, (1, 2 * HEAD_DIM), 1) < HEAD_DIM
    zero = jnp.zeros((), BF16)
    for pair in range(heads // 2):
        lanes = slice(pair * 128, pair * 128 + 128)
        query = qkv_ref[:, lanes] * jnp.asarray(HEAD_DIM ** -0.5, BF16)
        key = qkv_ref[:, width + pair * 128 : width + pair * 128 + 128]
        value = qkv_ref[:, 2 * width + pair * 128 : 2 * width + pair * 128 + 128]
        total = None
        for half in range(2):
            mine = first if half == 0 else jnp.logical_not(first)
            scores = dot_t(query, jnp.where(mine, key, zero)) + closed
            raised = jnp.exp(scores - jnp.max(scores, axis=1, keepdims=True))
            probs = (raised * (1.0 / jnp.sum(raised, axis=1, keepdims=True))).astype(BF16)
            probs_ref[0, 2 * pair + half] = probs
            term = dot(probs, jnp.where(mine, value, zero))
            total = term if total is None else total + term
        att_ref[:, lanes] = total.astype(BF16)
    attn_out = dot(att_ref[...], wproj_ref[...]) + as_row(bproj_ref)
    valid = lax.broadcasted_iota(jnp.int32, (slots, 1), 0).astype(F32) < count
    attn_kept = jnp.where(valid, attn_out, 0.0)
    middle = rows + attn_kept
    mid_ref[...] = middle
    sums_ref[0, 0:1] = jnp.sum(attn_kept * attn_kept, axis=0, keepdims=True)
    sums_ref[0, 1:2] = jnp.broadcast_to(count, (1, width))
    scaled, _ = norm_rows(middle)
    hid_ref[...] = (scaled * as_row(g2_ref) + as_row(b2_ref)).astype(BF16)
    if exchange:
        trade(False)


def mlp_kernel(hid_ref, gm_ref, w1_ref, b1_ref, w2_ref, out_ref, gh_ref, dw1_ref, dw2_ref, db1_ref):
    step = pl.program_id(0)
    hid, gm = hid_ref[...], gm_ref[...]
    w1, w2 = w1_ref[0], w2_ref[0]
    pre = dot(hid, w1) + b1_ref[0].astype(F32)
    act, slope = gelu_pair(pre)
    act = act.astype(BF16)
    grad_act = dot_t(gm, w2).astype(BF16).astype(F32)
    grad_pre_f = grad_act * slope
    grad_pre = grad_pre_f.astype(BF16)
    dw2_ref[0] = t_dot(act, gm).astype(BF16)
    dw1_ref[0] = t_dot(hid, grad_pre).astype(BF16)
    db1_ref[0] = jnp.sum(grad_pre.astype(F32), axis=0, keepdims=True)

    @pl.when(step == 0)
    def _():
        out_ref[...] = dot(act, w2)
        gh_ref[...] = dot_t(grad_pre, w1)

    @pl.when(step > 0)
    def _():
        out_ref[...] += dot(act, w2)
        gh_ref[...] += dot_t(grad_pre, w1)


def backward_kernel(
    images, slots, groups,
    sel_ref, x_ref, normed_ref, qkv_ref, probs_ref, att_ref, mid_ref, gm_ref, gh_ref, mlp_ref, valid_ref,
    g1_ref, g2_ref, bfc2_ref, wqkv_ref, wproj_ref, img_ref, cot_ref,
    lo_ref, gi_ref, dwp_ref, dwq_ref, vec_ref,
    gmid_ref, gatt_ref, gq_ref, gk_ref, gv_ref, gn_ref,
):
    step = pl.program_id(0)
    rows, width = x_ref.shape

    @pl.when(step == 0)
    def _():
        middle = mid_ref[...]
        valid = valid_ref[...] > 0
        mlp_out = jnp.where(valid, mlp_ref[...] + bfc2_ref[...].astype(F32), 0.0)
        block = middle + mlp_out
        kept = jnp.where(valid, block, 0.0)
        vec_ref[8:9] = jnp.sum(kept * kept, axis=0, keepdims=True)
        vec_ref[9:10] = jnp.sum(mlp_out * mlp_out, axis=0, keepdims=True)
        low = block.astype(BF16)
        for i in range(images):
            put = t_dot(sel_ref[i], low[i * slots : (i + 1) * slots])
            here = jnp.sum(sel_ref[i].astype(F32), axis=0, keepdims=True)
            lo_ref[i] = put.astype(BF16)
        scaled, inverse = norm_rows(middle)
        grad_hidden = gh_ref[...]
        vec_ref[0:1] = jnp.sum(grad_hidden * scaled, axis=0, keepdims=True)
        vec_ref[1:2] = jnp.sum(grad_hidden, axis=0, keepdims=True)
        gm = gm_ref[...].astype(F32)
        vec_ref[2:3] = jnp.sum(gm, axis=0, keepdims=True)
        grad_middle = gm + norm_back(grad_hidden * g2_ref[...], scaled, inverse)
        gmid_ref[...] = grad_middle
        grad_attn = grad_middle.astype(BF16)
        vec_ref[3:4] = jnp.sum(grad_attn.astype(F32), axis=0, keepdims=True)
        dwp_ref[...] = t_dot(att_ref[...], grad_attn).astype(BF16)
        gatt_ref[...] = dot_t(grad_attn, wproj_ref[...]).astype(BF16)
        gn_ref[...] = jnp.zeros_like(gn_ref)

    first = lax.broadcasted_iota(jnp.int32, (1, 2 * HEAD_DIM), 1) < HEAD_DIM
    zero = jnp.zeros((), BF16)
    scale = jnp.asarray(HEAD_DIM ** -0.5, BF16)
    pairs = width // 128 // groups
    for group in range(groups):

        @pl.when(step == group + 1)
        def _():
            base = group * pairs * 128

            @pl.loop(0, images)
            def _(i):
                here = pl.ds(pl.multiple_of(i * slots, 16), slots)
                for pair in range(pairs):
                    at = base + pair * 128
                    own = slice(pair * 128, pair * 128 + 128)
                    query = qkv_ref[here, at : at + 128]
                    key = qkv_ref[here, width + at : width + at + 128]
                    value = qkv_ref[here, 2 * width + at : 2 * width + at + 128]
                    grad_att = gatt_ref[here, at : at + 128]
                    gq = gk = gv = None
                    for half in range(2):
                        mine = first if half == 0 else jnp.logical_not(first)
                        low = probs_ref[i, 2 * (base // 128 + pair) + half]
                        probs = low.astype(F32)
                        g_mine = jnp.where(mine, grad_att, zero)
                        grad_probs = dot_t(g_mine, value).astype(BF16).astype(F32)
                        inner = jnp.sum(probs * grad_probs, axis=1, keepdims=True)
                        grad_scores = (probs * (grad_probs - inner)).astype(BF16) * scale
                        tv = t_dot(low, g_mine)
                        tq = dot(grad_scores, jnp.where(mine, key, zero))
                        tk = t_dot(grad_scores, jnp.where(mine, query, zero))
                        gq = tq if gq is None else gq + tq
                        gk = tk if gk is None else gk + tk
                        gv = tv if gv is None else gv + tv
                    gq_ref[here, own] = gq.astype(BF16)
                    gk_ref[here, own] = gk.astype(BF16)
                    gv_ref[here, own] = gv.astype(BF16)

            span = pairs * 128
            vec_ref[4:5, base : base + span] = jnp.sum(gq_ref[...].astype(F32), axis=0, keepdims=True)
            vec_ref[5:6, base : base + span] = jnp.sum(gv_ref[...].astype(F32), axis=0, keepdims=True)
            for part, ref in enumerate((gq_ref, gk_ref, gv_ref)):
                cols = slice(part * width + base, part * width + base + span)
                dwq_ref[:, cols] = t_dot(normed_ref[...], ref[...]).astype(BF16)
                gn_ref[...] += dot_t(ref[...], wqkv_ref[:, cols])

    @pl.when(step == groups + 1)
    def _():
        scaled, inverse = norm_rows(x_ref[...].astype(F32))
        grad_normed = gn_ref[...]
        vec_ref[6:7] = jnp.sum(grad_normed * scaled, axis=0, keepdims=True)
        vec_ref[7:8] = jnp.sum(grad_normed, axis=0, keepdims=True)
        change = gmid_ref[...] + norm_back(grad_normed * g1_ref[...], scaled, inverse)
        high = change.astype(BF16)
        rest = (change - high.astype(F32)).astype(BF16)
        for i in range(images):
            here = slice(i * slots, (i + 1) * slots)
            gi_ref[i] = t_dot(sel_ref[i], high[here]) + t_dot(sel_ref[i], rest[here])


def whole(shape):
    return pl.BlockSpec(shape, lambda *_: (0,) * len(shape), pipeline_mode=pl.Buffered(1))


def plain_device(
    images, keep_mask, ln1_gain, ln1_bias, w_qkv, bias_q, bias_v, w_proj, b_proj,
    ln2_gain, ln2_bias, w_fc1, b_fc1, w_fc2, b_fc2, cotangent,
):
    count, patches, width = images.shape
    slots = slots_of(patches)
    rows = count * slots
    heads = width // HEAD_DIM
    shard = w_fc1.shape[1]
    row = lambda v: v.reshape(1, -1)
    whole_w1 = lax.all_gather(w_fc1, "mlp")
    whole_w2 = lax.all_gather(w_fc2, "mlp")
    whole_b1 = lax.all_gather(b_fc1, "mlp").reshape(2, 1, shard)
    shape = jax.ShapeDtypeStruct
    limit = pltpu.CompilerParams(vmem_limit_bytes=60 * 2**20)
    per_image = lambda *tail: pl.BlockSpec((1,) + tail, lambda i: (i,) + (0,) * len(tail))
    per_rows = lambda cols: pl.BlockSpec((slots, cols), lambda i: (i, 0))
    sel, x, normed, qkv, probs, att, mid, hid, gm, sums = pl.pallas_call(
        functools.partial(forward_kernel, slots, False),
        grid=(count,),
        out_shape=(
            shape((count, slots, patches), BF16),
            shape((rows, width), BF16),
            shape((rows, width), BF16),
            shape((rows, 3 * width), BF16),
            shape((count, heads, slots, slots), BF16),
            shape((rows, width), BF16),
            shape((rows, width), F32),
            shape((rows, width), BF16),
            shape((rows, width), BF16),
            shape((count, 8, width), F32),
        ),
        in_specs=[
            whole((count, patches)), per_image(patches, width), per_image(patches, width),
            whole((width,)), whole((width,)), whole((width, 3 * width)), whole((width,)), whole((width,)),
            whole((width, width)), whole((width,)), whole((width,)), whole((width,)),
        ],
        out_specs=(
            per_image(slots, patches), per_rows(width), per_rows(width), per_rows(3 * width),
            per_image(heads, slots, slots), per_rows(width), per_rows(width), per_rows(width), per_rows(width),
            per_image(8, width),
        ),
        compiler_params=limit,
        name="attention_forward",
    )(
        keep_mask, images, cotangent, ln1_gain, ln1_bias, w_qkv, bias_q, bias_v, w_proj, b_proj, ln2_gain, ln2_bias,
    )
    chunk = 512 if shard % 512 == 0 else 256
    each = shard // chunk
    mlp_out, grad_hidden, dw1, dw2, db1 = pl.pallas_call(
        mlp_kernel,
        grid=(2 * each,),
        out_shape=(
            shape((rows, width), F32), shape((rows, width), F32),
            shape((2, width, shard), BF16), shape((2, shard, width), BF16), shape((2, 1, shard), F32),
        ),
        in_specs=[
            whole((rows, width)), whole((rows, width)),
            pl.BlockSpec((1, width, chunk), lambda c: (c // each, 0, c % each)),
            pl.BlockSpec((1, 1, chunk), lambda c: (c // each, 0, c % each)),
            pl.BlockSpec((1, chunk, width), lambda c: (c // each, c % each, 0)),
        ],
        out_specs=(
            whole((rows, width)), whole((rows, width)),
            pl.BlockSpec((1, width, chunk), lambda c: (c // each, 0, c % each)),
            pl.BlockSpec((1, chunk, width), lambda c: (c // each, c % each, 0)),
            pl.BlockSpec((1, 1, chunk), lambda c: (c // each, 0, c % each)),
        ),
        compiler_params=limit,
        name="mlp_both_ways",
    )(hid, gm, whole_w1, whole_b1, whole_w2)
    kept = jnp.sum(keep_mask, axis=1, keepdims=True)
    valid = (jnp.arange(slots, dtype=jnp.int32)[None, :] < kept).astype(F32).reshape(rows, 1)
    groups = 3
    span = width // groups
    low, put, dwp, dwq, vec = pl.pallas_call(
        functools.partial(backward_kernel, count, slots, groups),
        grid=(groups + 2,),
        out_shape=(
            shape((count, patches, width), BF16), shape((count, patches, width), F32),
            shape((width, width), BF16), shape((width, 3 * width), BF16), shape((16, width), F32),
        ),
        in_specs=[
            whole((count, slots, patches)), whole((rows, width)), whole((rows, width)), whole((rows, 3 * width)),
            whole((count, heads, slots, slots)), whole((rows, width)), whole((rows, width)), whole((rows, width)),
            whole((rows, width)), whole((rows, width)), whole((rows, 1)),
            whole((1, width)), whole((1, width)), whole((1, width)), whole((width, 3 * width)), whole((width, width)),
            pl.BlockSpec(memory_space=pl.ANY), pl.BlockSpec(memory_space=pl.ANY),
        ],
        out_specs=(
            whole((count, patches, width)), whole((count, patches, width)),
            whole((width, width)), whole((width, 3 * width)), whole((16, width)),
        ),
        scratch_shapes=[
            pltpu.VMEM((rows, width), F32), pltpu.VMEM((rows, width), BF16),
            pltpu.VMEM((rows, span), BF16), pltpu.VMEM((rows, span), BF16), pltpu.VMEM((rows, span), BF16),
            pltpu.VMEM((rows, width), F32),
        ],
        compiler_params=limit,
        name="attention_backward",
    )(
        sel, x, normed, qkv, probs, att, mid, gm, grad_hidden, mlp_out, valid,
        row(ln1_gain), row(ln2_gain), row(b_fc2), w_qkv, w_proj, images, cotangent,
    )
    kept_at = (keep_mask > 0)[:, :, None]
    layer_out = jnp.where(kept_at, low, images)
    grad_images = jnp.where(kept_at, put, cotangent.astype(F32))
    both = ("img", "mlp")
    place = lax.axis_index("mlp")
    dw1s = lax.psum_scatter(dw1.reshape(2 * width, shard), "mlp", scatter_dimension=0, tiled=True)
    dw2s = lax.psum_scatter(dw2.reshape(2 * shard, width), "mlp", scatter_dimension=0, tiled=True)
    s_w1, s_w2 = lax.psum((dw1s, dw2s), "img")
    s_wq, s_wp = lax.psum((dwq, dwp), both)
    vec, sums, s_b1 = lax.psum((vec, jnp.sum(sums, axis=0), db1.reshape(2, shard)), both)
    s_b1 = lax.dynamic_index_in_dim(s_b1, place, 0, keepdims=False)
    stream_sq, mlp_sq, attn_sq = jnp.sum(vec[8]), jnp.sum(vec[9]), jnp.sum(sums[0])
    root_means = jnp.sqrt(jnp.stack([stream_sq, attn_sq, mlp_sq]) / (sums[1, 0] * width))
    f = lambda v: v.astype(F32)
    return (
        layer_out, grad_images, vec[6], vec[7], f(s_wq), vec[4], vec[5], f(s_wp), vec[3], vec[0], vec[1],
        f(s_w1), s_b1, f(s_w2), vec[2], root_means,
    )


class Place:
    def __init__(self, deep, width):
        spot, self.core = lax.axis_index("img"), lax.axis_index("mlp")
        x, y, self.z = spot % 2, (spot // 2) % 2, spot // 4
        core = self.core
        self.bit1 = x * (1 - core) + y * core
        self.bit2 = y * (1 - core) + x * core
        step_x, step_y = 1 - 2 * x, 2 - 4 * y
        self.deep = deep
        self.other = {"mlp": 1 - core}
        self.peer1 = {"img": spot + step_x * (1 - core) + step_y * core}
        self.peer2 = {"img": spot + step_y * (1 - core) + step_x * core}
        self.peer_z = [{"img": ((self.z + k) % deep) * 4 + spot % 4} for k in range(1, deep)]
        self.half, self.quarter = width // 2, width // 4
        self.piece = width // 4 // deep
        self.half_at = self.bit1 * self.half
        self.half_off = (1 - self.bit1) * self.half
        self.quarter_at = self.half_at + self.bit2 * self.quarter
        self.quarter_off = self.half_at + (1 - self.bit2) * self.quarter

    def piece_at(self, z):
        return self.quarter_at + z * self.piece

    def everyone(self):
        return [self.other, self.peer1, self.peer2] + self.peer_z

    def greet(self):
        for peer in self.everyone():
            pl.semaphore_signal(pltpu.get_barrier_semaphore(), inc=1, device_id=peer, device_id_type=MESH)

    def all_here(self):
        pl.semaphore_wait(pltpu.get_barrier_semaphore(), len(self.everyone()))


def span(start, size):
    return pl.ds(pl.multiple_of(start, 16), size)


def remote(source, target, send_sem, recv_sem, peer):
    return pltpu.make_async_remote_copy(
        src_ref=source, dst_ref=target, send_sem=send_sem, recv_sem=recv_sem, device_id=peer, device_id_type=MESH
    )


def added(left, right):
    return (left.astype(F32) + right.astype(F32)).astype(BF16)


class Reduce:
    def __init__(self, place, partial, sending, total, got_core, got1, got2, got_z, send, recv, send_z, recv_z):
        self.place, self.partial, self.sending, self.total = place, partial, sending, total
        self.got_core, self.got1, self.got2, self.got_z = got_core, got1, got2, got_z
        self.send, self.recv, self.send_z, self.recv_z = send, recv, send_z, recv_z

    def copies(self, c, stage):
        p = self.place
        if stage == 0:
            return [remote(self.sending(c), self.got_core.at[c], self.send.at[c, 0], self.recv.at[c, 0], p.other)]
        total = self.total(c)
        if stage == 1:
            part = total.at[:, span(p.half_off, p.half), :]
            return [remote(part, self.got1.at[c], self.send.at[c, 1], self.recv.at[c, 1], p.peer1)]
        if stage == 2:
            part = total.at[:, span(p.quarter_off, p.quarter), :]
            return [remote(part, self.got2.at[c], self.send.at[c, 2], self.recv.at[c, 2], p.peer2)]
        made = []
        for k, peer in enumerate(p.peer_z):
            part = total.at[:, span(p.piece_at((p.z + k + 1) % p.deep), p.piece), :]
            made.append(remote(part, self.got_z.at[c, k], self.send_z.at[c, k], self.recv_z.at[c, k], peer))
        return made

    def begin(self, c, stage):
        for copy in self.copies(c, stage):
            copy.start()

    def arrive(self, c, stage):
        for copy in self.copies(c, stage):
            copy.wait_recv()

    def sent(self, c):
        for stage in range(4):
            for copy in self.copies(c, stage):
                copy.wait_send()

    def plane1(self, c):
        self.arrive(c, 0)
        total, partial, got = self.total(c), self.partial(c), self.got_core.at[c]
        total[...] = added(partial[...], got[...])
        self.begin(c, 1)

    def plane2(self, c):
        p = self.place
        self.arrive(c, 1)
        rows = span(p.half_at, p.half)
        total = self.total(c)
        total[:, rows, :] = added(total[:, rows, :], self.got1[c])
        self.begin(c, 2)

    def along_z(self, c):
        p = self.place
        self.arrive(c, 2)
        rows = span(p.quarter_at, p.quarter)
        total = self.total(c)
        total[:, rows, :] = added(total[:, rows, :], self.got2[c])
        self.begin(c, 3)

    def finish(self, c):
        p = self.place
        self.arrive(c, 3)
        rows = span(p.piece_at(p.z), p.piece)
        value = self.total(c)[:, rows, :].astype(F32)
        for k in range(p.deep - 1):
            value = value + self.got_z[c, k].astype(F32)
        return value.astype(BF16)


class Gather:
    def __init__(self, place, piece, result, mirror, local, send, recv, send_z, recv_z):
        self.place, self.piece, self.result, self.mirror, self.local = place, piece, result, mirror, local
        self.send, self.recv, self.send_z, self.recv_z = send, recv, send_z, recv_z

    def kept(self, c):
        p = self.place
        return pltpu.make_async_copy(
            self.piece(c), self.result(c).at[:, span(p.piece_at(p.z), p.piece), :], self.local.at[c]
        )

    def copies(self, c, stage, landing=False):
        p, result = self.place, self.result(c)
        if stage == 0:
            made = []
            for k, peer in enumerate(p.peer_z):
                z = (p.z - k - 1 + p.deep) % p.deep if landing else p.z
                target = result.at[:, span(p.piece_at(z), p.piece), :]
                made.append(remote(self.piece(c), target, self.send_z.at[c, k], self.recv_z.at[c, k], peer))
            return made
        if stage == 1:
            source = result.at[:, span(p.quarter_at, p.quarter), :]
            target = result.at[:, span(p.quarter_off if landing else p.quarter_at, p.quarter), :]
            return [remote(source, target, self.send.at[c, 0], self.recv.at[c, 0], p.peer2)]
        if stage == 2:
            source = result.at[:, span(p.half_at, p.half), :]
            target = result.at[:, span(p.half_off if landing else p.half_at, p.half), :]
            return [remote(source, target, self.send.at[c, 1], self.recv.at[c, 1], p.peer1)]
        return [remote(result, self.mirror(c) if landing else result, self.send.at[c, 2], self.recv.at[c, 2], p.other)]

    def begin(self, c, stage):
        for copy in self.copies(c, stage):
            copy.start()

    def arrive(self, c, stage):
        for copy in self.copies(c, stage, landing=True):
            copy.wait_recv()

    def along_z(self, c):
        self.kept(c).start()
        self.begin(c, 0)

    def plane2(self, c):
        self.kept(c).wait()
        self.arrive(c, 0)
        self.begin(c, 1)

    def plane1(self, c):
        self.arrive(c, 1)
        self.begin(c, 2)

    def across(self, c):
        self.arrive(c, 2)
        self.begin(c, 3)

    def sent(self, c):
        for stage in range(3 if self.mirror is None else 4):
            for copy in self.copies(c, stage):
                copy.wait_send()


def vec_slot(slot, width):
    return slice(slot // 2, slot // 2 + 1), slice(slot % 2 * width, slot % 2 * width + width)


def mlp_staged_kernel(
    deep, images, slots, ticks,
    hid_ref, gm_ref, att_ref, mid_ref, sel_ref, sums_ref, w1a_ref, w1b_ref, b1a_ref, b1b_ref, w2a_ref, w2b_ref,
    wproj_ref, g2_ref, bfc2_ref,
    red_ref, gmid_ref, gatt_ref, dwp_ref, lo_ref, vec_ref, early_ref,
    out_ref, gh_ref, bias_ref, give_ref, own_ref, got_core, got1, got2, got_z, send, recv, send_z, recv_z,
    b_local, b_send, b_recv, b_send_z, b_recv_z,
):
    step = pl.program_id(0)
    rows, width = hid_ref.shape
    place = Place(deep, width)
    panels = 4
    chunk = w1a_ref.shape[1]
    reduce = Reduce(
        place, lambda c: own_ref.at[c], lambda c: give_ref.at[c], lambda c: own_ref.at[c],
        got_core, got1, got2, got_z, send, recv, send_z, recv_z,
    )

    back = Gather(
        place, lambda c: red_ref.at[pl.ds(c * panels, panels)], lambda c: early_ref.at[pl.ds(c * panels, panels)],
        None, b_local, b_send, b_recv, b_send_z, b_recv_z,
    )
    early = early_ref.shape[0] // panels

    def put_red(c):
        red_ref[pl.ds(c * panels, panels)] = reduce.finish(c)

    def half(w1_ref, b1, w2_ref, target, db_row):
        hid, gm = hid_ref[...], gm_ref[...]
        w1, w2 = w1_ref[...], w2_ref[...]
        pre = dot(hid, w1) + bias_ref[b1, pl.ds(step, 1)]
        act, slope = gelu_pair(pre)
        act = act.astype(BF16)
        grad_act = dot_t(gm, w2).astype(BF16).astype(F32)
        grad_pre = (grad_act * slope).astype(BF16)
        d2 = t_dot(act, gm).astype(BF16)
        for j in range(width // 128):
            at = j % 3 * chunk
            target[2 + j // 3, at : at + chunk, :] = d2[:, j * 128 : j * 128 + 128]
        d1 = t_dot(hid, grad_pre).astype(BF16)
        target[0] = d1[:, :128]
        target[1] = d1[:, 128:]
        cols = pl.ds(pl.multiple_of(step * chunk, chunk), chunk)
        vec_ref[pl.ds(db_row, 1), cols] = jnp.sum(grad_pre.astype(F32), axis=0, keepdims=True)
        out_ref[...] += dot(act, w2)
        gh_ref[...] += dot_t(grad_pre, w1)

    @pl.when(step == 0)
    def _():
        place.greet()
        out_ref[...] = jnp.zeros_like(out_ref)
        gh_ref[...] = jnp.zeros_like(gh_ref)
        for side, ref in enumerate((b1a_ref, b1b_ref)):
            line = as_row(ref)
            for c in range(ticks):
                bias_ref[side, c : c + 1] = line[:, c * chunk : (c + 1) * chunk]
        place.all_here()

    @pl.when((step >= 1) & (step <= ticks))
    def _():
        reduce.plane1(step - 1)

    @pl.when(step == ticks)
    def _():
        back.plane1(0)

    @pl.when((step >= 2) & (step <= ticks))
    def _():
        reduce.plane2(step - 2)

    @pl.when((step >= 3) & (step <= ticks))
    def _():
        reduce.along_z(step - 3)

    @pl.when((step >= 4) & (step <= ticks))
    def _():
        put_red(step - 4)
        back.along_z(step - 4)

    @pl.when(step < ticks)
    def _():
        half(w1b_ref, 1, w2b_ref, give_ref.at[step], 7 - place.core)

    @pl.when(step == ticks - 1)
    def _():
        back.plane2(0)

    @pl.when(step < ticks)
    def _():
        reduce.begin(step, 0)
        half(w1a_ref, 0, w2a_ref, own_ref.at[step], 6 + place.core)

    def note(slot, value):
        at_row, at_col = vec_slot(slot, width)
        vec_ref[at_row, at_col] = value

    def column_sum(value):
        return jnp.sum(value, axis=0, keepdims=True)

    @pl.when(step == ticks)
    def _():
        stream = mlp_sq = jnp.zeros((1, width), F32)
        gain = shift = b_two = b_proj = jnp.zeros((1, width), F32)
        for i in range(images):
            here = slice(i * slots, i * slots + slots)
            sel = sel_ref[i]
            middle = mid_ref[here]
            valid = jnp.sum(sel.astype(F32), axis=1, keepdims=True) > 0
            mlp_out = jnp.where(valid, out_ref[here] + as_row(bfc2_ref), 0.0)
            block = middle + mlp_out
            kept = jnp.where(valid, block, 0.0)
            stream = stream + column_sum(kept * kept)
            mlp_sq = mlp_sq + column_sum(mlp_out * mlp_out)
            lo_ref[i] = t_dot(sel, block.astype(BF16)).astype(BF16)
            scaled, inverse = norm_rows(middle)
            grad_hidden = gh_ref[here]
            gain = gain + column_sum(grad_hidden * scaled)
            shift = shift + column_sum(grad_hidden)
            gm = gm_ref[here].astype(F32)
            b_two = b_two + column_sum(gm)
            grad_middle = gm + norm_back(grad_hidden * as_row(g2_ref), scaled, inverse)
            gmid_ref[here] = grad_middle
            grad_attn = grad_middle.astype(BF16)
            b_proj = b_proj + column_sum(grad_attn.astype(F32))
            gatt_ref[here] = grad_attn
            if i == 2:
                back.plane2(1)
        for slot, value in enumerate((gain, shift, b_two, b_proj)):
            note(slot, value)
        note(8, stream)
        note(9, mlp_sq)
        note(10, sum(sums_ref[i, 0:1] for i in range(images)))
        note(11, sum(sums_ref[i, 1:2] for i in range(images)))
        reduce.plane2(ticks - 1)
        reduce.along_z(ticks - 2)
        put_red(ticks - 3)
        back.plane1(1)
        back.plane2(2)
        grad_attn = gatt_ref[...]
        for part in range(3):
            cols = slice(part * width // 3, (part + 1) * width // 3)
            d = t_dot(att_ref[...], grad_attn[:, cols]).astype(BF16)
            dwp_ref[0, part] = d[:, :128]
            dwp_ref[1, part] = d[:, 128:]
        reduce.along_z(ticks - 1)
        put_red(ticks - 2)
        gatt_ref[...] = dot_t(grad_attn, wproj_ref[...]).astype(BF16)
        back.plane1(2)
        put_red(ticks - 1)

        @pl.loop(0, ticks)
        def _(c):
            reduce.sent(c)

        @pl.loop(0, early)
        def _(c):
            back.arrive(c, 2)
            back.sent(c)


def attention_staged_kernel(
    deep, images, slots, groups, ticks,
    q_ref, k_ref, v_ref, probs_ref, gatt_ref, wq_ref, wk_ref, wv_ref, normed_ref, x_ref, gmid_ref, sel_ref, g1_ref,
    dwp_ref, red_ref, vecin_ref,
    mlp_ref, attn_ref, gi_ref, vec_ref,
    gq_ref, gk_ref, gv_ref, gn_ref, stage_ref, total_ref, piece_ref, got_core, got1, got2, got_z,
    vsum_ref, vgot_ref, vz_ref,
    send, recv, send_z, recv_z, m_local, m_send, m_recv, m_send_z, m_recv_z,
    a_local, a_send, a_recv, a_send_z, a_recv_z, v_send, v_recv, v_send_z, v_recv_z,
):
    step = pl.program_id(0)
    rows, width = x_ref.shape
    place = Place(deep, width)
    core = place.core
    polls = images + 2

    def partial_of(owner):
        def pick(c):
            if isinstance(c, int) and c == 0:
                return dwp_ref.at[owner]
            return stage_ref.at[c - 1, owner]

        return pick

    reduce = Reduce(
        place, partial_of(core), partial_of(1 - core), lambda c: total_ref.at[c],
        got_core, got1, got2, got_z, send, recv, send_z, recv_z,
    )
    back = Gather(
        place, lambda c: piece_ref.at[c], lambda c: attn_ref.at[core, pl.ds(3 * c, 3)],
        lambda c: attn_ref.at[1 - core, pl.ds(3 * c, 3)], a_local, a_send, a_recv, a_send_z, a_recv_z,
    )
    late = mlp_ref.shape[0] // 4
    mlp = Gather(
        place, lambda c: red_ref.at[pl.ds(4 * (ticks - late + c), 4)], lambda c: mlp_ref.at[pl.ds(4 * c, 4)], None,
        m_local, m_send, m_recv, m_send_z, m_recv_z,
    )

    def turn(c):
        piece_ref[c] = reduce.finish(c)
        back.along_z(c)

    def do(name, c):
        return {
            "X": reduce.plane1, "Y": reduce.plane2, "Z": reduce.along_z, "R": turn,
            "ay": back.plane2, "ax": back.plane1, "ac": back.across,
            "my": mlp.plane2, "mx": mlp.plane1,
        }[name](c - (ticks - late) if name[0] == "m" else c)

    plan = {}
    for at, name, c in (
        (2, "X", 0), (6, "Y", 0), (8, "my", 3), (9, "X", 1), (9, "my", 4), (10, "Z", 0), (12, "my", 5),
        (13, "mx", 3), (15, "R", 0), (16, "X", 2), (16, "Y", 1), (20, "ay", 0), (20, "Z", 1), (23, "X", 3),
    ):
        plan.setdefault(at, []).append((name, c))
    tail = (
        ("ax", 0), ("Y", 2), ("R", 1), ("Y", 3), ("Z", 2), ("mx", 5), ("ay", 1), ("Z", 3), ("ac", 0), ("R", 2),
        ("ax", 1), ("R", 3), ("mx", 4), ("ac", 1), ("ay", 2), ("ay", 3), ("ax", 2), ("ax", 3), ("ac", 2),
        ("ac", 3),
    )

    def run(at, now):
        for moment, jobs in sorted(plan.items()):
            if moment < groups * polls and at(moment % polls):

                @pl.when(now == moment)
                def _(jobs=jobs):
                    for name, c in jobs:
                        do(name, c)

    first = lax.broadcasted_iota(jnp.int32, (1, 2 * HEAD_DIM), 1) < HEAD_DIM
    zero = jnp.zeros((), BF16)
    scale = jnp.asarray(HEAD_DIM ** -0.5, BF16)
    pairs = width // 128 // groups
    wide = pairs * 128

    @pl.when(step == 0)
    def _():
        place.greet()
        gn_ref[...] = jnp.zeros_like(gn_ref)
        vsum_ref[0] = vecin_ref[...]
        place.all_here()
        reduce.begin(0, 0)
        for c in range(late):
            mlp.along_z(c)

    @pl.when(step < groups)
    def _():
        @pl.loop(0, images)
        def _(i):
            run(lambda at: at < images, step * polls + i)
            here = pl.ds(pl.multiple_of(i * slots, 16), slots)
            for pair in range(pairs):
                own = slice(pair * 128, pair * 128 + 128)
                query, key, value = q_ref[here, own], k_ref[here, own], v_ref[here, own]
                grad_att = gatt_ref[here, own]
                gq = gk = gv = None
                for half in range(2):
                    mine = first if half == 0 else jnp.logical_not(first)
                    low = probs_ref[i, 2 * pair + half]
                    probs = low.astype(F32)
                    g_mine = jnp.where(mine, grad_att, zero)
                    grad_probs = dot_t(g_mine, value).astype(BF16).astype(F32)
                    inner = jnp.sum(probs * grad_probs, axis=1, keepdims=True)
                    grad_scores = (probs * (grad_probs - inner)).astype(BF16) * scale
                    tv = t_dot(low, g_mine)
                    tq = dot(grad_scores, jnp.where(mine, key, zero))
                    tk = t_dot(grad_scores, jnp.where(mine, query, zero))
                    gq = tq if gq is None else gq + tq
                    gk = tk if gk is None else gk + tk
                    gv = tv if gv is None else gv + tv
                gq_ref[here, own] = gq.astype(BF16)
                gk_ref[here, own] = gk.astype(BF16)
                gv_ref[here, own] = gv.astype(BF16)

        run(lambda at: at == images, step * polls + images)
        cols = pl.ds(pl.multiple_of(step * wide, wide), wide)
        shifted = pl.ds(pl.multiple_of(width + step * wide, wide), wide)
        vsum_ref[0, 2:3, cols] = jnp.sum(gq_ref[...].astype(F32), axis=0, keepdims=True)
        vsum_ref[0, 2:3, shifted] = jnp.sum(gv_ref[...].astype(F32), axis=0, keepdims=True)
        for part, ref in enumerate((gq_ref, gk_ref, gv_ref)):
            d = t_dot(normed_ref[...], ref[...]).astype(BF16)
            stage_ref[step, 0, part] = d[:, :128]
            stage_ref[step, 1, part] = d[:, 128:]
        reduce.begin(step + 1, 0)
        for ref, w_ref in ((gq_ref, wq_ref), (gk_ref, wk_ref), (gv_ref, wv_ref)):
            gn_ref[...] += dot_t(ref[...], w_ref[...])
        run(lambda at: at == images + 1, step * polls + images + 1)

    def vec_copies(stage):
        if stage < 3:
            peer = (place.other, place.peer1, place.peer2)[stage]
            return [remote(vsum_ref.at[stage], vgot_ref.at[stage], v_send.at[stage], v_recv.at[stage], peer)]
        return [
            remote(vsum_ref.at[3], vz_ref.at[k], v_send_z.at[k], v_recv_z.at[k], peer)
            for k, peer in enumerate(place.peer_z)
        ]

    def vec_begin(stage):
        for copy in vec_copies(stage):
            copy.start()

    def vec_next(stage):
        for copy in vec_copies(stage):
            copy.wait_recv()
        if stage < 3:
            vsum_ref[stage + 1] = vsum_ref[stage] + vgot_ref[stage]
            vec_begin(stage + 1)

    @pl.when(step == groups)
    def _():
        g1 = as_row(g1_ref)
        gain = shift = jnp.zeros((1, width), F32)
        for i in range(images):
            for name, c in plan.get(groups * polls + i, ()):
                do(name, c)
            here = slice(i * slots, i * slots + slots)
            sel = sel_ref[i]
            scaled, inverse = norm_rows(x_ref[here].astype(F32))
            grad_normed = gn_ref[here]
            gain = gain + jnp.sum(grad_normed * scaled, axis=0, keepdims=True)
            shift = shift + jnp.sum(grad_normed, axis=0, keepdims=True)
            change = gmid_ref[here] + norm_back(grad_normed * g1, scaled, inverse)
            high = change.astype(BF16)
            rest = (change - high.astype(F32)).astype(BF16)
            gi_ref[i] = t_dot(sel, high) + t_dot(sel, rest)
        at_row, at_col = vec_slot(6, width)
        vsum_ref[0, at_row, at_col] = gain
        at_row, at_col = vec_slot(7, width)
        vsum_ref[0, at_row, at_col] = shift
        vec_begin(0)
        for at, (name, c) in enumerate(tail):
            do(name, c)
            if at % 3 == 2 and at // 3 < 4:
                vec_next(at // 3)
        value = None
        for z in range(deep):
            mine = vsum_ref[3]
            from_k = [vz_ref[k] for k in range(deep - 1)]
            term = mine
            for k in range(deep - 1):
                term = jnp.where((place.z - k - 1 + deep) % deep == z, from_k[k], term)
            value = term if value is None else value + term
        vec_ref[...] = value
        for c in range(late):
            mlp.arrive(c, 2)
            mlp.sent(c)
        for c in range(groups + 1):
            back.arrive(c, 3)
            back.sent(c)
            reduce.sent(c)
        for stage in range(4):
            for copy in vec_copies(stage):
                copy.wait_send()


def finish_kernel(
    groups, early,
    first_ref, second_ref, attn_ref, low_ref, put_ref, img_ref, cot_ref, keep_ref, vec_ref,
    lo_ref, gi_ref, wq_ref, wp_ref, w1_ref, w2_ref, b1_ref, root_ref, *small_refs,
):
    step = pl.program_id(0)
    width = low_ref.shape[2]
    chunk = w1_ref.shape[1]
    for big_ref, mine in ((first_ref, step < early), (second_ref, step >= early)):

        @pl.when(mine)
        def _(big_ref=big_ref):
            for j in range(chunk // 128):
                w1_ref[:, j * 128 : j * 128 + 128] = big_ref[j].astype(F32)
            for j in range(width // 128):
                at = j % 3 * chunk
                w2_ref[:, j * 128 : j * 128 + 128] = big_ref[2 + j // 3, at : at + chunk].astype(F32)

    for owner in range(2):
        for j in range(3):
            at = (2 * j + owner) * 128
            wp_ref[:, at : at + 128] = attn_ref[owner, j].astype(F32)
            for group in range(groups):
                at = j * width + (2 * group + owner) * 128
                wq_ref[:, at : at + 128] = attn_ref[owner, 3 + 3 * group + j].astype(F32)

    @pl.when(step < keep_ref.shape[0])
    def _():
        keep = keep_ref[pl.ds(step, 1)].astype(F32)
        eight = jnp.broadcast_to(keep, (8, keep.shape[1])).astype(BF16)
        once = jnp.where(lax.broadcasted_iota(jnp.int32, (8, 128), 0) == 0, 1.0, 0.0).astype(BF16)
        kept = t_dot(eight, once)[:, 0:1] > 0.5
        lo_ref[0] = jnp.where(kept, low_ref[0], img_ref[0])
        gi_ref[0] = jnp.where(kept, put_ref[0], cot_ref[0].astype(F32))

    @pl.when(step == 0)
    def _():
        def line(slot):
            at_row, at_col = vec_slot(slot, width)
            return vec_ref[at_row, at_col]

        for slot, ref in enumerate(small_refs):
            ref[...] = line(slot).reshape(width)
        b1_ref[...] = vec_ref[pl.ds(6 + lax.axis_index("mlp"), 1)].reshape(2 * width)
        count = line(11)[:, 0:1]
        lane = lax.broadcasted_iota(jnp.int32, (1, 128), 1)
        sums = jnp.where(lane == 0, jnp.sum(line(8)), jnp.where(lane == 1, jnp.sum(line(10)), jnp.sum(line(9))))
        root_ref[...] = jnp.sqrt(sums / (count * width)).reshape(128)[:3]


def staged_device(
    deep, images, keep_mask, ln1_gain, ln1_bias, w_qkv, bias_q, bias_v, w_proj, b_proj,
    ln2_gain, ln2_bias, w_fc1, b_fc1, w_fc2, b_fc2, cotangent,
):
    count, patches, width = images.shape
    slots = slots_of(patches)
    rows = count * slots
    heads = width // HEAD_DIM
    shard = w_fc1.shape[1]
    row = lambda v: v.reshape(1, -1)
    shape = jax.ShapeDtypeStruct
    limit = 62 * 2**20
    any_space = pl.BlockSpec(memory_space=pl.ANY)
    per_image = lambda *tail: pl.BlockSpec((1,) + tail, lambda i: (i,) + (0,) * len(tail))
    per_rows = lambda cols: pl.BlockSpec((slots, cols), lambda i: (i, 0))
    dma = pltpu.SemaphoreType.DMA
    sel, x, normed, qkv, probs, att, mid, hid, gm, sums, far_w1, far_b1, far_w2 = pl.pallas_call(
        functools.partial(forward_kernel, slots, True),
        grid=(count,),
        out_shape=(
            shape((count, slots, patches), BF16),
            shape((rows, width), BF16),
            shape((rows, width), BF16),
            shape((rows, 3 * width), BF16),
            shape((count, heads, slots, slots), BF16),
            shape((rows, width), BF16),
            shape((rows, width), F32),
            shape((rows, width), BF16),
            shape((rows, width), BF16),
            shape((count, 8, width), F32),
            shape((width, shard), BF16), shape((shard,), BF16), shape((shard, width), BF16),
        ),
        in_specs=[
            whole((count, patches)), per_image(patches, width), per_image(patches, width),
            whole((width,)), whole((width,)), whole((width, 3 * width)), whole((width,)), whole((width,)),
            whole((width, width)), whole((width,)), whole((width,)), whole((width,)),
            any_space, any_space, any_space,
        ],
        out_specs=(
            per_image(slots, patches), per_rows(width), per_rows(width), per_rows(3 * width),
            per_image(heads, slots, slots), per_rows(width), per_rows(width), per_rows(width), per_rows(width),
            per_image(8, width), any_space, any_space, any_space,
        ),
        scratch_shapes=[dma((3,)), dma((3,))],
        compiler_params=pltpu.CompilerParams(vmem_limit_bytes=limit, collective_id=0, has_side_effects=True),
        name="attention_forward",
    )(
        keep_mask, images, cotangent, ln1_gain, ln1_bias, w_qkv, bias_q, bias_v, w_proj, b_proj, ln2_gain, ln2_bias,
        w_fc1, b_fc1, w_fc2,
    )
    chunk = 256
    ticks = shard // chunk
    groups = 3
    piece = width // 4 // deep
    by_cols = lambda *lead: pl.BlockSpec(lead + (chunk,), lambda c: (0, c - c // ticks))
    by_rows = pl.BlockSpec((chunk, width), lambda c: (c - c // ticks, 0))
    early = ticks // 2
    red, gmid, gatt, dwp, low, vec, first = pl.pallas_call(
        functools.partial(mlp_staged_kernel, deep, count, slots, ticks),
        grid=(ticks + 1,),
        out_shape=(
            shape((4 * ticks, piece, 128), BF16), shape((rows, width), F32), shape((rows, width), BF16),
            shape((2, 3, width, 128), BF16), shape((count, patches, width), BF16), shape((8, 2 * width), F32),
            shape((4 * early, width, 128), BF16),
        ),
        in_specs=[
            whole((rows, width)), whole((rows, width)), whole((rows, width)), whole((rows, width)),
            whole((count, slots, patches)), whole((count, 8, width)),
            by_cols(width), by_cols(width), whole((shard,)), whole((shard,)), by_rows, by_rows,
            whole((width, width)), whole((width,)), whole((width,)),
        ],
        out_specs=(
            whole((4 * ticks, piece, 128)), whole((rows, width)), whole((rows, width)),
            whole((2, 3, width, 128)), whole((count, patches, width)), whole((8, 2 * width)), any_space,
        ),
        scratch_shapes=[
            pltpu.VMEM((rows, width), F32), pltpu.VMEM((rows, width), F32), pltpu.VMEM((2, 8, chunk), F32),
            pltpu.VMEM((ticks, 4, width, 128), BF16), pltpu.VMEM((ticks, 4, width, 128), BF16),
            pltpu.VMEM((ticks, 4, width, 128), BF16), pltpu.VMEM((ticks, 4, width // 2, 128), BF16),
            pltpu.VMEM((ticks, 4, width // 4, 128), BF16), pltpu.VMEM((ticks, deep - 1, 4, piece, 128), BF16),
            dma((ticks, 3)), dma((ticks, 3)), dma((ticks, deep - 1)), dma((ticks, deep - 1)),
            dma((early,)), dma((early, 2)), dma((early, 2)), dma((early, deep - 1)), dma((early, deep - 1)),
        ],
        compiler_params=pltpu.CompilerParams(vmem_limit_bytes=limit, collective_id=1, has_side_effects=True),
        name="mlp_both_ways",
    )(
        hid, gm, att, mid, sel, sums, w_fc1, far_w1, b_fc1, far_b1, w_fc2, far_w2, w_proj, ln2_gain, b_fc2,
    )
    wide = width // groups
    chunks = groups + 1
    now = lambda g: g - g // groups
    third = lambda lead, part: pl.BlockSpec((lead, wide), lambda g: (0, part * groups + now(g)))
    late = ticks - early
    second, attn, put, vec = pl.pallas_call(
        functools.partial(attention_staged_kernel, deep, count, slots, groups, ticks),
        grid=(groups + 1,),
        out_shape=(
            shape((4 * late, width, 128), BF16), shape((2, 3 * chunks, width, 128), BF16),
            shape((count, patches, width), F32), shape((8, 2 * width), F32),
        ),
        in_specs=[
            third(rows, 0), third(rows, 1), third(rows, 2),
            pl.BlockSpec((count, heads // groups, slots, slots), lambda g: (0, now(g), 0, 0)),
            third(rows, 0), third(width, 0), third(width, 1), third(width, 2),
            whole((rows, width)), whole((rows, width)), whole((rows, width)), whole((count, slots, patches)),
            whole((width,)), whole((2, 3, width, 128)), whole((4 * ticks, piece, 128)), whole((8, 2 * width)),
        ],
        out_specs=(any_space, any_space, whole((count, patches, width)), whole((8, 2 * width))),
        scratch_shapes=[
            pltpu.VMEM((rows, wide), BF16), pltpu.VMEM((rows, wide), BF16), pltpu.VMEM((rows, wide), BF16),
            pltpu.VMEM((rows, width), F32),
            pltpu.VMEM((groups, 2, 3, width, 128), BF16), pltpu.VMEM((chunks, 3, width, 128), BF16),
            pltpu.VMEM((chunks, 3, piece, 128), BF16), pltpu.VMEM((chunks, 3, width, 128), BF16),
            pltpu.VMEM((chunks, 3, width // 2, 128), BF16), pltpu.VMEM((chunks, 3, width // 4, 128), BF16),
            pltpu.VMEM((chunks, deep - 1, 3, piece, 128), BF16),
            pltpu.VMEM((4, 8, 2 * width), F32), pltpu.VMEM((3, 8, 2 * width), F32),
            pltpu.VMEM((deep - 1, 8, 2 * width), F32),
            dma((chunks, 3)), dma((chunks, 3)), dma((chunks, deep - 1)), dma((chunks, deep - 1)),
            dma((late,)), dma((late, 2)), dma((late, 2)), dma((late, deep - 1)), dma((late, deep - 1)),
            dma((chunks,)), dma((chunks, 3)), dma((chunks, 3)), dma((chunks, deep - 1)), dma((chunks, deep - 1)),
            dma((3,)), dma((3,)), dma((deep - 1,)), dma((deep - 1,)),
        ],
        compiler_params=pltpu.CompilerParams(vmem_limit_bytes=limit, collective_id=2, has_side_effects=True),
        name="attention_backward",
    )(
        qkv, qkv, qkv, probs, gatt, w_qkv, w_qkv, w_qkv, normed, x, gmid, sel, ln1_gain, dwp, red, vec,
    )
    deal = width // ticks
    turn = lambda t: (t - t // count, 0, 0)
    layer_out, grad_images, s_wq, s_wp, s_w1, s_w2, s_b1, root_means, *small = pl.pallas_call(
        functools.partial(finish_kernel, groups, early),
        grid=(ticks,),
        out_shape=(
            shape((count, patches, width), BF16), shape((count, patches, width), F32),
            shape((width, 3 * width), F32), shape((width, width), F32), shape((width, shard), F32),
            shape((shard, width), F32), shape((shard,), F32), shape((3,), F32),
        ) + 8 * (shape((width,), F32),),
        in_specs=[
            pl.BlockSpec((4, width, 128), lambda t: (jnp.minimum(t, early - 1), 0, 0)),
            pl.BlockSpec((4, width, 128), lambda t: (jnp.maximum(t - early, 0), 0, 0)),
            pl.BlockSpec((2, 3 * chunks, deal, 128), lambda t: (0, 0, t, 0)),
            pl.BlockSpec((1, patches, width), turn), pl.BlockSpec((1, patches, width), turn),
            pl.BlockSpec((1, patches, width), turn), pl.BlockSpec((1, patches, width), turn),
            whole((count, patches)), whole((8, 2 * width)),
        ],
        out_specs=(
            pl.BlockSpec((1, patches, width), turn), pl.BlockSpec((1, patches, width), turn),
            pl.BlockSpec((deal, 3 * width), lambda t: (t, 0)), pl.BlockSpec((deal, width), lambda t: (t, 0)),
            pl.BlockSpec((width, chunk), lambda t: (0, t)), pl.BlockSpec((chunk, width), lambda t: (t, 0)),
            whole((shard,)), whole((3,)),
        ) + 8 * (whole((width,)),),
        compiler_params=pltpu.CompilerParams(vmem_limit_bytes=limit),
        name="results",
    )(first, second, attn, low, put, images, cotangent, keep_mask, vec)
    gain2, shift2, b_two, b_project, b_query, b_value, gain1, shift1 = small
    return (
        layer_out, grad_images, gain1, shift1, s_wq, b_query, b_value, s_wp, b_project, gain2, shift2,
        s_w1, s_b1, s_w2, b_two, root_means,
    )


def solution(mesh):
    rows, line = P(("img", "mlp"), None, None), P(("img", "mlp"), None)
    deep = mesh.shape["img"] // 4
    staged = mesh.shape["img"] == 4 * deep and mesh.shape["mlp"] == 2 and 1 < deep <= 4
    return jax.shard_map(
        functools.partial(staged_device, deep) if staged else plain_device,
        mesh=mesh,
        in_specs=(
            rows, line, P(), P(), P(), P(), P(), P(), P(), P(), P(),
            P(None, "mlp"), P("mlp"), P("mlp", None), P(), rows,
        ),
        out_specs=(
            rows, rows, P(), P(), P(), P(), P(), P(), P(), P(), P(),
            P(None, "mlp"), P("mlp"), P("mlp", None), P(), P(),
        ),
        check_vma=False,
    )
```

```python
import functools

import jax
import jax.numpy as jnp
from jax import lax
from jax.experimental import pallas as pl
from jax.experimental.pallas import tpu as pltpu
from jax.sharding import PartitionSpec as P

HEAD_DIM = 64
NORM_EPS = 1e-06
F32 = jnp.float32
BF16 = jnp.bfloat16
MESH = pl.DeviceIdType.MESH
ERFC_POLY = (
    -0.05792342897865154,
    0.27982426175045266,
    -0.47905523971588865,
    0.27061712140601424,
    -0.022718349995155727,
    0.2015184791612061,
    0.24328701077158832,
    0.2823637910445855,
    0.2820864086305586,
)


def dot(a, b):
    return jnp.dot(a, b, preferred_element_type=F32)


def dot_t(a, b):
    return lax.dot_general(a, b, (((1,), (1,)), ((), ())), preferred_element_type=F32)


def t_dot(a, b):
    return lax.dot_general(a, b, (((0,), (0,)), ((), ())), preferred_element_type=F32)


def slots_of(patches):
    most = 4 * patches // 5
    return -(-most // 16) * 16


def norm_rows(rows):
    center = rows - jnp.mean(rows, axis=1, keepdims=True)
    inverse = lax.rsqrt(jnp.mean(center * center, axis=1, keepdims=True) + NORM_EPS)
    return center * inverse, inverse


def norm_back(weighted, scaled, inverse):
    return inverse * (
        weighted
        - jnp.mean(weighted, axis=1, keepdims=True)
        - scaled * jnp.mean(weighted * scaled, axis=1, keepdims=True)
    )


def gelu_pair(values):
    reach = jnp.abs(values) * 0.7071067811865476
    inv = 1.0 / (1.0 + 0.5 * reach)
    decay = jnp.exp(-0.5 * (values * values))
    poly = jnp.full_like(values, ERFC_POLY[0])
    for coefficient in ERFC_POLY[1:]:
        poly = poly * inv + coefficient
    tail = (0.5 * inv) * poly * decay
    share = jnp.where(values > 0, 1.0 - tail, tail)
    return values * share, share + values * (decay * 0.3989422804014327)


def swap_weights(ours, theirs, send_sem, recv_sem):
    other = {"mlp": 1 - lax.axis_index("mlp")}
    copies = [
        pltpu.make_async_remote_copy(
            src_ref=ours[j], dst_ref=theirs[j], send_sem=send_sem.at[j], recv_sem=recv_sem.at[j],
            device_id=other, device_id_type=MESH,
        )
        for j in range(len(ours))
    ]

    def trade(begin):
        @pl.when(pl.program_id(0) == (0 if begin else pl.num_programs(0) - 1))
        def _():
            if begin:
                barrier = pltpu.get_barrier_semaphore()
                pl.semaphore_signal(barrier, inc=1, device_id=other, device_id_type=MESH)
                pl.semaphore_wait(barrier, 1)
            for copy in copies:
                if begin:
                    copy.start()
                else:
                    copy.wait()

    return trade


def as_row(ref):
    return ref[...].astype(F32).reshape(1, -1)


def forward_kernel(
    slots, exchange,
    keep_ref, img_ref, cot_ref, g1_ref, b1_ref, wqkv_ref, bq_ref, bv_ref, wproj_ref, bproj_ref, g2_ref, b2_ref,
    *refs,
):
    if exchange:
        ours, refs, (send_sem, recv_sem) = refs[:3], refs[3:-2], refs[-2:]
        theirs, refs = refs[-3:], refs[:-3]
        trade = swap_weights(ours, theirs, send_sem, recv_sem)
        trade(True)
    sel_ref, x_ref, normed_ref, qkv_ref, probs_ref, att_ref, mid_ref, hid_ref, gm_ref, sums_ref = refs
    patches, width = img_ref.shape[1:]
    heads = width // HEAD_DIM
    keep = keep_ref[pl.ds(pl.program_id(0), 1)].astype(F32)
    upto = lax.broadcasted_iota(jnp.int32, (patches, patches), 0) <= lax.broadcasted_iota(
        jnp.int32, (patches, patches), 1
    )
    keep8 = jnp.broadcast_to(keep, (8, patches)).astype(BF16)
    rank = dot(keep8, upto.astype(F32).astype(BF16))[0:1]
    count = jnp.sum(keep, axis=1, keepdims=True)
    slot = lax.broadcasted_iota(jnp.int32, (slots, patches), 0).astype(F32)
    sel = jnp.where((slot == rank - 1.0) & (keep > 0), 1.0, 0.0).astype(BF16)
    sel_ref[0] = sel
    gm_ref[...] = dot(sel, cot_ref[0]).astype(BF16)
    rows = dot(sel, img_ref[0])
    x_ref[...] = rows.astype(BF16)
    scaled, _ = norm_rows(rows)
    normed = (scaled * as_row(g1_ref) + as_row(b1_ref)).astype(BF16)
    normed_ref[...] = normed
    for part in range(3):
        cols = slice(part * width, (part + 1) * width)
        block = dot(normed, wqkv_ref[:, cols])
        if part == 0:
            block = block + as_row(bq_ref)
        if part == 2:
            block = block + as_row(bv_ref)
        qkv_ref[:, cols] = block.astype(BF16)
    closed = jnp.where(
        lax.broadcasted_iota(jnp.int32, (1, slots), 1).astype(F32) < count, 0.0, -1e30
    )
    first = lax.broadcasted_iota(jnp.int32, (1, 2 * HEAD_DIM), 1) < HEAD_DIM
    zero = jnp.zeros((), BF16)
    for pair in range(heads // 2):
        lanes = slice(pair * 128, pair * 128 + 128)
        query = qkv_ref[:, lanes] * jnp.asarray(HEAD_DIM ** -0.5, BF16)
        key = qkv_ref[:, width + pair * 128 : width + pair * 128 + 128]
        value = qkv_ref[:, 2 * width + pair * 128 : 2 * width + pair * 128 + 128]
        total = None
        for half in range(2):
            mine = first if half == 0 else jnp.logical_not(first)
            scores = dot_t(query, jnp.where(mine, key, zero)) + closed
            raised = jnp.exp(scores - jnp.max(scores, axis=1, keepdims=True))
            probs = (raised * (1.0 / jnp.sum(raised, axis=1, keepdims=True))).astype(BF16)
            probs_ref[0, 2 * pair + half] = probs
            term = dot(probs, jnp.where(mine, value, zero))
            total = term if total is None else total + term
        att_ref[:, lanes] = total.astype(BF16)
    attn_out = dot(att_ref[...], wproj_ref[...]) + as_row(bproj_ref)
    valid = lax.broadcasted_iota(jnp.int32, (slots, 1), 0).astype(F32) < count
    attn_kept = jnp.where(valid, attn_out, 0.0)
    middle = rows + attn_kept
    mid_ref[...] = middle
    sums_ref[0, 0:1] = jnp.sum(attn_kept * attn_kept, axis=0, keepdims=True)
    sums_ref[0, 1:2] = jnp.broadcast_to(count, (1, width))
    scaled, _ = norm_rows(middle)
    hid_ref[...] = (scaled * as_row(g2_ref) + as_row(b2_ref)).astype(BF16)
    if exchange:
        trade(False)


def mlp_kernel(hid_ref, gm_ref, w1_ref, b1_ref, w2_ref, out_ref, gh_ref, dw1_ref, dw2_ref, db1_ref):
    step = pl.program_id(0)
    hid, gm = hid_ref[...], gm_ref[...]
    w1, w2 = w1_ref[0], w2_ref[0]
    pre = dot(hid, w1) + b1_ref[0].astype(F32)
    act, slope = gelu_pair(pre)
    act = act.astype(BF16)
    grad_act = dot_t(gm, w2).astype(BF16).astype(F32)
    grad_pre_f = grad_act * slope
    grad_pre = grad_pre_f.astype(BF16)
    dw2_ref[0] = t_dot(act, gm).astype(BF16)
    dw1_ref[0] = t_dot(hid, grad_pre).astype(BF16)
    db1_ref[0] = jnp.sum(grad_pre.astype(F32), axis=0, keepdims=True)

    @pl.when(step == 0)
    def _():
        out_ref[...] = dot(act, w2)
        gh_ref[...] = dot_t(grad_pre, w1)

    @pl.when(step > 0)
    def _():
        out_ref[...] += dot(act, w2)
        gh_ref[...] += dot_t(grad_pre, w1)


def backward_kernel(
    images, slots, groups,
    sel_ref, x_ref, normed_ref, qkv_ref, probs_ref, att_ref, mid_ref, gm_ref, gh_ref, mlp_ref, valid_ref,
    g1_ref, g2_ref, bfc2_ref, wqkv_ref, wproj_ref, img_ref, cot_ref,
    lo_ref, gi_ref, dwp_ref, dwq_ref, vec_ref,
    gmid_ref, gatt_ref, gq_ref, gk_ref, gv_ref, gn_ref,
):
    step = pl.program_id(0)
    rows, width = x_ref.shape

    @pl.when(step == 0)
    def _():
        middle = mid_ref[...]
        valid = valid_ref[...] > 0
        mlp_out = jnp.where(valid, mlp_ref[...] + bfc2_ref[...].astype(F32), 0.0)
        block = middle + mlp_out
        kept = jnp.where(valid, block, 0.0)
        vec_ref[8:9] = jnp.sum(kept * kept, axis=0, keepdims=True)
        vec_ref[9:10] = jnp.sum(mlp_out * mlp_out, axis=0, keepdims=True)
        low = block.astype(BF16)
        for i in range(images):
            put = t_dot(sel_ref[i], low[i * slots : (i + 1) * slots])
            here = jnp.sum(sel_ref[i].astype(F32), axis=0, keepdims=True)
            lo_ref[i] = put.astype(BF16)
        scaled, inverse = norm_rows(middle)
        grad_hidden = gh_ref[...]
        vec_ref[0:1] = jnp.sum(grad_hidden * scaled, axis=0, keepdims=True)
        vec_ref[1:2] = jnp.sum(grad_hidden, axis=0, keepdims=True)
        gm = gm_ref[...].astype(F32)
        vec_ref[2:3] = jnp.sum(gm, axis=0, keepdims=True)
        grad_middle = gm + norm_back(grad_hidden * g2_ref[...], scaled, inverse)
        gmid_ref[...] = grad_middle
        grad_attn = grad_middle.astype(BF16)
        vec_ref[3:4] = jnp.sum(grad_attn.astype(F32), axis=0, keepdims=True)
        dwp_ref[...] = t_dot(att_ref[...], grad_attn).astype(BF16)
        gatt_ref[...] = dot_t(grad_attn, wproj_ref[...]).astype(BF16)
        gn_ref[...] = jnp.zeros_like(gn_ref)

    first = lax.broadcasted_iota(jnp.int32, (1, 2 * HEAD_DIM), 1) < HEAD_DIM
    zero = jnp.zeros((), BF16)
    scale = jnp.asarray(HEAD_DIM ** -0.5, BF16)
    pairs = width // 128 // groups
    for group in range(groups):

        @pl.when(step == group + 1)
        def _():
            base = group * pairs * 128

            @pl.loop(0, images)
            def _(i):
                here = pl.ds(pl.multiple_of(i * slots, 16), slots)
                for pair in range(pairs):
                    at = base + pair * 128
                    own = slice(pair * 128, pair * 128 + 128)
                    query = qkv_ref[here, at : at + 128]
                    key = qkv_ref[here, width + at : width + at + 128]
                    value = qkv_ref[here, 2 * width + at : 2 * width + at + 128]
                    grad_att = gatt_ref[here, at : at + 128]
                    gq = gk = gv = None
                    for half in range(2):
                        mine = first if half == 0 else jnp.logical_not(first)
                        low = probs_ref[i, 2 * (base // 128 + pair) + half]
                        probs = low.astype(F32)
                        g_mine = jnp.where(mine, grad_att, zero)
                        grad_probs = dot_t(g_mine, value).astype(BF16).astype(F32)
                        inner = jnp.sum(probs * grad_probs, axis=1, keepdims=True)
                        grad_scores = (probs * (grad_probs - inner)).astype(BF16) * scale
                        tv = t_dot(low, g_mine)
                        tq = dot(grad_scores, jnp.where(mine, key, zero))
                        tk = t_dot(grad_scores, jnp.where(mine, query, zero))
                        gq = tq if gq is None else gq + tq
                        gk = tk if gk is None else gk + tk
                        gv = tv if gv is None else gv + tv
                    gq_ref[here, own] = gq.astype(BF16)
                    gk_ref[here, own] = gk.astype(BF16)
                    gv_ref[here, own] = gv.astype(BF16)

            span = pairs * 128
            vec_ref[4:5, base : base + span] = jnp.sum(gq_ref[...].astype(F32), axis=0, keepdims=True)
            vec_ref[5:6, base : base + span] = jnp.sum(gv_ref[...].astype(F32), axis=0, keepdims=True)
            for part, ref in enumerate((gq_ref, gk_ref, gv_ref)):
                cols = slice(part * width + base, part * width + base + span)
                dwq_ref[:, cols] = t_dot(normed_ref[...], ref[...]).astype(BF16)
                gn_ref[...] += dot_t(ref[...], wqkv_ref[:, cols])

    @pl.when(step == groups + 1)
    def _():
        scaled, inverse = norm_rows(x_ref[...].astype(F32))
        grad_normed = gn_ref[...]
        vec_ref[6:7] = jnp.sum(grad_normed * scaled, axis=0, keepdims=True)
        vec_ref[7:8] = jnp.sum(grad_normed, axis=0, keepdims=True)
        change = gmid_ref[...] + norm_back(grad_normed * g1_ref[...], scaled, inverse)
        high = change.astype(BF16)
        rest = (change - high.astype(F32)).astype(BF16)
        for i in range(images):
            here = slice(i * slots, (i + 1) * slots)
            gi_ref[i] = t_dot(sel_ref[i], high[here]) + t_dot(sel_ref[i], rest[here])


def whole(shape):
    return pl.BlockSpec(shape, lambda *_: (0,) * len(shape), pipeline_mode=pl.Buffered(1))


def plain_device(
    images, keep_mask, ln1_gain, ln1_bias, w_qkv, bias_q, bias_v, w_proj, b_proj,
    ln2_gain, ln2_bias, w_fc1, b_fc1, w_fc2, b_fc2, cotangent,
):
    count, patches, width = images.shape
    slots = slots_of(patches)
    rows = count * slots
    heads = width // HEAD_DIM
    shard = w_fc1.shape[1]
    row = lambda v: v.reshape(1, -1)
    whole_w1 = lax.all_gather(w_fc1, "mlp")
    whole_w2 = lax.all_gather(w_fc2, "mlp")
    whole_b1 = lax.all_gather(b_fc1, "mlp").reshape(2, 1, shard)
    shape = jax.ShapeDtypeStruct
    limit = pltpu.CompilerParams(vmem_limit_bytes=60 * 2**20)
    per_image = lambda *tail: pl.BlockSpec((1,) + tail, lambda i: (i,) + (0,) * len(tail))
    per_rows = lambda cols: pl.BlockSpec((slots, cols), lambda i: (i, 0))
    sel, x, normed, qkv, probs, att, mid, hid, gm, sums = pl.pallas_call(
        functools.partial(forward_kernel, slots, False),
        grid=(count,),
        out_shape=(
            shape((count, slots, patches), BF16),
            shape((rows, width), BF16),
            shape((rows, width), BF16),
            shape((rows, 3 * width), BF16),
            shape((count, heads, slots, slots), BF16),
            shape((rows, width), BF16),
            shape((rows, width), F32),
            shape((rows, width), BF16),
            shape((rows, width), BF16),
            shape((count, 8, width), F32),
        ),
        in_specs=[
            whole((count, patches)), per_image(patches, width), per_image(patches, width),
            whole((width,)), whole((width,)), whole((width, 3 * width)), whole((width,)), whole((width,)),
            whole((width, width)), whole((width,)), whole((width,)), whole((width,)),
        ],
        out_specs=(
            per_image(slots, patches), per_rows(width), per_rows(width), per_rows(3 * width),
            per_image(heads, slots, slots), per_rows(width), per_rows(width), per_rows(width), per_rows(width),
            per_image(8, width),
        ),
        compiler_params=limit,
        name="attention_forward",
    )(
        keep_mask, images, cotangent, ln1_gain, ln1_bias, w_qkv, bias_q, bias_v, w_proj, b_proj, ln2_gain, ln2_bias,
    )
    chunk = 512 if shard % 512 == 0 else 256
    each = shard // chunk
    mlp_out, grad_hidden, dw1, dw2, db1 = pl.pallas_call(
        mlp_kernel,
        grid=(2 * each,),
        out_shape=(
            shape((rows, width), F32), shape((rows, width), F32),
            shape((2, width, shard), BF16), shape((2, shard, width), BF16), shape((2, 1, shard), F32),
        ),
        in_specs=[
            whole((rows, width)), whole((rows, width)),
            pl.BlockSpec((1, width, chunk), lambda c: (c // each, 0, c % each)),
            pl.BlockSpec((1, 1, chunk), lambda c: (c // each, 0, c % each)),
            pl.BlockSpec((1, chunk, width), lambda c: (c // each, c % each, 0)),
        ],
        out_specs=(
            whole((rows, width)), whole((rows, width)),
            pl.BlockSpec((1, width, chunk), lambda c: (c // each, 0, c % each)),
            pl.BlockSpec((1, chunk, width), lambda c: (c // each, c % each, 0)),
            pl.BlockSpec((1, 1, chunk), lambda c: (c // each, 0, c % each)),
        ),
        compiler_params=limit,
        name="mlp_both_ways",
    )(hid, gm, whole_w1, whole_b1, whole_w2)
    kept = jnp.sum(keep_mask, axis=1, keepdims=True)
    valid = (jnp.arange(slots, dtype=jnp.int32)[None, :] < kept).astype(F32).reshape(rows, 1)
    groups = 3
    span = width // groups
    low, put, dwp, dwq, vec = pl.pallas_call(
        functools.partial(backward_kernel, count, slots, groups),
        grid=(groups + 2,),
        out_shape=(
            shape((count, patches, width), BF16), shape((count, patches, width), F32),
            shape((width, width), BF16), shape((width, 3 * width), BF16), shape((16, width), F32),
        ),
        in_specs=[
            whole((count, slots, patches)), whole((rows, width)), whole((rows, width)), whole((rows, 3 * width)),
            whole((count, heads, slots, slots)), whole((rows, width)), whole((rows, width)), whole((rows, width)),
            whole((rows, width)), whole((rows, width)), whole((rows, 1)),
            whole((1, width)), whole((1, width)), whole((1, width)), whole((width, 3 * width)), whole((width, width)),
            pl.BlockSpec(memory_space=pl.ANY), pl.BlockSpec(memory_space=pl.ANY),
        ],
        out_specs=(
            whole((count, patches, width)), whole((count, patches, width)),
            whole((width, width)), whole((width, 3 * width)), whole((16, width)),
        ),
        scratch_shapes=[
            pltpu.VMEM((rows, width), F32), pltpu.VMEM((rows, width), BF16),
            pltpu.VMEM((rows, span), BF16), pltpu.VMEM((rows, span), BF16), pltpu.VMEM((rows, span), BF16),
            pltpu.VMEM((rows, width), F32),
        ],
        compiler_params=limit,
        name="attention_backward",
    )(
        sel, x, normed, qkv, probs, att, mid, gm, grad_hidden, mlp_out, valid,
        row(ln1_gain), row(ln2_gain), row(b_fc2), w_qkv, w_proj, images, cotangent,
    )
    kept_at = (keep_mask > 0)[:, :, None]
    layer_out = jnp.where(kept_at, low, images)
    grad_images = jnp.where(kept_at, put, cotangent.astype(F32))
    both = ("img", "mlp")
    place = lax.axis_index("mlp")
    dw1s = lax.psum_scatter(dw1.reshape(2 * width, shard), "mlp", scatter_dimension=0, tiled=True)
    dw2s = lax.psum_scatter(dw2.reshape(2 * shard, width), "mlp", scatter_dimension=0, tiled=True)
    s_w1, s_w2 = lax.psum((dw1s, dw2s), "img")
    s_wq, s_wp = lax.psum((dwq, dwp), both)
    vec, sums, s_b1 = lax.psum((vec, jnp.sum(sums, axis=0), db1.reshape(2, shard)), both)
    s_b1 = lax.dynamic_index_in_dim(s_b1, place, 0, keepdims=False)
    stream_sq, mlp_sq, attn_sq = jnp.sum(vec[8]), jnp.sum(vec[9]), jnp.sum(sums[0])
    root_means = jnp.sqrt(jnp.stack([stream_sq, attn_sq, mlp_sq]) / (sums[1, 0] * width))
    f = lambda v: v.astype(F32)
    return (
        layer_out, grad_images, vec[6], vec[7], f(s_wq), vec[4], vec[5], f(s_wp), vec[3], vec[0], vec[1],
        f(s_w1), s_b1, f(s_w2), vec[2], root_means,
    )


class Place:
    def __init__(self, deep, width):
        spot, self.core = lax.axis_index("img"), lax.axis_index("mlp")
        x, y, self.z = spot % 2, (spot // 2) % 2, spot // 4
        core = self.core
        self.bit1 = x * (1 - core) + y * core
        self.bit2 = y * (1 - core) + x * core
        step_x, step_y = 1 - 2 * x, 2 - 4 * y
        self.deep = deep
        self.other = {"mlp": 1 - core}
        self.peer1 = {"img": spot + step_x * (1 - core) + step_y * core}
        self.peer2 = {"img": spot + step_y * (1 - core) + step_x * core}
        self.peer_z = [{"img": ((self.z + k) % deep) * 4 + spot % 4} for k in range(1, deep)]
        self.half, self.quarter = width // 2, width // 4
        self.piece = width // 4 // deep
        self.half_at = self.bit1 * self.half
        self.half_off = (1 - self.bit1) * self.half
        self.quarter_at = self.half_at + self.bit2 * self.quarter
        self.quarter_off = self.half_at + (1 - self.bit2) * self.quarter

    def piece_at(self, z):
        return self.quarter_at + z * self.piece

    def everyone(self):
        return [self.other, self.peer1, self.peer2] + self.peer_z

    def greet(self):
        for peer in self.everyone():
            pl.semaphore_signal(pltpu.get_barrier_semaphore(), inc=1, device_id=peer, device_id_type=MESH)

    def all_here(self):
        pl.semaphore_wait(pltpu.get_barrier_semaphore(), len(self.everyone()))


def span(start, size):
    return pl.ds(pl.multiple_of(start, 16), size)


def remote(source, target, send_sem, recv_sem, peer):
    return pltpu.make_async_remote_copy(
        src_ref=source, dst_ref=target, send_sem=send_sem, recv_sem=recv_sem, device_id=peer, device_id_type=MESH
    )


def added(left, right):
    return (left.astype(F32) + right.astype(F32)).astype(BF16)


class Reduce:
    def __init__(self, place, partial, sending, total, got_core, got1, got2, got_z, send, recv, send_z, recv_z):
        self.place, self.partial, self.sending, self.total = place, partial, sending, total
        self.got_core, self.got1, self.got2, self.got_z = got_core, got1, got2, got_z
        self.send, self.recv, self.send_z, self.recv_z = send, recv, send_z, recv_z

    def copies(self, c, stage):
        p = self.place
        if stage == 0:
            return [remote(self.sending(c), self.got_core.at[c], self.send.at[c, 0], self.recv.at[c, 0], p.other)]
        total = self.total(c)
        if stage == 1:
            part = total.at[:, span(p.half_off, p.half), :]
            return [remote(part, self.got1.at[c], self.send.at[c, 1], self.recv.at[c, 1], p.peer1)]
        if stage == 2:
            part = total.at[:, span(p.quarter_off, p.quarter), :]
            return [remote(part, self.got2.at[c], self.send.at[c, 2], self.recv.at[c, 2], p.peer2)]
        made = []
        for k, peer in enumerate(p.peer_z):
            part = total.at[:, span(p.piece_at((p.z + k + 1) % p.deep), p.piece), :]
            made.append(remote(part, self.got_z.at[c, k], self.send_z.at[c, k], self.recv_z.at[c, k], peer))
        return made

    def begin(self, c, stage):
        for copy in self.copies(c, stage):
            copy.start()

    def arrive(self, c, stage):
        for copy in self.copies(c, stage):
            copy.wait_recv()

    def sent(self, c):
        for stage in range(4):
            for copy in self.copies(c, stage):
                copy.wait_send()

    def plane1(self, c):
        self.arrive(c, 0)
        total, partial, got = self.total(c), self.partial(c), self.got_core.at[c]
        total[...] = added(partial[...], got[...])
        self.begin(c, 1)

    def plane2(self, c):
        p = self.place
        self.arrive(c, 1)
        rows = span(p.half_at, p.half)
        total = self.total(c)
        total[:, rows, :] = added(total[:, rows, :], self.got1[c])
        self.begin(c, 2)

    def along_z(self, c):
        p = self.place
        self.arrive(c, 2)
        rows = span(p.quarter_at, p.quarter)
        total = self.total(c)
        total[:, rows, :] = added(total[:, rows, :], self.got2[c])
        self.begin(c, 3)

    def finish(self, c):
        p = self.place
        self.arrive(c, 3)
        rows = span(p.piece_at(p.z), p.piece)
        value = self.total(c)[:, rows, :].astype(F32)
        for k in range(p.deep - 1):
            value = value + self.got_z[c, k].astype(F32)
        return value.astype(BF16)


class Gather:
    def __init__(self, place, piece, result, mirror, local, send, recv, send_z, recv_z):
        self.place, self.piece, self.result, self.mirror, self.local = place, piece, result, mirror, local
        self.send, self.recv, self.send_z, self.recv_z = send, recv, send_z, recv_z

    def kept(self, c):
        p = self.place
        return pltpu.make_async_copy(
            self.piece(c), self.result(c).at[:, span(p.piece_at(p.z), p.piece), :], self.local.at[c]
        )

    def copies(self, c, stage, landing=False):
        p, result = self.place, self.result(c)
        if stage == 0:
            made = []
            for k, peer in enumerate(p.peer_z):
                z = (p.z - k - 1 + p.deep) % p.deep if landing else p.z
                target = result.at[:, span(p.piece_at(z), p.piece), :]
                made.append(remote(self.piece(c), target, self.send_z.at[c, k], self.recv_z.at[c, k], peer))
            return made
        if stage == 1:
            source = result.at[:, span(p.quarter_at, p.quarter), :]
            target = result.at[:, span(p.quarter_off if landing else p.quarter_at, p.quarter), :]
            return [remote(source, target, self.send.at[c, 0], self.recv.at[c, 0], p.peer2)]
        if stage == 2:
            source = result.at[:, span(p.half_at, p.half), :]
            target = result.at[:, span(p.half_off if landing else p.half_at, p.half), :]
            return [remote(source, target, self.send.at[c, 1], self.recv.at[c, 1], p.peer1)]
        return [remote(result, self.mirror(c) if landing else result, self.send.at[c, 2], self.recv.at[c, 2], p.other)]

    def begin(self, c, stage):
        for copy in self.copies(c, stage):
            copy.start()

    def arrive(self, c, stage):
        for copy in self.copies(c, stage, landing=True):
            copy.wait_recv()

    def along_z(self, c):
        self.kept(c).start()
        self.begin(c, 0)

    def plane2(self, c):
        self.kept(c).wait()
        self.arrive(c, 0)
        self.begin(c, 1)

    def plane1(self, c):
        self.arrive(c, 1)
        self.begin(c, 2)

    def across(self, c):
        self.arrive(c, 2)
        self.begin(c, 3)

    def sent(self, c):
        for stage in range(3 if self.mirror is None else 4):
            for copy in self.copies(c, stage):
                copy.wait_send()


def vec_slot(slot, width):
    return slice(slot // 2, slot // 2 + 1), slice(slot % 2 * width, slot % 2 * width + width)


def head_back(slots, i, q_ref, k_ref, v_ref, probs_ref, gatt_ref, gq_ref, gk_ref, gv_ref):
    first = lax.broadcasted_iota(jnp.int32, (1, 2 * HEAD_DIM), 1) < HEAD_DIM
    zero = jnp.zeros((), BF16)
    scale = jnp.asarray(HEAD_DIM ** -0.5, BF16)
    pairs = q_ref.shape[1] // 128
    here = pl.ds(pl.multiple_of(i * slots, 16), slots)
    for pair in range(pairs):
        own = slice(pair * 128, pair * 128 + 128)
        query, key, value = q_ref[here, own], k_ref[here, own], v_ref[here, own]
        grad_att = gatt_ref[here, own]
        gq = gk = gv = None
        for half in range(2):
            mine = first if half == 0 else jnp.logical_not(first)
            low = probs_ref[i, 2 * pair + half]
            probs = low.astype(F32)
            g_mine = jnp.where(mine, grad_att, zero)
            grad_probs = dot_t(g_mine, value).astype(BF16).astype(F32)
            inner = jnp.sum(probs * grad_probs, axis=1, keepdims=True)
            grad_scores = (probs * (grad_probs - inner)).astype(BF16) * scale
            tv = t_dot(low, g_mine)
            tq = dot(grad_scores, jnp.where(mine, key, zero))
            tk = t_dot(grad_scores, jnp.where(mine, query, zero))
            gq = tq if gq is None else gq + tq
            gk = tk if gk is None else gk + tk
            gv = tv if gv is None else gv + tv
        gq_ref[here, own] = gq.astype(BF16)
        gk_ref[here, own] = gk.astype(BF16)
        gv_ref[here, own] = gv.astype(BF16)


def mlp_staged_kernel(
    deep, images, slots, ticks,
    hid_ref, gm_ref, sums_ref, w1a_ref, w1b_ref, b1a_ref, b1b_ref, w2a_ref, w2b_ref, g2_ref, bfc2_ref,
    att_hbm, mid_hbm, sel_hbm, wproj_hbm, normed_hbm, qkv_hbm, probs_hbm, wqkv_hbm,
    red_ref, gmid_ref, gatt_ref, dwp_ref, lo_ref, vec_ref, early_ref, dwh_ref, gn_hbm,
    att_ref, mid_ref, sel_ref, wproj_ref, normed_ref, q_ref, k_ref, v_ref, probs_ref, wq_ref, wk_ref, wv_ref,
    gq_ref, gk_ref, gv_ref, fetch_sem,
    out_ref, gh_ref, bias_ref, give_ref, own_ref, got_core, got1, got2, got_z, send, recv, send_z, recv_z,
    b_local, b_send, b_recv, b_send_z, b_recv_z,
):
    step = pl.program_id(0)
    rows, width = hid_ref.shape
    place = Place(deep, width)
    panels = 4
    chunk = w1a_ref.shape[1]
    reduce = Reduce(
        place, lambda c: own_ref.at[c], lambda c: give_ref.at[c], lambda c: own_ref.at[c],
        got_core, got1, got2, got_z, send, recv, send_z, recv_z,
    )

    back = Gather(
        place, lambda c: red_ref.at[pl.ds(c * panels, panels)], lambda c: early_ref.at[pl.ds(c * panels, panels)],
        None, b_local, b_send, b_recv, b_send_z, b_recv_z,
    )
    early = early_ref.shape[0] // panels

    wide = q_ref.shape[1]
    thirds = [slice(part * width, part * width + wide) for part in range(3)]
    sources = [att_hbm, mid_hbm, sel_hbm, wproj_hbm, normed_hbm] + [qkv_hbm.at[:, cols] for cols in thirds]
    sources += [probs_hbm.at[:, 0 : probs_ref.shape[1]]] + [wqkv_hbm.at[:, cols] for cols in thirds]
    held = [att_ref, mid_ref, sel_ref, wproj_ref, normed_ref, q_ref, k_ref, v_ref, probs_ref, wq_ref, wk_ref, wv_ref]
    fetched = [
        pltpu.make_async_copy(source, target, fetch_sem.at[j]) for j, (source, target) in enumerate(zip(sources, held))
    ]

    def put_red(c):
        red_ref[pl.ds(c * panels, panels)] = reduce.finish(c)

    def half(w1_ref, b1, w2_ref, target, db_row):
        hid, gm = hid_ref[...], gm_ref[...]
        w1, w2 = w1_ref[...], w2_ref[...]
        pre = dot(hid, w1) + bias_ref[b1, pl.ds(step, 1)]
        act, slope = gelu_pair(pre)
        act = act.astype(BF16)
        grad_act = dot_t(gm, w2).astype(BF16).astype(F32)
        grad_pre = (grad_act * slope).astype(BF16)
        d2 = t_dot(act, gm).astype(BF16)
        for j in range(width // 128):
            at = j % 3 * chunk
            target[2 + j // 3, at : at + chunk, :] = d2[:, j * 128 : j * 128 + 128]
        d1 = t_dot(hid, grad_pre).astype(BF16)
        target[0] = d1[:, :128]
        target[1] = d1[:, 128:]
        cols = pl.ds(pl.multiple_of(step * chunk, chunk), chunk)
        vec_ref[pl.ds(db_row, 1), cols] = jnp.sum(grad_pre.astype(F32), axis=0, keepdims=True)
        out_ref[...] += dot(act, w2)
        gh_ref[...] += dot_t(grad_pre, w1)

    @pl.when(step == 0)
    def _():
        for copy in fetched:
            copy.start()
        place.greet()
        out_ref[...] = jnp.zeros_like(out_ref)
        gh_ref[...] = jnp.zeros_like(gh_ref)
        for side, ref in enumerate((b1a_ref, b1b_ref)):
            line = as_row(ref)
            for c in range(ticks):
                bias_ref[side, c : c + 1] = line[:, c * chunk : (c + 1) * chunk]
        place.all_here()

    @pl.when((step >= 1) & (step <= ticks))
    def _():
        reduce.plane1(step - 1)

    @pl.when(step == ticks)
    def _():
        back.plane1(0)

    @pl.when((step >= 2) & (step <= ticks))
    def _():
        reduce.plane2(step - 2)

    @pl.when((step >= 3) & (step <= ticks))
    def _():
        reduce.along_z(step - 3)

    @pl.when((step >= 4) & (step <= ticks))
    def _():
        put_red(step - 4)
        back.along_z(step - 4)

    @pl.when(step < ticks)
    def _():
        half(w1b_ref, 1, w2b_ref, give_ref.at[step], 7 - place.core)

    @pl.when(step == ticks - 1)
    def _():
        back.plane2(0)

    @pl.when(step < ticks)
    def _():
        reduce.begin(step, 0)
        half(w1a_ref, 0, w2a_ref, own_ref.at[step], 6 + place.core)

    def note(slot, value):
        at_row, at_col = vec_slot(slot, width)
        vec_ref[at_row, at_col] = value

    def column_sum(value):
        return jnp.sum(value, axis=0, keepdims=True)

    @pl.when(step == ticks)
    def _():
        for copy in fetched:
            copy.wait()
        stream = mlp_sq = jnp.zeros((1, width), F32)
        gain = shift = b_two = b_proj = jnp.zeros((1, width), F32)
        for i in range(images):
            here = slice(i * slots, i * slots + slots)
            sel = sel_ref[i]
            middle = mid_ref[here]
            valid = jnp.sum(sel.astype(F32), axis=1, keepdims=True) > 0
            mlp_out = jnp.where(valid, out_ref[here] + as_row(bfc2_ref), 0.0)
            block = middle + mlp_out
            kept = jnp.where(valid, block, 0.0)
            stream = stream + column_sum(kept * kept)
            mlp_sq = mlp_sq + column_sum(mlp_out * mlp_out)
            lo_ref[i] = t_dot(sel, block.astype(BF16)).astype(BF16)
            scaled, inverse = norm_rows(middle)
            grad_hidden = gh_ref[here]
            gain = gain + column_sum(grad_hidden * scaled)
            shift = shift + column_sum(grad_hidden)
            gm = gm_ref[here].astype(F32)
            b_two = b_two + column_sum(gm)
            grad_middle = gm + norm_back(grad_hidden * as_row(g2_ref), scaled, inverse)
            gmid_ref[here] = grad_middle
            grad_attn = grad_middle.astype(BF16)
            b_proj = b_proj + column_sum(grad_attn.astype(F32))
            gatt_ref[here] = grad_attn
            if i == 2:
                back.plane2(1)
        for slot, value in enumerate((gain, shift, b_two, b_proj)):
            note(slot, value)
        note(8, stream)
        note(9, mlp_sq)
        note(10, sum(sums_ref[i, 0:1] for i in range(images)))
        note(11, sum(sums_ref[i, 1:2] for i in range(images)))
        reduce.plane2(ticks - 1)
        reduce.along_z(ticks - 2)
        put_red(ticks - 3)
        back.plane1(1)
        back.plane2(2)
        grad_attn = gatt_ref[...]
        for part in range(3):
            cols = slice(part * width // 3, (part + 1) * width // 3)
            d = t_dot(att_ref[...], grad_attn[:, cols]).astype(BF16)
            dwp_ref[0, part] = d[:, :128]
            dwp_ref[1, part] = d[:, 128:]
        gatt_ref[...] = dot_t(grad_attn, wproj_ref[...]).astype(BF16)

        @pl.loop(0, images)
        def _(i):
            @pl.when(i == 2)
            def _():
                reduce.along_z(ticks - 1)
                back.plane1(2)

            @pl.when(i == 4)
            def _():
                put_red(ticks - 2)

            head_back(slots, i, q_ref, k_ref, v_ref, probs_ref, gatt_ref, gq_ref, gk_ref, gv_ref)

        vec_ref[2:3, 0:wide] = column_sum(gq_ref[...].astype(F32))
        vec_ref[2:3, width : width + wide] = column_sum(gv_ref[...].astype(F32))
        total = None
        for part, (ref, w_ref) in enumerate(((gq_ref, wq_ref), (gk_ref, wk_ref), (gv_ref, wv_ref))):
            d = t_dot(normed_ref[...], ref[...]).astype(BF16)
            dwh_ref[0, part] = d[:, :128]
            dwh_ref[1, part] = d[:, 128:]
            term = dot_t(ref[...], w_ref[...])
            total = term if total is None else total + term
        gh_ref[...] = total
        keep_gn = pltpu.make_async_copy(gh_ref, gn_hbm, fetch_sem.at[0])
        keep_gn.start()
        put_red(ticks - 1)
        keep_gn.wait()

        @pl.loop(0, ticks)
        def _(c):
            reduce.sent(c)

        @pl.loop(0, early)
        def _(c):
            back.arrive(c, 2)
            back.sent(c)


def attention_staged_kernel(
    deep, images, slots, groups, ticks,
    q_ref, k_ref, v_ref, probs_ref, gatt_ref, wq_ref, wk_ref, wv_ref, g1_ref, dwp_ref, dwh_ref, red_ref, vecin_ref,
    normed_hbm, x_hbm, gmid_hbm, sel_hbm, gn_hbm,
    mlp_ref, attn_ref, gi_ref, vec_ref,
    gq_ref, gk_ref, gv_ref, gn_ref, stage_ref, total_ref, piece_ref, got_core, got1, got2, got_z,
    vsum_ref, vgot_ref, vz_ref,
    send, recv, send_z, recv_z, m_local, m_send, m_recv, m_send_z, m_recv_z,
    a_local, a_send, a_recv, a_send_z, a_recv_z, v_send, v_recv, v_send_z, v_recv_z,
    normed_ref, x_ref, gmid_ref, sel_ref, fetch_sem,
):
    step = pl.program_id(0)
    rows, width = x_ref.shape
    fetched = [
        pltpu.make_async_copy(source, target, fetch_sem.at[j])
        for j, (source, target) in enumerate(
            ((normed_hbm, normed_ref), (gn_hbm, gn_ref), (x_hbm, x_ref), (gmid_hbm, gmid_ref), (sel_hbm, sel_ref))
        )
    ]
    place = Place(deep, width)
    core = place.core
    polls = images + 2

    def partial_of(owner):
        def pick(c):
            if isinstance(c, int) and c < 2:
                return (dwp_ref, dwh_ref)[c].at[owner]
            return stage_ref.at[c - 2, owner]

        return pick

    reduce = Reduce(
        place, partial_of(core), partial_of(1 - core), lambda c: total_ref.at[c],
        got_core, got1, got2, got_z, send, recv, send_z, recv_z,
    )
    back = Gather(
        place, lambda c: piece_ref.at[c], lambda c: attn_ref.at[core, pl.ds(3 * c, 3)],
        lambda c: attn_ref.at[1 - core, pl.ds(3 * c, 3)], a_local, a_send, a_recv, a_send_z, a_recv_z,
    )
    late = mlp_ref.shape[0] // 4
    mlp = Gather(
        place, lambda c: red_ref.at[pl.ds(4 * (ticks - late + c), 4)], lambda c: mlp_ref.at[pl.ds(4 * c, 4)], None,
        m_local, m_send, m_recv, m_send_z, m_recv_z,
    )

    def turn(c):
        piece_ref[c] = reduce.finish(c)
        back.along_z(c)

    def do(name, c):
        return {
            "X": reduce.plane1, "Y": reduce.plane2, "Z": reduce.along_z, "R": turn,
            "ay": back.plane2, "ax": back.plane1, "ac": back.across,
            "my": mlp.plane2, "mx": mlp.plane1,
        }[name](c - (ticks - late) if name[0] == "m" else c)

    plan = {}
    for at, name, c in (
        (2, "X", 0), (2, "X", 1), (6, "Y", 0), (8, "my", 3), (9, "X", 2), (9, "Y", 1), (10, "Z", 0), (12, "my", 5),
        (13, "mx", 3), (15, "Z", 1), (16, "Y", 2), (16, "X", 3), (16, "R", 0), (18, "my", 4),
    ):
        plan.setdefault(at, []).append((name, c))
    tail = (
        ("Z", 2), ("R", 1), ("ay", 0), ("mx", 5), ("Y", 3), ("R", 2), ("ax", 0), ("ay", 1), ("Z", 3), ("ay", 2),
        ("ax", 1), ("ac", 0), ("R", 3), ("mx", 4), ("ax", 2), ("ac", 1), ("ay", 3), ("ac", 2), ("ax", 3),
        ("ac", 3),
    )

    def run(at, now):
        for moment, jobs in sorted(plan.items()):
            if moment < groups * polls and at(moment % polls):

                @pl.when(now == moment)
                def _(jobs=jobs):
                    for name, c in jobs:
                        do(name, c)

    wide = width // (groups + 1)

    @pl.when(step == 0)
    def _():
        for copy in fetched:
            copy.start()
        place.greet()
        vsum_ref[0] = vecin_ref[...]
        place.all_here()
        reduce.begin(0, 0)
        reduce.begin(1, 0)
        for c in range(late):
            mlp.along_z(c)

    @pl.when(step < groups)
    def _():
        @pl.loop(0, images)
        def _(i):
            run(lambda at: at < images, step * polls + i)
            head_back(slots, i, q_ref, k_ref, v_ref, probs_ref, gatt_ref, gq_ref, gk_ref, gv_ref)

        run(lambda at: at == images, step * polls + images)

        @pl.when(step == 0)
        def _():
            for copy in fetched[:2]:
                copy.wait()

        cols = pl.ds(pl.multiple_of((step + 1) * wide, wide), wide)
        shifted = pl.ds(pl.multiple_of(width + (step + 1) * wide, wide), wide)
        vsum_ref[0, 2:3, cols] = jnp.sum(gq_ref[...].astype(F32), axis=0, keepdims=True)
        vsum_ref[0, 2:3, shifted] = jnp.sum(gv_ref[...].astype(F32), axis=0, keepdims=True)
        for part, ref in enumerate((gq_ref, gk_ref, gv_ref)):
            d = t_dot(normed_ref[...], ref[...]).astype(BF16)
            stage_ref[step, 0, part] = d[:, :128]
            stage_ref[step, 1, part] = d[:, 128:]
        reduce.begin(step + 2, 0)
        for ref, w_ref in ((gq_ref, wq_ref), (gk_ref, wk_ref), (gv_ref, wv_ref)):
            gn_ref[...] += dot_t(ref[...], w_ref[...])
        run(lambda at: at == images + 1, step * polls + images + 1)

    def vec_copies(stage):
        if stage < 3:
            peer = (place.other, place.peer1, place.peer2)[stage]
            return [remote(vsum_ref.at[stage], vgot_ref.at[stage], v_send.at[stage], v_recv.at[stage], peer)]
        return [
            remote(vsum_ref.at[3], vz_ref.at[k], v_send_z.at[k], v_recv_z.at[k], peer)
            for k, peer in enumerate(place.peer_z)
        ]

    def vec_begin(stage):
        for copy in vec_copies(stage):
            copy.start()

    def vec_next(stage):
        for copy in vec_copies(stage):
            copy.wait_recv()
        if stage < 3:
            vsum_ref[stage + 1] = vsum_ref[stage] + vgot_ref[stage]
            vec_begin(stage + 1)

    @pl.when(step == groups)
    def _():
        for copy in fetched[2:]:
            copy.wait()
        g1 = as_row(g1_ref)
        gain = shift = jnp.zeros((1, width), F32)
        for i in range(images):
            for name, c in plan.get(groups * polls + i, ()):
                do(name, c)
            here = slice(i * slots, i * slots + slots)
            sel = sel_ref[i]
            scaled, inverse = norm_rows(x_ref[here].astype(F32))
            grad_normed = gn_ref[here]
            gain = gain + jnp.sum(grad_normed * scaled, axis=0, keepdims=True)
            shift = shift + jnp.sum(grad_normed, axis=0, keepdims=True)
            change = gmid_ref[here] + norm_back(grad_normed * g1, scaled, inverse)
            high = change.astype(BF16)
            rest = (change - high.astype(F32)).astype(BF16)
            gi_ref[i] = t_dot(sel, high) + t_dot(sel, rest)
        at_row, at_col = vec_slot(6, width)
        vsum_ref[0, at_row, at_col] = gain
        at_row, at_col = vec_slot(7, width)
        vsum_ref[0, at_row, at_col] = shift
        vec_begin(0)
        for at, (name, c) in enumerate(tail):
            do(name, c)
            if at % 3 == 2 and at // 3 < 4:
                vec_next(at // 3)
        value = None
        for z in range(deep):
            mine = vsum_ref[3]
            from_k = [vz_ref[k] for k in range(deep - 1)]
            term = mine
            for k in range(deep - 1):
                term = jnp.where((place.z - k - 1 + deep) % deep == z, from_k[k], term)
            value = term if value is None else value + term
        vec_ref[...] = value
        for c in range(late):
            mlp.arrive(c, 2)
            mlp.sent(c)
        for c in range(groups + 2):
            back.arrive(c, 3)
            back.sent(c)
            reduce.sent(c)
        for stage in range(4):
            for copy in vec_copies(stage):
                copy.wait_send()


def finish_kernel(
    groups, early,
    first_ref, second_ref, attn_ref, low_ref, put_ref, img_ref, cot_ref, keep_ref, vec_ref,
    lo_ref, gi_ref, wq_ref, wp_ref, w1_ref, w2_ref, b1_ref, root_ref, *small_refs,
):
    step = pl.program_id(0)
    width = low_ref.shape[2]
    chunk = w1_ref.shape[1]
    for big_ref, mine in ((first_ref, step < early), (second_ref, step >= early)):

        @pl.when(mine)
        def _(big_ref=big_ref):
            for j in range(chunk // 128):
                w1_ref[:, j * 128 : j * 128 + 128] = big_ref[j].astype(F32)
            for j in range(width // 128):
                at = j % 3 * chunk
                w2_ref[:, j * 128 : j * 128 + 128] = big_ref[2 + j // 3, at : at + chunk].astype(F32)

    for owner in range(2):
        for j in range(3):
            at = (2 * j + owner) * 128
            wp_ref[:, at : at + 128] = attn_ref[owner, j].astype(F32)
            for group in range(groups):
                at = j * width + (2 * group + owner) * 128
                wq_ref[:, at : at + 128] = attn_ref[owner, 3 + 3 * group + j].astype(F32)

    @pl.when(step < keep_ref.shape[0])
    def _():
        keep = keep_ref[pl.ds(step, 1)].astype(F32)
        eight = jnp.broadcast_to(keep, (8, keep.shape[1])).astype(BF16)
        once = jnp.where(lax.broadcasted_iota(jnp.int32, (8, 128), 0) == 0, 1.0, 0.0).astype(BF16)
        kept = t_dot(eight, once)[:, 0:1] > 0.5
        lo_ref[0] = jnp.where(kept, low_ref[0], img_ref[0])
        gi_ref[0] = jnp.where(kept, put_ref[0], cot_ref[0].astype(F32))

    @pl.when(step == 0)
    def _():
        def line(slot):
            at_row, at_col = vec_slot(slot, width)
            return vec_ref[at_row, at_col]

        for slot, ref in enumerate(small_refs):
            ref[...] = line(slot).reshape(width)
        b1_ref[...] = vec_ref[pl.ds(6 + lax.axis_index("mlp"), 1)].reshape(2 * width)
        count = line(11)[:, 0:1]
        lane = lax.broadcasted_iota(jnp.int32, (1, 128), 1)
        sums = jnp.where(lane == 0, jnp.sum(line(8)), jnp.where(lane == 1, jnp.sum(line(10)), jnp.sum(line(9))))
        root_ref[...] = jnp.sqrt(sums / (count * width)).reshape(128)[:3]


def staged_device(
    deep, images, keep_mask, ln1_gain, ln1_bias, w_qkv, bias_q, bias_v, w_proj, b_proj,
    ln2_gain, ln2_bias, w_fc1, b_fc1, w_fc2, b_fc2, cotangent,
):
    count, patches, width = images.shape
    slots = slots_of(patches)
    rows = count * slots
    heads = width // HEAD_DIM
    shard = w_fc1.shape[1]
    row = lambda v: v.reshape(1, -1)
    shape = jax.ShapeDtypeStruct
    limit = 62 * 2**20
    any_space = pl.BlockSpec(memory_space=pl.ANY)
    per_image = lambda *tail: pl.BlockSpec((1,) + tail, lambda i: (i,) + (0,) * len(tail))
    per_rows = lambda cols: pl.BlockSpec((slots, cols), lambda i: (i, 0))
    dma = pltpu.SemaphoreType.DMA
    sel, x, normed, qkv, probs, att, mid, hid, gm, sums, far_w1, far_b1, far_w2 = pl.pallas_call(
        functools.partial(forward_kernel, slots, True),
        grid=(count,),
        out_shape=(
            shape((count, slots, patches), BF16),
            shape((rows, width), BF16),
            shape((rows, width), BF16),
            shape((rows, 3 * width), BF16),
            shape((count, heads, slots, slots), BF16),
            shape((rows, width), BF16),
            shape((rows, width), F32),
            shape((rows, width), BF16),
            shape((rows, width), BF16),
            shape((count, 8, width), F32),
            shape((width, shard), BF16), shape((shard,), BF16), shape((shard, width), BF16),
        ),
        in_specs=[
            whole((count, patches)), per_image(patches, width), per_image(patches, width),
            whole((width,)), whole((width,)), whole((width, 3 * width)), whole((width,)), whole((width,)),
            whole((width, width)), whole((width,)), whole((width,)), whole((width,)),
            any_space, any_space, any_space,
        ],
        out_specs=(
            per_image(slots, patches), per_rows(width), per_rows(width), per_rows(3 * width),
            per_image(heads, slots, slots), per_rows(width), per_rows(width), per_rows(width), per_rows(width),
            per_image(8, width), any_space, any_space, any_space,
        ),
        scratch_shapes=[dma((3,)), dma((3,))],
        compiler_params=pltpu.CompilerParams(vmem_limit_bytes=limit, collective_id=0, has_side_effects=True),
        name="attention_forward",
    )(
        keep_mask, images, cotangent, ln1_gain, ln1_bias, w_qkv, bias_q, bias_v, w_proj, b_proj, ln2_gain, ln2_bias,
        w_fc1, b_fc1, w_fc2,
    )
    chunk = 256
    ticks = shard // chunk
    groups = 3
    piece = width // 4 // deep
    by_cols = lambda *lead: pl.BlockSpec(lead + (chunk,), lambda c: (0, c - c // ticks))
    by_rows = pl.BlockSpec((chunk, width), lambda c: (c - c // ticks, 0))
    early = ticks // 2
    wide = width // groups
    red, gmid, gatt, dwp, low, vec, first, dwh, gn = pl.pallas_call(
        functools.partial(mlp_staged_kernel, deep, count, slots, ticks),
        grid=(ticks + 1,),
        out_shape=(
            shape((4 * ticks, piece, 128), BF16), shape((rows, width), F32), shape((rows, width), BF16),
            shape((2, 3, width, 128), BF16), shape((count, patches, width), BF16), shape((8, 2 * width), F32),
            shape((4 * early, width, 128), BF16), shape((2, 3, width, 128), BF16), shape((rows, width), F32),
        ),
        in_specs=[
            whole((rows, width)), whole((rows, width)), whole((count, 8, width)),
            by_cols(width), by_cols(width), whole((shard,)), whole((shard,)), by_rows, by_rows,
            whole((width,)), whole((width,)),
        ] + 8 * [any_space],
        out_specs=(
            whole((4 * ticks, piece, 128)), whole((rows, width)), whole((rows, width)),
            whole((2, 3, width, 128)), whole((count, patches, width)), whole((8, 2 * width)), any_space,
            whole((2, 3, width, 128)), any_space,
        ),
        scratch_shapes=[
            pltpu.VMEM((rows, width), BF16), pltpu.VMEM((rows, width), F32), pltpu.VMEM((count, slots, patches), BF16),
            pltpu.VMEM((width, width), BF16), pltpu.VMEM((rows, width), BF16),
            pltpu.VMEM((rows, wide), BF16), pltpu.VMEM((rows, wide), BF16), pltpu.VMEM((rows, wide), BF16),
            pltpu.VMEM((count, heads // groups, slots, slots), BF16),
            pltpu.VMEM((width, wide), BF16), pltpu.VMEM((width, wide), BF16), pltpu.VMEM((width, wide), BF16),
            pltpu.VMEM((rows, wide), BF16), pltpu.VMEM((rows, wide), BF16), pltpu.VMEM((rows, wide), BF16), dma((12,)),
            pltpu.VMEM((rows, width), F32), pltpu.VMEM((rows, width), F32), pltpu.VMEM((2, 8, chunk), F32),
            pltpu.VMEM((ticks, 4, width, 128), BF16), pltpu.VMEM((ticks, 4, width, 128), BF16),
            pltpu.VMEM((ticks, 4, width, 128), BF16), pltpu.VMEM((ticks, 4, width // 2, 128), BF16),
            pltpu.VMEM((ticks, 4, width // 4, 128), BF16), pltpu.VMEM((ticks, deep - 1, 4, piece, 128), BF16),
            dma((ticks, 3)), dma((ticks, 3)), dma((ticks, deep - 1)), dma((ticks, deep - 1)),
            dma((early,)), dma((early, 2)), dma((early, 2)), dma((early, deep - 1)), dma((early, deep - 1)),
        ],
        compiler_params=pltpu.CompilerParams(vmem_limit_bytes=limit, collective_id=1, has_side_effects=True),
        name="mlp_both_ways",
    )(
        hid, gm, sums, w_fc1, far_w1, b_fc1, far_b1, w_fc2, far_w2, ln2_gain, b_fc2,
        att, mid, sel, w_proj, normed, qkv, probs, w_qkv,
    )
    chunks = groups + 1
    left = groups - 1
    now = lambda g: 1 + g - g // left
    third = lambda lead, part: pl.BlockSpec((lead, wide), lambda g: (0, part * groups + now(g)))
    late = ticks - early
    second, attn, put, vec = pl.pallas_call(
        functools.partial(attention_staged_kernel, deep, count, slots, left, ticks),
        grid=(left + 1,),
        out_shape=(
            shape((4 * late, width, 128), BF16), shape((2, 3 * chunks, width, 128), BF16),
            shape((count, patches, width), F32), shape((8, 2 * width), F32),
        ),
        in_specs=[
            third(rows, 0), third(rows, 1), third(rows, 2),
            pl.BlockSpec((count, heads // groups, slots, slots), lambda g: (0, now(g), 0, 0)),
            third(rows, 0), third(width, 0), third(width, 1), third(width, 2),
            whole((width,)), whole((2, 3, width, 128)), whole((2, 3, width, 128)), whole((4 * ticks, piece, 128)),
            whole((8, 2 * width)),
        ] + 5 * [any_space],
        out_specs=(any_space, any_space, whole((count, patches, width)), whole((8, 2 * width))),
        scratch_shapes=[
            pltpu.VMEM((rows, wide), BF16), pltpu.VMEM((rows, wide), BF16), pltpu.VMEM((rows, wide), BF16),
            pltpu.VMEM((rows, width), F32),
            pltpu.VMEM((left, 2, 3, width, 128), BF16), pltpu.VMEM((chunks, 3, width, 128), BF16),
            pltpu.VMEM((chunks, 3, piece, 128), BF16), pltpu.VMEM((chunks, 3, width, 128), BF16),
            pltpu.VMEM((chunks, 3, width // 2, 128), BF16), pltpu.VMEM((chunks, 3, width // 4, 128), BF16),
            pltpu.VMEM((chunks, deep - 1, 3, piece, 128), BF16),
            pltpu.VMEM((4, 8, 2 * width), F32), pltpu.VMEM((3, 8, 2 * width), F32),
            pltpu.VMEM((deep - 1, 8, 2 * width), F32),
            dma((chunks, 3)), dma((chunks, 3)), dma((chunks, deep - 1)), dma((chunks, deep - 1)),
            dma((late,)), dma((late, 2)), dma((late, 2)), dma((late, deep - 1)), dma((late, deep - 1)),
            dma((chunks,)), dma((chunks, 3)), dma((chunks, 3)), dma((chunks, deep - 1)), dma((chunks, deep - 1)),
            dma((3,)), dma((3,)), dma((deep - 1,)), dma((deep - 1,)),
            pltpu.VMEM((rows, width), BF16), pltpu.VMEM((rows, width), BF16), pltpu.VMEM((rows, width), F32),
            pltpu.VMEM((count, slots, patches), BF16), dma((5,)),
        ],
        compiler_params=pltpu.CompilerParams(vmem_limit_bytes=limit, collective_id=2, has_side_effects=True),
        name="attention_backward",
    )(
        qkv, qkv, qkv, probs, gatt, w_qkv, w_qkv, w_qkv, ln1_gain, dwp, dwh, red, vec, normed, x, gmid, sel, gn,
    )
    deal = width // ticks
    turn = lambda t: (t - t // count, 0, 0)
    layer_out, grad_images, s_wq, s_wp, s_w1, s_w2, s_b1, root_means, *small = pl.pallas_call(
        functools.partial(finish_kernel, groups, early),
        grid=(ticks,),
        out_shape=(
            shape((count, patches, width), BF16), shape((count, patches, width), F32),
            shape((width, 3 * width), F32), shape((width, width), F32), shape((width, shard), F32),
            shape((shard, width), F32), shape((shard,), F32), shape((3,), F32),
        ) + 8 * (shape((width,), F32),),
        in_specs=[
            pl.BlockSpec((4, width, 128), lambda t: (jnp.minimum(t, early - 1), 0, 0)),
            pl.BlockSpec((4, width, 128), lambda t: (jnp.maximum(t - early, 0), 0, 0)),
            pl.BlockSpec((2, 3 * chunks, deal, 128), lambda t: (0, 0, t, 0)),
            pl.BlockSpec((1, patches, width), turn), pl.BlockSpec((1, patches, width), turn),
            pl.BlockSpec((1, patches, width), turn), pl.BlockSpec((1, patches, width), turn),
            whole((count, patches)), whole((8, 2 * width)),
        ],
        out_specs=(
            pl.BlockSpec((1, patches, width), turn), pl.BlockSpec((1, patches, width), turn),
            pl.BlockSpec((deal, 3 * width), lambda t: (t, 0)), pl.BlockSpec((deal, width), lambda t: (t, 0)),
            pl.BlockSpec((width, chunk), lambda t: (0, t)), pl.BlockSpec((chunk, width), lambda t: (t, 0)),
            whole((shard,)), whole((3,)),
        ) + 8 * (whole((width,)),),
        compiler_params=pltpu.CompilerParams(vmem_limit_bytes=limit),
        name="results",
    )(first, second, attn, low, put, images, cotangent, keep_mask, vec)
    gain2, shift2, b_two, b_project, b_query, b_value, gain1, shift1 = small
    return (
        layer_out, grad_images, gain1, shift1, s_wq, b_query, b_value, s_wp, b_project, gain2, shift2,
        s_w1, s_b1, s_w2, b_two, root_means,
    )


def solution(mesh):
    rows, line = P(("img", "mlp"), None, None), P(("img", "mlp"), None)
    deep = mesh.shape["img"] // 4
    staged = mesh.shape["img"] == 4 * deep and mesh.shape["mlp"] == 2 and 1 < deep <= 4
    return jax.shard_map(
        functools.partial(staged_device, deep) if staged else plain_device,
        mesh=mesh,
        in_specs=(
            rows, line, P(), P(), P(), P(), P(), P(), P(), P(), P(),
            P(None, "mlp"), P("mlp"), P("mlp", None), P(), rows,
        ),
        out_specs=(
            rows, rows, P(), P(), P(), P(), P(), P(), P(), P(), P(),
            P(None, "mlp"), P("mlp"), P("mlp", None), P(), P(),
        ),
        check_vma=False,
    )
```

```python
import functools

import jax
import jax.numpy as jnp
from jax import lax
from jax.experimental import pallas as pl
from jax.experimental.pallas import tpu as pltpu
from jax.sharding import PartitionSpec as P

HEAD_DIM = 64
NORM_EPS = 1e-06
F32 = jnp.float32
BF16 = jnp.bfloat16
MESH = pl.DeviceIdType.MESH
ERFC_POLY = (
    -0.05792342897865154,
    0.27982426175045266,
    -0.47905523971588865,
    0.27061712140601424,
    -0.022718349995155727,
    0.2015184791612061,
    0.24328701077158832,
    0.2823637910445855,
    0.2820864086305586,
)


def dot(a, b):
    return jnp.dot(a, b, preferred_element_type=F32)


def dot_t(a, b):
    return lax.dot_general(a, b, (((1,), (1,)), ((), ())), preferred_element_type=F32)


def t_dot(a, b):
    return lax.dot_general(a, b, (((0,), (0,)), ((), ())), preferred_element_type=F32)


def slots_of(patches):
    most = 4 * patches // 5
    return -(-most // 16) * 16


def norm_rows(rows):
    center = rows - jnp.mean(rows, axis=1, keepdims=True)
    inverse = lax.rsqrt(jnp.mean(center * center, axis=1, keepdims=True) + NORM_EPS)
    return center * inverse, inverse


def norm_back(weighted, scaled, inverse):
    return inverse * (
        weighted
        - jnp.mean(weighted, axis=1, keepdims=True)
        - scaled * jnp.mean(weighted * scaled, axis=1, keepdims=True)
    )


def gelu_pair(values):
    reach = jnp.abs(values) * 0.7071067811865476
    inv = 1.0 / (1.0 + 0.5 * reach)
    decay = jnp.exp(-0.5 * (values * values))
    poly = jnp.full_like(values, ERFC_POLY[0])
    for coefficient in ERFC_POLY[1:]:
        poly = poly * inv + coefficient
    tail = (0.5 * inv) * poly * decay
    share = jnp.where(values > 0, 1.0 - tail, tail)
    return values * share, share + values * (decay * 0.3989422804014327)


def swap_weights(ours, theirs, send_sem, recv_sem):
    other = {"mlp": 1 - lax.axis_index("mlp")}
    copies = [
        pltpu.make_async_remote_copy(
            src_ref=ours[j], dst_ref=theirs[j], send_sem=send_sem.at[j], recv_sem=recv_sem.at[j],
            device_id=other, device_id_type=MESH,
        )
        for j in range(len(ours))
    ]

    def trade(begin):
        @pl.when(pl.program_id(0) == (0 if begin else pl.num_programs(0) - 1))
        def _():
            if begin:
                barrier = pltpu.get_barrier_semaphore()
                pl.semaphore_signal(barrier, inc=1, device_id=other, device_id_type=MESH)
                pl.semaphore_wait(barrier, 1)
            for copy in copies:
                if begin:
                    copy.start()
                else:
                    copy.wait()

    return trade


def as_row(ref):
    return ref[...].astype(F32).reshape(1, -1)


def forward_kernel(
    slots,
    keep_ref, img_ref, cot_ref, g1_ref, b1_ref, wqkv_ref, bq_ref, bv_ref, wproj_ref, bproj_ref, g2_ref, b2_ref,
    sel_ref, x_ref, normed_ref, qkv_ref, probs_ref, att_ref, mid_ref, hid_ref, gm_ref, sums_ref,
):
    patches, width = img_ref.shape[1:]
    heads = width // HEAD_DIM
    keep = keep_ref[pl.ds(pl.program_id(0), 1)].astype(F32)
    upto = lax.broadcasted_iota(jnp.int32, (patches, patches), 0) <= lax.broadcasted_iota(
        jnp.int32, (patches, patches), 1
    )
    keep8 = jnp.broadcast_to(keep, (8, patches)).astype(BF16)
    rank = dot(keep8, upto.astype(F32).astype(BF16))[0:1]
    count = jnp.sum(keep, axis=1, keepdims=True)
    slot = lax.broadcasted_iota(jnp.int32, (slots, patches), 0).astype(F32)
    sel = jnp.where((slot == rank - 1.0) & (keep > 0), 1.0, 0.0).astype(BF16)
    sel_ref[0] = sel
    gm_ref[...] = dot(sel, cot_ref[0]).astype(BF16)
    rows = dot(sel, img_ref[0])
    x_ref[...] = rows.astype(BF16)
    scaled, _ = norm_rows(rows)
    normed = (scaled * as_row(g1_ref) + as_row(b1_ref)).astype(BF16)
    normed_ref[...] = normed
    for part in range(3):
        cols = slice(part * width, (part + 1) * width)
        block = dot(normed, wqkv_ref[:, cols])
        if part == 0:
            block = block + as_row(bq_ref)
        if part == 2:
            block = block + as_row(bv_ref)
        qkv_ref[:, cols] = block.astype(BF16)
    closed = jnp.where(
        lax.broadcasted_iota(jnp.int32, (1, slots), 1).astype(F32) < count, 0.0, -1e30
    )
    first = lax.broadcasted_iota(jnp.int32, (1, 2 * HEAD_DIM), 1) < HEAD_DIM
    zero = jnp.zeros((), BF16)
    for pair in range(heads // 2):
        lanes = slice(pair * 128, pair * 128 + 128)
        query = qkv_ref[:, lanes] * jnp.asarray(HEAD_DIM ** -0.5, BF16)
        key = qkv_ref[:, width + pair * 128 : width + pair * 128 + 128]
        value = qkv_ref[:, 2 * width + pair * 128 : 2 * width + pair * 128 + 128]
        total = None
        for half in range(2):
            mine = first if half == 0 else jnp.logical_not(first)
            scores = dot_t(query, jnp.where(mine, key, zero)) + closed
            raised = jnp.exp(scores - jnp.max(scores, axis=1, keepdims=True))
            probs = (raised * (1.0 / jnp.sum(raised, axis=1, keepdims=True))).astype(BF16)
            probs_ref[0, 2 * pair + half] = probs
            term = dot(probs, jnp.where(mine, value, zero))
            total = term if total is None else total + term
        att_ref[:, lanes] = total.astype(BF16)
    attn_out = dot(att_ref[...], wproj_ref[...]) + as_row(bproj_ref)
    valid = lax.broadcasted_iota(jnp.int32, (slots, 1), 0).astype(F32) < count
    attn_kept = jnp.where(valid, attn_out, 0.0)
    middle = rows + attn_kept
    mid_ref[...] = middle
    sums_ref[0, 0:1] = jnp.sum(attn_kept * attn_kept, axis=0, keepdims=True)
    sums_ref[0, 1:2] = jnp.broadcast_to(count, (1, width))
    scaled, _ = norm_rows(middle)
    hid_ref[...] = (scaled * as_row(g2_ref) + as_row(b2_ref)).astype(BF16)


def forward_staged_kernel(
    slots,
    keep_ref, g1_ref, b1_ref, bq_ref, bv_ref, bproj_ref, g2_ref, b2_ref,
    img_hbm, cot_hbm, wqkv_hbm, wproj_hbm, w1_hbm, bias1_hbm, w2_hbm,
    sums_ref, sel_hbm, x_hbm, normed_hbm, qkv_hbm, probs_hbm, att_hbm, mid_hbm, hid_hbm, gm_hbm,
    far_w1, far_bias1, far_w2,
    img_ref, cot_ref,
    wqkv_ref, wproj_ref, sel_ref, x_ref, normed_ref, qkv_ref, probs_ref, att_ref, mid_ref, hid_ref, gm_ref,
    row_sem, in_sem, out_sem, probs_sem, part_sem, send_sem, recv_sem,
):
    images, patches, width = img_ref.shape
    heads = width // HEAD_DIM
    fetched = [
        pltpu.make_async_copy(wqkv_hbm, wqkv_ref, in_sem.at[0]), pltpu.make_async_copy(wproj_hbm, wproj_ref, in_sem.at[1])
    ]

    def row_copies(i):
        return [
            pltpu.make_async_copy(img_hbm.at[i], img_ref.at[i], row_sem.at[i, 0]),
            pltpu.make_async_copy(cot_hbm.at[i], cot_ref.at[i], row_sem.at[i, 1]),
        ]

    for i in range(images):
        for copy in row_copies(i):
            copy.start()
    for copy in fetched:
        copy.start()
    trade = swap_weights((w1_hbm, bias1_hbm, w2_hbm), (far_w1, far_bias1, far_w2), send_sem, recv_sem)
    trade(True)
    upto = lax.broadcasted_iota(jnp.int32, (patches, patches), 0) <= lax.broadcasted_iota(
        jnp.int32, (patches, patches), 1
    )
    upto = upto.astype(F32).astype(BF16)
    slot = lax.broadcasted_iota(jnp.int32, (slots, patches), 0).astype(F32)
    g1, b1, g2, b2 = (as_row(ref) for ref in (g1_ref, b1_ref, g2_ref, b2_ref))

    def rows_of(i):
        return pl.ds(pl.multiple_of(i * slots, 16), slots)

    def count_of(i):
        return jnp.sum(keep_ref[pl.ds(i, 1)].astype(F32), axis=1, keepdims=True)

    @pl.loop(0, images)
    def _(i):
        for copy in row_copies(i):
            copy.wait()
        here = rows_of(i)
        keep = keep_ref[pl.ds(i, 1)].astype(F32)
        keep8 = jnp.broadcast_to(keep, (8, patches)).astype(BF16)
        rank = dot(keep8, upto)[0:1]
        sel = jnp.where((slot == rank - 1.0) & (keep > 0), 1.0, 0.0).astype(BF16)
        sel_ref[i] = sel
        gm_ref[here] = dot(sel, cot_ref[i]).astype(BF16)
        rows = dot(sel, img_ref[i])
        x_ref[here] = rows.astype(BF16)
        scaled, _ = norm_rows(rows)
        normed_ref[here] = (scaled * g1 + b1).astype(BF16)

    sent = [
        pltpu.make_async_copy(source, target, out_sem.at[j])
        for j, (source, target) in enumerate(
            (
                (sel_ref, sel_hbm), (x_ref, x_hbm), (normed_ref, normed_hbm), (gm_ref, gm_hbm), (qkv_ref, qkv_hbm),
                (att_ref, att_hbm),
            )
        )
    ]
    for copy in sent[:4]:
        copy.start()
    fetched[0].wait()
    wide = width // 3
    for j in range(9):
        cols = slice(j * wide, j * wide + wide)
        block = dot(normed_ref[...], wqkv_ref[:, cols])
        own = slice(j % 3 * wide, j % 3 * wide + wide)
        if j < 3:
            block = block + as_row(bq_ref)[:, own]
        if j >= 6:
            block = block + as_row(bv_ref)[:, own]
        qkv_ref[:, cols] = block.astype(BF16)
    sent[4].start()
    first = lax.broadcasted_iota(jnp.int32, (1, 2 * HEAD_DIM), 1) < HEAD_DIM
    zero = jnp.zeros((), BF16)

    def probs_copy(i):
        return pltpu.make_async_copy(probs_ref.at[i], probs_hbm.at[i], probs_sem.at[i])

    @pl.loop(0, images)
    def _(i):
        here = rows_of(i)
        closed = jnp.where(
            lax.broadcasted_iota(jnp.int32, (1, slots), 1).astype(F32) < count_of(i), 0.0, -1e30
        )
        for pair in range(heads // 2):
            lanes = slice(pair * 128, pair * 128 + 128)
            query = qkv_ref[here, lanes] * jnp.asarray(HEAD_DIM ** -0.5, BF16)
            key = qkv_ref[here, width + pair * 128 : width + pair * 128 + 128]
            value = qkv_ref[here, 2 * width + pair * 128 : 2 * width + pair * 128 + 128]
            total = None
            for half in range(2):
                mine = first if half == 0 else jnp.logical_not(first)
                scores = dot_t(query, jnp.where(mine, key, zero)) + closed
                raised = jnp.exp(scores - jnp.max(scores, axis=1, keepdims=True))
                probs = (raised * (1.0 / jnp.sum(raised, axis=1, keepdims=True))).astype(BF16)
                probs_ref[i, 2 * pair + half] = probs
                term = dot(probs, jnp.where(mine, value, zero))
                total = term if total is None else total + term
            att_ref[here, lanes] = total.astype(BF16)
        probs_copy(i).start()

    sent[5].start()
    fetched[1].wait()
    mid_ref[...] = dot(att_ref[...], wproj_ref[...]) + as_row(bproj_ref)

    def part_copies(i):
        here = rows_of(i)
        return [
            pltpu.make_async_copy(mid_ref.at[here], mid_hbm.at[here], part_sem.at[i, 0]),
            pltpu.make_async_copy(hid_ref.at[here], hid_hbm.at[here], part_sem.at[i, 1]),
        ]

    @pl.loop(0, images)
    def _(i):
        here = rows_of(i)
        count = count_of(i)
        valid = lax.broadcasted_iota(jnp.int32, (slots, 1), 0).astype(F32) < count
        attn_kept = jnp.where(valid, mid_ref[here], 0.0)
        middle = x_ref[here].astype(F32) + attn_kept
        mid_ref[here] = middle
        sums_ref[i, 0:1] = jnp.sum(attn_kept * attn_kept, axis=0, keepdims=True)
        sums_ref[i, 1:2] = jnp.broadcast_to(count, (1, width))
        scaled, _ = norm_rows(middle)
        hid_ref[here] = (scaled * g2 + b2).astype(BF16)
        for copy in part_copies(i):
            copy.start()

    for copy in sent:
        copy.wait()

    @pl.loop(0, images)
    def _(i):
        probs_copy(i).wait()
        for copy in part_copies(i):
            copy.wait()

    trade(False)


def mlp_kernel(hid_ref, gm_ref, w1_ref, b1_ref, w2_ref, out_ref, gh_ref, dw1_ref, dw2_ref, db1_ref):
    step = pl.program_id(0)
    hid, gm = hid_ref[...], gm_ref[...]
    w1, w2 = w1_ref[0], w2_ref[0]
    pre = dot(hid, w1) + b1_ref[0].astype(F32)
    act, slope = gelu_pair(pre)
    act = act.astype(BF16)
    grad_act = dot_t(gm, w2).astype(BF16).astype(F32)
    grad_pre_f = grad_act * slope
    grad_pre = grad_pre_f.astype(BF16)
    dw2_ref[0] = t_dot(act, gm).astype(BF16)
    dw1_ref[0] = t_dot(hid, grad_pre).astype(BF16)
    db1_ref[0] = jnp.sum(grad_pre.astype(F32), axis=0, keepdims=True)

    @pl.when(step == 0)
    def _():
        out_ref[...] = dot(act, w2)
        gh_ref[...] = dot_t(grad_pre, w1)

    @pl.when(step > 0)
    def _():
        out_ref[...] += dot(act, w2)
        gh_ref[...] += dot_t(grad_pre, w1)


def backward_kernel(
    images, slots, groups,
    sel_ref, x_ref, normed_ref, qkv_ref, probs_ref, att_ref, mid_ref, gm_ref, gh_ref, mlp_ref, valid_ref,
    g1_ref, g2_ref, bfc2_ref, wqkv_ref, wproj_ref, img_ref, cot_ref,
    lo_ref, gi_ref, dwp_ref, dwq_ref, vec_ref,
    gmid_ref, gatt_ref, gq_ref, gk_ref, gv_ref, gn_ref,
):
    step = pl.program_id(0)
    rows, width = x_ref.shape

    @pl.when(step == 0)
    def _():
        middle = mid_ref[...]
        valid = valid_ref[...] > 0
        mlp_out = jnp.where(valid, mlp_ref[...] + bfc2_ref[...].astype(F32), 0.0)
        block = middle + mlp_out
        kept = jnp.where(valid, block, 0.0)
        vec_ref[8:9] = jnp.sum(kept * kept, axis=0, keepdims=True)
        vec_ref[9:10] = jnp.sum(mlp_out * mlp_out, axis=0, keepdims=True)
        low = block.astype(BF16)
        for i in range(images):
            put = t_dot(sel_ref[i], low[i * slots : (i + 1) * slots])
            here = jnp.sum(sel_ref[i].astype(F32), axis=0, keepdims=True)
            lo_ref[i] = put.astype(BF16)
        scaled, inverse = norm_rows(middle)
        grad_hidden = gh_ref[...]
        vec_ref[0:1] = jnp.sum(grad_hidden * scaled, axis=0, keepdims=True)
        vec_ref[1:2] = jnp.sum(grad_hidden, axis=0, keepdims=True)
        gm = gm_ref[...].astype(F32)
        vec_ref[2:3] = jnp.sum(gm, axis=0, keepdims=True)
        grad_middle = gm + norm_back(grad_hidden * g2_ref[...], scaled, inverse)
        gmid_ref[...] = grad_middle
        grad_attn = grad_middle.astype(BF16)
        vec_ref[3:4] = jnp.sum(grad_attn.astype(F32), axis=0, keepdims=True)
        dwp_ref[...] = t_dot(att_ref[...], grad_attn).astype(BF16)
        gatt_ref[...] = dot_t(grad_attn, wproj_ref[...]).astype(BF16)
        gn_ref[...] = jnp.zeros_like(gn_ref)

    first = lax.broadcasted_iota(jnp.int32, (1, 2 * HEAD_DIM), 1) < HEAD_DIM
    zero = jnp.zeros((), BF16)
    scale = jnp.asarray(HEAD_DIM ** -0.5, BF16)
    pairs = width // 128 // groups
    for group in range(groups):

        @pl.when(step == group + 1)
        def _():
            base = group * pairs * 128

            @pl.loop(0, images)
            def _(i):
                here = pl.ds(pl.multiple_of(i * slots, 16), slots)
                for pair in range(pairs):
                    at = base + pair * 128
                    own = slice(pair * 128, pair * 128 + 128)
                    query = qkv_ref[here, at : at + 128]
                    key = qkv_ref[here, width + at : width + at + 128]
                    value = qkv_ref[here, 2 * width + at : 2 * width + at + 128]
                    grad_att = gatt_ref[here, at : at + 128]
                    gq = gk = gv = None
                    for half in range(2):
                        mine = first if half == 0 else jnp.logical_not(first)
                        low = probs_ref[i, 2 * (base // 128 + pair) + half]
                        probs = low.astype(F32)
                        g_mine = jnp.where(mine, grad_att, zero)
                        grad_probs = dot_t(g_mine, value).astype(BF16).astype(F32)
                        inner = jnp.sum(probs * grad_probs, axis=1, keepdims=True)
                        grad_scores = (probs * (grad_probs - inner)).astype(BF16) * scale
                        tv = t_dot(low, g_mine)
                        tq = dot(grad_scores, jnp.where(mine, key, zero))
                        tk = t_dot(grad_scores, jnp.where(mine, query, zero))
                        gq = tq if gq is None else gq + tq
                        gk = tk if gk is None else gk + tk
                        gv = tv if gv is None else gv + tv
                    gq_ref[here, own] = gq.astype(BF16)
                    gk_ref[here, own] = gk.astype(BF16)
                    gv_ref[here, own] = gv.astype(BF16)

            span = pairs * 128
            vec_ref[4:5, base : base + span] = jnp.sum(gq_ref[...].astype(F32), axis=0, keepdims=True)
            vec_ref[5:6, base : base + span] = jnp.sum(gv_ref[...].astype(F32), axis=0, keepdims=True)
            for part, ref in enumerate((gq_ref, gk_ref, gv_ref)):
                cols = slice(part * width + base, part * width + base + span)
                dwq_ref[:, cols] = t_dot(normed_ref[...], ref[...]).astype(BF16)
                gn_ref[...] += dot_t(ref[...], wqkv_ref[:, cols])

    @pl.when(step == groups + 1)
    def _():
        scaled, inverse = norm_rows(x_ref[...].astype(F32))
        grad_normed = gn_ref[...]
        vec_ref[6:7] = jnp.sum(grad_normed * scaled, axis=0, keepdims=True)
        vec_ref[7:8] = jnp.sum(grad_normed, axis=0, keepdims=True)
        change = gmid_ref[...] + norm_back(grad_normed * g1_ref[...], scaled, inverse)
        high = change.astype(BF16)
        rest = (change - high.astype(F32)).astype(BF16)
        for i in range(images):
            here = slice(i * slots, (i + 1) * slots)
            gi_ref[i] = t_dot(sel_ref[i], high[here]) + t_dot(sel_ref[i], rest[here])


def whole(shape):
    return pl.BlockSpec(shape, lambda *_: (0,) * len(shape), pipeline_mode=pl.Buffered(1))


def plain_device(
    images, keep_mask, ln1_gain, ln1_bias, w_qkv, bias_q, bias_v, w_proj, b_proj,
    ln2_gain, ln2_bias, w_fc1, b_fc1, w_fc2, b_fc2, cotangent,
):
    count, patches, width = images.shape
    slots = slots_of(patches)
    rows = count * slots
    heads = width // HEAD_DIM
    shard = w_fc1.shape[1]
    row = lambda v: v.reshape(1, -1)
    whole_w1 = lax.all_gather(w_fc1, "mlp")
    whole_w2 = lax.all_gather(w_fc2, "mlp")
    whole_b1 = lax.all_gather(b_fc1, "mlp").reshape(2, 1, shard)
    shape = jax.ShapeDtypeStruct
    limit = pltpu.CompilerParams(vmem_limit_bytes=60 * 2**20)
    per_image = lambda *tail: pl.BlockSpec((1,) + tail, lambda i: (i,) + (0,) * len(tail))
    per_rows = lambda cols: pl.BlockSpec((slots, cols), lambda i: (i, 0))
    sel, x, normed, qkv, probs, att, mid, hid, gm, sums = pl.pallas_call(
        functools.partial(forward_kernel, slots),
        grid=(count,),
        out_shape=(
            shape((count, slots, patches), BF16),
            shape((rows, width), BF16),
            shape((rows, width), BF16),
            shape((rows, 3 * width), BF16),
            shape((count, heads, slots, slots), BF16),
            shape((rows, width), BF16),
            shape((rows, width), F32),
            shape((rows, width), BF16),
            shape((rows, width), BF16),
            shape((count, 8, width), F32),
        ),
        in_specs=[
            whole((count, patches)), per_image(patches, width), per_image(patches, width),
            whole((width,)), whole((width,)), whole((width, 3 * width)), whole((width,)), whole((width,)),
            whole((width, width)), whole((width,)), whole((width,)), whole((width,)),
        ],
        out_specs=(
            per_image(slots, patches), per_rows(width), per_rows(width), per_rows(3 * width),
            per_image(heads, slots, slots), per_rows(width), per_rows(width), per_rows(width), per_rows(width),
            per_image(8, width),
        ),
        compiler_params=limit,
        name="attention_forward",
    )(
        keep_mask, images, cotangent, ln1_gain, ln1_bias, w_qkv, bias_q, bias_v, w_proj, b_proj, ln2_gain, ln2_bias,
    )
    chunk = 512 if shard % 512 == 0 else 256
    each = shard // chunk
    mlp_out, grad_hidden, dw1, dw2, db1 = pl.pallas_call(
        mlp_kernel,
        grid=(2 * each,),
        out_shape=(
            shape((rows, width), F32), shape((rows, width), F32),
            shape((2, width, shard), BF16), shape((2, shard, width), BF16), shape((2, 1, shard), F32),
        ),
        in_specs=[
            whole((rows, width)), whole((rows, width)),
            pl.BlockSpec((1, width, chunk), lambda c: (c // each, 0, c % each)),
            pl.BlockSpec((1, 1, chunk), lambda c: (c // each, 0, c % each)),
            pl.BlockSpec((1, chunk, width), lambda c: (c // each, c % each, 0)),
        ],
        out_specs=(
            whole((rows, width)), whole((rows, width)),
            pl.BlockSpec((1, width, chunk), lambda c: (c // each, 0, c % each)),
            pl.BlockSpec((1, chunk, width), lambda c: (c // each, c % each, 0)),
            pl.BlockSpec((1, 1, chunk), lambda c: (c // each, 0, c % each)),
        ),
        compiler_params=limit,
        name="mlp_both_ways",
    )(hid, gm, whole_w1, whole_b1, whole_w2)
    kept = jnp.sum(keep_mask, axis=1, keepdims=True)
    valid = (jnp.arange(slots, dtype=jnp.int32)[None, :] < kept).astype(F32).reshape(rows, 1)
    groups = 3
    span = width // groups
    low, put, dwp, dwq, vec = pl.pallas_call(
        functools.partial(backward_kernel, count, slots, groups),
        grid=(groups + 2,),
        out_shape=(
            shape((count, patches, width), BF16), shape((count, patches, width), F32),
            shape((width, width), BF16), shape((width, 3 * width), BF16), shape((16, width), F32),
        ),
        in_specs=[
            whole((count, slots, patches)), whole((rows, width)), whole((rows, width)), whole((rows, 3 * width)),
            whole((count, heads, slots, slots)), whole((rows, width)), whole((rows, width)), whole((rows, width)),
            whole((rows, width)), whole((rows, width)), whole((rows, 1)),
            whole((1, width)), whole((1, width)), whole((1, width)), whole((width, 3 * width)), whole((width, width)),
            pl.BlockSpec(memory_space=pl.ANY), pl.BlockSpec(memory_space=pl.ANY),
        ],
        out_specs=(
            whole((count, patches, width)), whole((count, patches, width)),
            whole((width, width)), whole((width, 3 * width)), whole((16, width)),
        ),
        scratch_shapes=[
            pltpu.VMEM((rows, width), F32), pltpu.VMEM((rows, width), BF16),
            pltpu.VMEM((rows, span), BF16), pltpu.VMEM((rows, span), BF16), pltpu.VMEM((rows, span), BF16),
            pltpu.VMEM((rows, width), F32),
        ],
        compiler_params=limit,
        name="attention_backward",
    )(
        sel, x, normed, qkv, probs, att, mid, gm, grad_hidden, mlp_out, valid,
        row(ln1_gain), row(ln2_gain), row(b_fc2), w_qkv, w_proj, images, cotangent,
    )
    kept_at = (keep_mask > 0)[:, :, None]
    layer_out = jnp.where(kept_at, low, images)
    grad_images = jnp.where(kept_at, put, cotangent.astype(F32))
    both = ("img", "mlp")
    place = lax.axis_index("mlp")
    dw1s = lax.psum_scatter(dw1.reshape(2 * width, shard), "mlp", scatter_dimension=0, tiled=True)
    dw2s = lax.psum_scatter(dw2.reshape(2 * shard, width), "mlp", scatter_dimension=0, tiled=True)
    s_w1, s_w2 = lax.psum((dw1s, dw2s), "img")
    s_wq, s_wp = lax.psum((dwq, dwp), both)
    vec, sums, s_b1 = lax.psum((vec, jnp.sum(sums, axis=0), db1.reshape(2, shard)), both)
    s_b1 = lax.dynamic_index_in_dim(s_b1, place, 0, keepdims=False)
    stream_sq, mlp_sq, attn_sq = jnp.sum(vec[8]), jnp.sum(vec[9]), jnp.sum(sums[0])
    root_means = jnp.sqrt(jnp.stack([stream_sq, attn_sq, mlp_sq]) / (sums[1, 0] * width))
    f = lambda v: v.astype(F32)
    return (
        layer_out, grad_images, vec[6], vec[7], f(s_wq), vec[4], vec[5], f(s_wp), vec[3], vec[0], vec[1],
        f(s_w1), s_b1, f(s_w2), vec[2], root_means,
    )


class Place:
    def __init__(self, deep, width):
        spot, self.core = lax.axis_index("img"), lax.axis_index("mlp")
        x, y, self.z = spot % 2, (spot // 2) % 2, spot // 4
        core = self.core
        self.bit1 = x * (1 - core) + y * core
        self.bit2 = y * (1 - core) + x * core
        step_x, step_y = 1 - 2 * x, 2 - 4 * y
        self.deep = deep
        self.other = {"mlp": 1 - core}
        self.peer1 = {"img": spot + step_x * (1 - core) + step_y * core}
        self.peer2 = {"img": spot + step_y * (1 - core) + step_x * core}
        self.peer_z = [{"img": ((self.z + k) % deep) * 4 + spot % 4} for k in range(1, deep)]
        self.half, self.quarter = width // 2, width // 4
        self.piece = width // 4 // deep
        self.half_at = self.bit1 * self.half
        self.half_off = (1 - self.bit1) * self.half
        self.quarter_at = self.half_at + self.bit2 * self.quarter
        self.quarter_off = self.half_at + (1 - self.bit2) * self.quarter

    def piece_at(self, z):
        return self.quarter_at + z * self.piece

    def everyone(self):
        return [self.other, self.peer1, self.peer2] + self.peer_z

    def greet(self):
        for peer in self.everyone():
            pl.semaphore_signal(pltpu.get_barrier_semaphore(), inc=1, device_id=peer, device_id_type=MESH)

    def all_here(self):
        pl.semaphore_wait(pltpu.get_barrier_semaphore(), len(self.everyone()))


def span(start, size):
    return pl.ds(pl.multiple_of(start, 16), size)


def remote(source, target, send_sem, recv_sem, peer):
    return pltpu.make_async_remote_copy(
        src_ref=source, dst_ref=target, send_sem=send_sem, recv_sem=recv_sem, device_id=peer, device_id_type=MESH
    )


def added(left, right):
    return (left.astype(F32) + right.astype(F32)).astype(BF16)


class Reduce:
    def __init__(self, place, partial, sending, total, got_core, got1, got2, got_z, send, recv, send_z, recv_z):
        self.place, self.partial, self.sending, self.total = place, partial, sending, total
        self.got_core, self.got1, self.got2, self.got_z = got_core, got1, got2, got_z
        self.send, self.recv, self.send_z, self.recv_z = send, recv, send_z, recv_z

    def copies(self, c, stage):
        p = self.place
        if stage == 0:
            return [remote(self.sending(c), self.got_core.at[c], self.send.at[c, 0], self.recv.at[c, 0], p.other)]
        total = self.total(c)
        if stage == 1:
            part = total.at[:, span(p.half_off, p.half), :]
            return [remote(part, self.got1.at[c], self.send.at[c, 1], self.recv.at[c, 1], p.peer1)]
        if stage == 2:
            part = total.at[:, span(p.quarter_off, p.quarter), :]
            return [remote(part, self.got2.at[c], self.send.at[c, 2], self.recv.at[c, 2], p.peer2)]
        made = []
        for k, peer in enumerate(p.peer_z):
            part = total.at[:, span(p.piece_at((p.z + k + 1) % p.deep), p.piece), :]
            made.append(remote(part, self.got_z.at[c, k], self.send_z.at[c, k], self.recv_z.at[c, k], peer))
        return made

    def begin(self, c, stage):
        for copy in self.copies(c, stage):
            copy.start()

    def arrive(self, c, stage):
        for copy in self.copies(c, stage):
            copy.wait_recv()

    def sent(self, c):
        for stage in range(4):
            for copy in self.copies(c, stage):
                copy.wait_send()

    def plane1(self, c):
        self.arrive(c, 0)
        total, partial, got = self.total(c), self.partial(c), self.got_core.at[c]
        total[...] = added(partial[...], got[...])
        self.begin(c, 1)

    def plane2(self, c):
        p = self.place
        self.arrive(c, 1)
        rows = span(p.half_at, p.half)
        total = self.total(c)
        total[:, rows, :] = added(total[:, rows, :], self.got1[c])
        self.begin(c, 2)

    def along_z(self, c):
        p = self.place
        self.arrive(c, 2)
        rows = span(p.quarter_at, p.quarter)
        total = self.total(c)
        total[:, rows, :] = added(total[:, rows, :], self.got2[c])
        self.begin(c, 3)

    def finish(self, c):
        p = self.place
        self.arrive(c, 3)
        rows = span(p.piece_at(p.z), p.piece)
        value = self.total(c)[:, rows, :].astype(F32)
        for k in range(p.deep - 1):
            value = value + self.got_z[c, k].astype(F32)
        return value.astype(BF16)


class Gather:
    def __init__(self, place, piece, result, mirror, local, send, recv, send_z, recv_z):
        self.place, self.piece, self.result, self.mirror, self.local = place, piece, result, mirror, local
        self.send, self.recv, self.send_z, self.recv_z = send, recv, send_z, recv_z

    def kept(self, c):
        p = self.place
        return pltpu.make_async_copy(
            self.piece(c), self.result(c).at[:, span(p.piece_at(p.z), p.piece), :], self.local.at[c]
        )

    def copies(self, c, stage, landing=False):
        p, result = self.place, self.result(c)
        if stage == 0:
            made = []
            for k, peer in enumerate(p.peer_z):
                z = (p.z - k - 1 + p.deep) % p.deep if landing else p.z
                target = result.at[:, span(p.piece_at(z), p.piece), :]
                made.append(remote(self.piece(c), target, self.send_z.at[c, k], self.recv_z.at[c, k], peer))
            return made
        if stage == 1:
            source = result.at[:, span(p.quarter_at, p.quarter), :]
            target = result.at[:, span(p.quarter_off if landing else p.quarter_at, p.quarter), :]
            return [remote(source, target, self.send.at[c, 0], self.recv.at[c, 0], p.peer2)]
        if stage == 2:
            source = result.at[:, span(p.half_at, p.half), :]
            target = result.at[:, span(p.half_off if landing else p.half_at, p.half), :]
            return [remote(source, target, self.send.at[c, 1], self.recv.at[c, 1], p.peer1)]
        return [remote(result, self.mirror(c) if landing else result, self.send.at[c, 2], self.recv.at[c, 2], p.other)]

    def begin(self, c, stage):
        for copy in self.copies(c, stage):
            copy.start()

    def arrive(self, c, stage):
        for copy in self.copies(c, stage, landing=True):
            copy.wait_recv()

    def along_z(self, c):
        self.kept(c).start()
        self.begin(c, 0)

    def plane2(self, c):
        self.kept(c).wait()
        self.arrive(c, 0)
        self.begin(c, 1)

    def plane1(self, c):
        self.arrive(c, 1)
        self.begin(c, 2)

    def across(self, c):
        self.arrive(c, 2)
        self.begin(c, 3)

    def sent(self, c):
        for stage in range(3 if self.mirror is None else 4):
            for copy in self.copies(c, stage):
                copy.wait_send()


def vec_slot(slot, width):
    return slice(slot // 2, slot // 2 + 1), slice(slot % 2 * width, slot % 2 * width + width)


def head_back(slots, i, q_ref, k_ref, v_ref, probs_ref, gatt_ref, gq_ref, gk_ref, gv_ref):
    first = lax.broadcasted_iota(jnp.int32, (1, 2 * HEAD_DIM), 1) < HEAD_DIM
    zero = jnp.zeros((), BF16)
    scale = jnp.asarray(HEAD_DIM ** -0.5, BF16)
    pairs = q_ref.shape[1] // 128
    here = pl.ds(pl.multiple_of(i * slots, 16), slots)
    for pair in range(pairs):
        own = slice(pair * 128, pair * 128 + 128)
        query, key, value = q_ref[here, own], k_ref[here, own], v_ref[here, own]
        grad_att = gatt_ref[here, own]
        gq = gk = gv = None
        for half in range(2):
            mine = first if half == 0 else jnp.logical_not(first)
            low = probs_ref[i, 2 * pair + half]
            probs = low.astype(F32)
            g_mine = jnp.where(mine, grad_att, zero)
            grad_probs = dot_t(g_mine, value).astype(BF16).astype(F32)
            inner = jnp.sum(probs * grad_probs, axis=1, keepdims=True)
            grad_scores = (probs * (grad_probs - inner)).astype(BF16) * scale
            tv = t_dot(low, g_mine)
            tq = dot(grad_scores, jnp.where(mine, key, zero))
            tk = t_dot(grad_scores, jnp.where(mine, query, zero))
            gq = tq if gq is None else gq + tq
            gk = tk if gk is None else gk + tk
            gv = tv if gv is None else gv + tv
        gq_ref[here, own] = gq.astype(BF16)
        gk_ref[here, own] = gk.astype(BF16)
        gv_ref[here, own] = gv.astype(BF16)


def mlp_staged_kernel(
    deep, images, slots, ticks,
    hid_ref, gm_ref, sums_ref, w1a_ref, w1b_ref, b1a_ref, b1b_ref, w2a_ref, w2b_ref, g2_ref, bfc2_ref,
    att_hbm, mid_hbm, sel_hbm, wproj_hbm, normed_hbm, qkv_hbm, probs_hbm, wqkv_hbm,
    red_ref, gmid_ref, gatt_ref, dwp_ref, lo_ref, vec_ref, early_ref, dwh_ref, gn_hbm,
    att_ref, mid_ref, sel_ref, wproj_ref, normed_ref, q_ref, k_ref, v_ref, probs_ref, wq_ref, wk_ref, wv_ref,
    gq_ref, gk_ref, gv_ref, fetch_sem,
    out_ref, gh_ref, bias_ref, give_ref, own_ref, got_core, got1, got2, got_z, send, recv, send_z, recv_z,
    b_local, b_send, b_recv, b_send_z, b_recv_z,
):
    step = pl.program_id(0)
    rows, width = hid_ref.shape
    place = Place(deep, width)
    panels = 4
    chunk = w1a_ref.shape[1]
    reduce = Reduce(
        place, lambda c: own_ref.at[c], lambda c: give_ref.at[c], lambda c: own_ref.at[c],
        got_core, got1, got2, got_z, send, recv, send_z, recv_z,
    )

    back = Gather(
        place, lambda c: red_ref.at[pl.ds(c * panels, panels)], lambda c: early_ref.at[pl.ds(c * panels, panels)],
        None, b_local, b_send, b_recv, b_send_z, b_recv_z,
    )
    early = early_ref.shape[0] // panels

    wide = q_ref.shape[1]
    thirds = [slice(part * width, part * width + wide) for part in range(3)]
    sources = [att_hbm, mid_hbm, sel_hbm, wproj_hbm, normed_hbm] + [qkv_hbm.at[:, cols] for cols in thirds]
    sources += [probs_hbm.at[:, 0 : probs_ref.shape[1]]] + [wqkv_hbm.at[:, cols] for cols in thirds]
    held = [att_ref, mid_ref, sel_ref, wproj_ref, normed_ref, q_ref, k_ref, v_ref, probs_ref, wq_ref, wk_ref, wv_ref]
    fetched = [
        pltpu.make_async_copy(source, target, fetch_sem.at[j]) for j, (source, target) in enumerate(zip(sources, held))
    ]

    def put_red(c):
        red_ref[pl.ds(c * panels, panels)] = reduce.finish(c)

    def half(w1_ref, b1, w2_ref, target, db_row):
        hid, gm = hid_ref[...], gm_ref[...]
        w1, w2 = w1_ref[...], w2_ref[...]
        pre = dot(hid, w1) + bias_ref[b1, pl.ds(step, 1)]
        act, slope = gelu_pair(pre)
        act = act.astype(BF16)
        grad_act = dot_t(gm, w2).astype(BF16).astype(F32)
        grad_pre = (grad_act * slope).astype(BF16)
        d2 = t_dot(act, gm).astype(BF16)
        for j in range(width // 128):
            at = j % 3 * chunk
            target[2 + j // 3, at : at + chunk, :] = d2[:, j * 128 : j * 128 + 128]
        d1 = t_dot(hid, grad_pre).astype(BF16)
        target[0] = d1[:, :128]
        target[1] = d1[:, 128:]
        cols = pl.ds(pl.multiple_of(step * chunk, chunk), chunk)
        vec_ref[pl.ds(db_row, 1), cols] = jnp.sum(grad_pre.astype(F32), axis=0, keepdims=True)
        out_ref[...] += dot(act, w2)
        gh_ref[...] += dot_t(grad_pre, w1)

    @pl.when(step == 0)
    def _():
        for copy in fetched:
            copy.start()
        place.greet()
        out_ref[...] = jnp.zeros_like(out_ref)
        gh_ref[...] = jnp.zeros_like(gh_ref)
        for side, ref in enumerate((b1a_ref, b1b_ref)):
            line = as_row(ref)
            for c in range(ticks):
                bias_ref[side, c : c + 1] = line[:, c * chunk : (c + 1) * chunk]
        place.all_here()

    @pl.when((step >= 1) & (step <= ticks))
    def _():
        reduce.plane1(step - 1)

    @pl.when(step == ticks)
    def _():
        back.plane1(0)

    @pl.when((step >= 2) & (step <= ticks))
    def _():
        reduce.plane2(step - 2)

    @pl.when((step >= 3) & (step <= ticks))
    def _():
        reduce.along_z(step - 3)

    @pl.when((step >= 4) & (step <= ticks))
    def _():
        put_red(step - 4)
        back.along_z(step - 4)

    @pl.when(step < ticks)
    def _():
        half(w1b_ref, 1, w2b_ref, give_ref.at[step], 7 - place.core)

    @pl.when(step == ticks - 1)
    def _():
        back.plane2(0)

    @pl.when(step < ticks)
    def _():
        reduce.begin(step, 0)
        half(w1a_ref, 0, w2a_ref, own_ref.at[step], 6 + place.core)

    def note(slot, value):
        at_row, at_col = vec_slot(slot, width)
        vec_ref[at_row, at_col] = value

    def column_sum(value):
        return jnp.sum(value, axis=0, keepdims=True)

    @pl.when(step == ticks)
    def _():
        for copy in fetched:
            copy.wait()
        stream = mlp_sq = jnp.zeros((1, width), F32)
        gain = shift = b_two = b_proj = jnp.zeros((1, width), F32)
        for i in range(images):
            here = slice(i * slots, i * slots + slots)
            sel = sel_ref[i]
            middle = mid_ref[here]
            valid = jnp.sum(sel.astype(F32), axis=1, keepdims=True) > 0
            mlp_out = jnp.where(valid, out_ref[here] + as_row(bfc2_ref), 0.0)
            block = middle + mlp_out
            kept = jnp.where(valid, block, 0.0)
            stream = stream + column_sum(kept * kept)
            mlp_sq = mlp_sq + column_sum(mlp_out * mlp_out)
            lo_ref[i] = t_dot(sel, block.astype(BF16)).astype(BF16)
            scaled, inverse = norm_rows(middle)
            grad_hidden = gh_ref[here]
            gain = gain + column_sum(grad_hidden * scaled)
            shift = shift + column_sum(grad_hidden)
            gm = gm_ref[here].astype(F32)
            b_two = b_two + column_sum(gm)
            grad_middle = gm + norm_back(grad_hidden * as_row(g2_ref), scaled, inverse)
            gmid_ref[here] = grad_middle
            grad_attn = grad_middle.astype(BF16)
            b_proj = b_proj + column_sum(grad_attn.astype(F32))
            gatt_ref[here] = grad_attn
            if i == 2:
                back.plane2(1)
        for slot, value in enumerate((gain, shift, b_two, b_proj)):
            note(slot, value)
        note(8, stream)
        note(9, mlp_sq)
        note(10, sum(sums_ref[i, 0:1] for i in range(images)))
        note(11, sum(sums_ref[i, 1:2] for i in range(images)))
        reduce.plane2(ticks - 1)
        reduce.along_z(ticks - 2)
        put_red(ticks - 3)
        back.plane1(1)
        back.plane2(2)
        grad_attn = gatt_ref[...]
        for part in range(3):
            cols = slice(part * width // 3, (part + 1) * width // 3)
            d = t_dot(att_ref[...], grad_attn[:, cols]).astype(BF16)
            dwp_ref[0, part] = d[:, :128]
            dwp_ref[1, part] = d[:, 128:]
        gatt_ref[...] = dot_t(grad_attn, wproj_ref[...]).astype(BF16)

        @pl.loop(0, images)
        def _(i):
            @pl.when(i == 2)
            def _():
                reduce.along_z(ticks - 1)
                back.plane1(2)

            @pl.when(i == 4)
            def _():
                put_red(ticks - 2)

            head_back(slots, i, q_ref, k_ref, v_ref, probs_ref, gatt_ref, gq_ref, gk_ref, gv_ref)

        vec_ref[2:3, 0:wide] = column_sum(gq_ref[...].astype(F32))
        vec_ref[2:3, width : width + wide] = column_sum(gv_ref[...].astype(F32))
        total = None
        for part, (ref, w_ref) in enumerate(((gq_ref, wq_ref), (gk_ref, wk_ref), (gv_ref, wv_ref))):
            d = t_dot(normed_ref[...], ref[...]).astype(BF16)
            dwh_ref[0, part] = d[:, :128]
            dwh_ref[1, part] = d[:, 128:]
            term = dot_t(ref[...], w_ref[...])
            total = term if total is None else total + term
        gh_ref[...] = total
        keep_gn = pltpu.make_async_copy(gh_ref, gn_hbm, fetch_sem.at[0])
        keep_gn.start()
        put_red(ticks - 1)
        keep_gn.wait()

        @pl.loop(0, ticks)
        def _(c):
            reduce.sent(c)

        @pl.loop(0, early)
        def _(c):
            back.arrive(c, 2)
            back.sent(c)


def attention_staged_kernel(
    deep, images, slots, groups, ticks,
    q_ref, k_ref, v_ref, probs_ref, gatt_ref, wq_ref, wk_ref, wv_ref, g1_ref, dwp_ref, dwh_ref, red_ref, vecin_ref,
    normed_hbm, x_hbm, gmid_hbm, sel_hbm, gn_hbm,
    mlp_ref, attn_ref, gi_ref, vec_ref,
    gq_ref, gk_ref, gv_ref, gn_ref, stage_ref, total_ref, piece_ref, got_core, got1, got2, got_z,
    vsum_ref, vgot_ref, vz_ref,
    send, recv, send_z, recv_z, m_local, m_send, m_recv, m_send_z, m_recv_z,
    a_local, a_send, a_recv, a_send_z, a_recv_z, v_send, v_recv, v_send_z, v_recv_z,
    normed_ref, x_ref, gmid_ref, sel_ref, fetch_sem,
):
    step = pl.program_id(0)
    rows, width = x_ref.shape
    fetched = [
        pltpu.make_async_copy(source, target, fetch_sem.at[j])
        for j, (source, target) in enumerate(
            ((normed_hbm, normed_ref), (gn_hbm, gn_ref), (x_hbm, x_ref), (gmid_hbm, gmid_ref), (sel_hbm, sel_ref))
        )
    ]
    place = Place(deep, width)
    core = place.core
    polls = images + 2

    def partial_of(owner):
        def pick(c):
            if isinstance(c, int) and c < 2:
                return (dwp_ref, dwh_ref)[c].at[owner]
            return stage_ref.at[c - 2, owner]

        return pick

    reduce = Reduce(
        place, partial_of(core), partial_of(1 - core), lambda c: total_ref.at[c],
        got_core, got1, got2, got_z, send, recv, send_z, recv_z,
    )
    back = Gather(
        place, lambda c: piece_ref.at[c], lambda c: attn_ref.at[core, pl.ds(3 * c, 3)],
        lambda c: attn_ref.at[1 - core, pl.ds(3 * c, 3)], a_local, a_send, a_recv, a_send_z, a_recv_z,
    )
    late = mlp_ref.shape[0] // 4
    mlp = Gather(
        place, lambda c: red_ref.at[pl.ds(4 * (ticks - late + c), 4)], lambda c: mlp_ref.at[pl.ds(4 * c, 4)], None,
        m_local, m_send, m_recv, m_send_z, m_recv_z,
    )

    def turn(c):
        piece_ref[c] = reduce.finish(c)
        back.along_z(c)

    def do(name, c):
        return {
            "X": reduce.plane1, "Y": reduce.plane2, "Z": reduce.along_z, "R": turn,
            "ay": back.plane2, "ax": back.plane1, "ac": back.across,
            "my": mlp.plane2, "mx": mlp.plane1,
        }[name](c - (ticks - late) if name[0] == "m" else c)

    plan = {}
    for at, name, c in (
        (2, "X", 0), (2, "X", 1), (6, "Y", 0), (8, "my", 3), (9, "X", 2), (9, "Y", 1), (10, "Z", 0), (12, "my", 5),
        (13, "mx", 3), (15, "Z", 1), (16, "Y", 2), (16, "X", 3), (16, "R", 0), (18, "my", 4),
    ):
        plan.setdefault(at, []).append((name, c))
    tail = (
        ("Z", 2), ("R", 1), ("ay", 0), ("mx", 5), ("Y", 3), ("R", 2), ("ax", 0), ("ay", 1), ("Z", 3), ("ay", 2),
        ("ax", 1), ("ac", 0), ("R", 3), ("mx", 4), ("ax", 2), ("ac", 1), ("ay", 3), ("ac", 2), ("ax", 3),
        ("ac", 3),
    )

    def run(at, now):
        for moment, jobs in sorted(plan.items()):
            if moment < groups * polls and at(moment % polls):

                @pl.when(now == moment)
                def _(jobs=jobs):
                    for name, c in jobs:
                        do(name, c)

    wide = width // (groups + 1)

    @pl.when(step == 0)
    def _():
        for copy in fetched:
            copy.start()
        place.greet()
        vsum_ref[0] = vecin_ref[...]
        place.all_here()
        reduce.begin(0, 0)
        reduce.begin(1, 0)
        for c in range(late):
            mlp.along_z(c)

    @pl.when(step < groups)
    def _():
        @pl.loop(0, images)
        def _(i):
            run(lambda at: at < images, step * polls + i)
            head_back(slots, i, q_ref, k_ref, v_ref, probs_ref, gatt_ref, gq_ref, gk_ref, gv_ref)

        run(lambda at: at == images, step * polls + images)

        @pl.when(step == 0)
        def _():
            for copy in fetched[:2]:
                copy.wait()

        cols = pl.ds(pl.multiple_of((step + 1) * wide, wide), wide)
        shifted = pl.ds(pl.multiple_of(width + (step + 1) * wide, wide), wide)
        vsum_ref[0, 2:3, cols] = jnp.sum(gq_ref[...].astype(F32), axis=0, keepdims=True)
        vsum_ref[0, 2:3, shifted] = jnp.sum(gv_ref[...].astype(F32), axis=0, keepdims=True)
        for part, ref in enumerate((gq_ref, gk_ref, gv_ref)):
            d = t_dot(normed_ref[...], ref[...]).astype(BF16)
            stage_ref[step, 0, part] = d[:, :128]
            stage_ref[step, 1, part] = d[:, 128:]
        reduce.begin(step + 2, 0)
        for ref, w_ref in ((gq_ref, wq_ref), (gk_ref, wk_ref), (gv_ref, wv_ref)):
            gn_ref[...] += dot_t(ref[...], w_ref[...])
        run(lambda at: at == images + 1, step * polls + images + 1)

    def vec_copies(stage):
        if stage < 3:
            peer = (place.other, place.peer1, place.peer2)[stage]
            return [remote(vsum_ref.at[stage], vgot_ref.at[stage], v_send.at[stage], v_recv.at[stage], peer)]
        return [
            remote(vsum_ref.at[3], vz_ref.at[k], v_send_z.at[k], v_recv_z.at[k], peer)
            for k, peer in enumerate(place.peer_z)
        ]

    def vec_begin(stage):
        for copy in vec_copies(stage):
            copy.start()

    def vec_next(stage):
        for copy in vec_copies(stage):
            copy.wait_recv()
        if stage < 3:
            vsum_ref[stage + 1] = vsum_ref[stage] + vgot_ref[stage]
            vec_begin(stage + 1)

    @pl.when(step == groups)
    def _():
        for copy in fetched[2:]:
            copy.wait()
        g1 = as_row(g1_ref)
        gain = shift = jnp.zeros((1, width), F32)
        for i in range(images):
            for name, c in plan.get(groups * polls + i, ()):
                do(name, c)
            here = slice(i * slots, i * slots + slots)
            sel = sel_ref[i]
            scaled, inverse = norm_rows(x_ref[here].astype(F32))
            grad_normed = gn_ref[here]
            gain = gain + jnp.sum(grad_normed * scaled, axis=0, keepdims=True)
            shift = shift + jnp.sum(grad_normed, axis=0, keepdims=True)
            change = gmid_ref[here] + norm_back(grad_normed * g1, scaled, inverse)
            high = change.astype(BF16)
            rest = (change - high.astype(F32)).astype(BF16)
            gi_ref[i] = t_dot(sel, high) + t_dot(sel, rest)
        at_row, at_col = vec_slot(6, width)
        vsum_ref[0, at_row, at_col] = gain
        at_row, at_col = vec_slot(7, width)
        vsum_ref[0, at_row, at_col] = shift
        vec_begin(0)
        for at, (name, c) in enumerate(tail):
            do(name, c)
            if at % 3 == 2 and at // 3 < 4:
                vec_next(at // 3)
        value = None
        for z in range(deep):
            mine = vsum_ref[3]
            from_k = [vz_ref[k] for k in range(deep - 1)]
            term = mine
            for k in range(deep - 1):
                term = jnp.where((place.z - k - 1 + deep) % deep == z, from_k[k], term)
            value = term if value is None else value + term
        vec_ref[...] = value
        for c in range(late):
            mlp.arrive(c, 2)
            mlp.sent(c)
        for c in range(groups + 2):
            back.arrive(c, 3)
            back.sent(c)
            reduce.sent(c)
        for stage in range(4):
            for copy in vec_copies(stage):
                copy.wait_send()


def finish_kernel(
    groups, early,
    first_ref, second_ref, attn_ref, low_ref, put_ref, img_ref, cot_ref, keep_ref, vec_ref,
    lo_ref, gi_ref, wq_ref, wp_ref, w1_ref, w2_ref, b1_ref, root_ref, *small_refs,
):
    step = pl.program_id(0)
    width = low_ref.shape[2]
    chunk = w1_ref.shape[1]
    for big_ref, mine in ((first_ref, step < early), (second_ref, step >= early)):

        @pl.when(mine)
        def _(big_ref=big_ref):
            for j in range(chunk // 128):
                w1_ref[:, j * 128 : j * 128 + 128] = big_ref[j].astype(F32)
            for j in range(width // 128):
                at = j % 3 * chunk
                w2_ref[:, j * 128 : j * 128 + 128] = big_ref[2 + j // 3, at : at + chunk].astype(F32)

    for owner in range(2):
        for j in range(3):
            at = (2 * j + owner) * 128
            wp_ref[:, at : at + 128] = attn_ref[owner, j].astype(F32)
            for group in range(groups):
                at = j * width + (2 * group + owner) * 128
                wq_ref[:, at : at + 128] = attn_ref[owner, 3 + 3 * group + j].astype(F32)

    @pl.when(step < keep_ref.shape[0])
    def _():
        keep = keep_ref[pl.ds(step, 1)].astype(F32)
        eight = jnp.broadcast_to(keep, (8, keep.shape[1])).astype(BF16)
        once = jnp.where(lax.broadcasted_iota(jnp.int32, (8, 128), 0) == 0, 1.0, 0.0).astype(BF16)
        kept = t_dot(eight, once)[:, 0:1] > 0.5
        lo_ref[0] = jnp.where(kept, low_ref[0], img_ref[0])
        gi_ref[0] = jnp.where(kept, put_ref[0], cot_ref[0].astype(F32))

    @pl.when(step == 0)
    def _():
        def line(slot):
            at_row, at_col = vec_slot(slot, width)
            return vec_ref[at_row, at_col]

        for slot, ref in enumerate(small_refs):
            ref[...] = line(slot).reshape(width)
        b1_ref[...] = vec_ref[pl.ds(6 + lax.axis_index("mlp"), 1)].reshape(2 * width)
        count = line(11)[:, 0:1]
        lane = lax.broadcasted_iota(jnp.int32, (1, 128), 1)
        sums = jnp.where(lane == 0, jnp.sum(line(8)), jnp.where(lane == 1, jnp.sum(line(10)), jnp.sum(line(9))))
        root_ref[...] = jnp.sqrt(sums / (count * width)).reshape(128)[:3]


def staged_device(
    deep, images, keep_mask, ln1_gain, ln1_bias, w_qkv, bias_q, bias_v, w_proj, b_proj,
    ln2_gain, ln2_bias, w_fc1, b_fc1, w_fc2, b_fc2, cotangent,
):
    count, patches, width = images.shape
    slots = slots_of(patches)
    rows = count * slots
    heads = width // HEAD_DIM
    shard = w_fc1.shape[1]
    row = lambda v: v.reshape(1, -1)
    shape = jax.ShapeDtypeStruct
    limit = 62 * 2**20
    any_space = pl.BlockSpec(memory_space=pl.ANY)
    per_image = lambda *tail: pl.BlockSpec((1,) + tail, lambda i: (i,) + (0,) * len(tail))
    per_rows = lambda cols: pl.BlockSpec((slots, cols), lambda i: (i, 0))
    dma = pltpu.SemaphoreType.DMA
    vmem = pltpu.VMEM
    stored = (
        shape((count, slots, patches), BF16), shape((rows, width), BF16), shape((rows, width), BF16),
        shape((rows, 3 * width), BF16), shape((count, heads, slots, slots), BF16), shape((rows, width), BF16),
        shape((rows, width), F32), shape((rows, width), BF16), shape((rows, width), BF16),
    )
    sums, sel, x, normed, qkv, probs, att, mid, hid, gm, far_w1, far_b1, far_w2 = pl.pallas_call(
        functools.partial(forward_staged_kernel, slots),
        grid=(1,),
        out_shape=(shape((count, 8, width), F32),) + stored + (
            shape((width, shard), BF16), shape((shard,), BF16), shape((shard, width), BF16),
        ),
        in_specs=[
            whole((count, patches)),
        ] + 7 * [whole((width,))] + 7 * [any_space],
        out_specs=(whole((count, 8, width)),) + 12 * (any_space,),
        scratch_shapes=[
            vmem((count, patches, width), BF16), vmem((count, patches, width), BF16),
            vmem((width, 3 * width), BF16), vmem((width, width), BF16),
        ]
        + [vmem(s.shape, s.dtype) for s in stored]
        + [dma((count, 2)), dma((2,)), dma((6,)), dma((count,)), dma((count, 2)), dma((3,)), dma((3,))],
        compiler_params=pltpu.CompilerParams(vmem_limit_bytes=limit, collective_id=0, has_side_effects=True),
        name="attention_forward",
    )(
        keep_mask, ln1_gain, ln1_bias, bias_q, bias_v, b_proj, ln2_gain, ln2_bias,
        images, cotangent, w_qkv, w_proj, w_fc1, b_fc1, w_fc2,
    )
    chunk = 256
    ticks = shard // chunk
    groups = 3
    piece = width // 4 // deep
    by_cols = lambda *lead: pl.BlockSpec(lead + (chunk,), lambda c: (0, c - c // ticks))
    by_rows = pl.BlockSpec((chunk, width), lambda c: (c - c // ticks, 0))
    early = ticks // 2
    wide = width // groups
    red, gmid, gatt, dwp, low, vec, first, dwh, gn = pl.pallas_call(
        functools.partial(mlp_staged_kernel, deep, count, slots, ticks),
        grid=(ticks + 1,),
        out_shape=(
            shape((4 * ticks, piece, 128), BF16), shape((rows, width), F32), shape((rows, width), BF16),
            shape((2, 3, width, 128), BF16), shape((count, patches, width), BF16), shape((8, 2 * width), F32),
            shape((4 * early, width, 128), BF16), shape((2, 3, width, 128), BF16), shape((rows, width), F32),
        ),
        in_specs=[
            whole((rows, width)), whole((rows, width)), whole((count, 8, width)),
            by_cols(width), by_cols(width), whole((shard,)), whole((shard,)), by_rows, by_rows,
            whole((width,)), whole((width,)),
        ] + 8 * [any_space],
        out_specs=(
            whole((4 * ticks, piece, 128)), whole((rows, width)), whole((rows, width)),
            whole((2, 3, width, 128)), whole((count, patches, width)), whole((8, 2 * width)), any_space,
            whole((2, 3, width, 128)), any_space,
        ),
        scratch_shapes=[
            pltpu.VMEM((rows, width), BF16), pltpu.VMEM((rows, width), F32), pltpu.VMEM((count, slots, patches), BF16),
            pltpu.VMEM((width, width), BF16), pltpu.VMEM((rows, width), BF16),
            pltpu.VMEM((rows, wide), BF16), pltpu.VMEM((rows, wide), BF16), pltpu.VMEM((rows, wide), BF16),
            pltpu.VMEM((count, heads // groups, slots, slots), BF16),
            pltpu.VMEM((width, wide), BF16), pltpu.VMEM((width, wide), BF16), pltpu.VMEM((width, wide), BF16),
            pltpu.VMEM((rows, wide), BF16), pltpu.VMEM((rows, wide), BF16), pltpu.VMEM((rows, wide), BF16), dma((12,)),
            pltpu.VMEM((rows, width), F32), pltpu.VMEM((rows, width), F32), pltpu.VMEM((2, 8, chunk), F32),
            pltpu.VMEM((ticks, 4, width, 128), BF16), pltpu.VMEM((ticks, 4, width, 128), BF16),
            pltpu.VMEM((ticks, 4, width, 128), BF16), pltpu.VMEM((ticks, 4, width // 2, 128), BF16),
            pltpu.VMEM((ticks, 4, width // 4, 128), BF16), pltpu.VMEM((ticks, deep - 1, 4, piece, 128), BF16),
            dma((ticks, 3)), dma((ticks, 3)), dma((ticks, deep - 1)), dma((ticks, deep - 1)),
            dma((early,)), dma((early, 2)), dma((early, 2)), dma((early, deep - 1)), dma((early, deep - 1)),
        ],
        compiler_params=pltpu.CompilerParams(vmem_limit_bytes=limit, collective_id=1, has_side_effects=True),
        name="mlp_both_ways",
    )(
        hid, gm, sums, w_fc1, far_w1, b_fc1, far_b1, w_fc2, far_w2, ln2_gain, b_fc2,
        att, mid, sel, w_proj, normed, qkv, probs, w_qkv,
    )
    chunks = groups + 1
    left = groups - 1
    now = lambda g: 1 + g - g // left
    third = lambda lead, part: pl.BlockSpec((lead, wide), lambda g: (0, part * groups + now(g)))
    late = ticks - early
    second, attn, put, vec = pl.pallas_call(
        functools.partial(attention_staged_kernel, deep, count, slots, left, ticks),
        grid=(left + 1,),
        out_shape=(
            shape((4 * late, width, 128), BF16), shape((2, 3 * chunks, width, 128), BF16),
            shape((count, patches, width), F32), shape((8, 2 * width), F32),
        ),
        in_specs=[
            third(rows, 0), third(rows, 1), third(rows, 2),
            pl.BlockSpec((count, heads // groups, slots, slots), lambda g: (0, now(g), 0, 0)),
            third(rows, 0), third(width, 0), third(width, 1), third(width, 2),
            whole((width,)), whole((2, 3, width, 128)), whole((2, 3, width, 128)), whole((4 * ticks, piece, 128)),
            whole((8, 2 * width)),
        ] + 5 * [any_space],
        out_specs=(any_space, any_space, whole((count, patches, width)), whole((8, 2 * width))),
        scratch_shapes=[
            pltpu.VMEM((rows, wide), BF16), pltpu.VMEM((rows, wide), BF16), pltpu.VMEM((rows, wide), BF16),
            pltpu.VMEM((rows, width), F32),
            pltpu.VMEM((left, 2, 3, width, 128), BF16), pltpu.VMEM((chunks, 3, width, 128), BF16),
            pltpu.VMEM((chunks, 3, piece, 128), BF16), pltpu.VMEM((chunks, 3, width, 128), BF16),
            pltpu.VMEM((chunks, 3, width // 2, 128), BF16), pltpu.VMEM((chunks, 3, width // 4, 128), BF16),
            pltpu.VMEM((chunks, deep - 1, 3, piece, 128), BF16),
            pltpu.VMEM((4, 8, 2 * width), F32), pltpu.VMEM((3, 8, 2 * width), F32),
            pltpu.VMEM((deep - 1, 8, 2 * width), F32),
            dma((chunks, 3)), dma((chunks, 3)), dma((chunks, deep - 1)), dma((chunks, deep - 1)),
            dma((late,)), dma((late, 2)), dma((late, 2)), dma((late, deep - 1)), dma((late, deep - 1)),
            dma((chunks,)), dma((chunks, 3)), dma((chunks, 3)), dma((chunks, deep - 1)), dma((chunks, deep - 1)),
            dma((3,)), dma((3,)), dma((deep - 1,)), dma((deep - 1,)),
            pltpu.VMEM((rows, width), BF16), pltpu.VMEM((rows, width), BF16), pltpu.VMEM((rows, width), F32),
            pltpu.VMEM((count, slots, patches), BF16), dma((5,)),
        ],
        compiler_params=pltpu.CompilerParams(vmem_limit_bytes=limit, collective_id=2, has_side_effects=True),
        name="attention_backward",
    )(
        qkv, qkv, qkv, probs, gatt, w_qkv, w_qkv, w_qkv, ln1_gain, dwp, dwh, red, vec, normed, x, gmid, sel, gn,
    )
    deal = width // ticks
    turn = lambda t: (t - t // count, 0, 0)
    layer_out, grad_images, s_wq, s_wp, s_w1, s_w2, s_b1, root_means, *small = pl.pallas_call(
        functools.partial(finish_kernel, groups, early),
        grid=(ticks,),
        out_shape=(
            shape((count, patches, width), BF16), shape((count, patches, width), F32),
            shape((width, 3 * width), F32), shape((width, width), F32), shape((width, shard), F32),
            shape((shard, width), F32), shape((shard,), F32), shape((3,), F32),
        ) + 8 * (shape((width,), F32),),
        in_specs=[
            pl.BlockSpec((4, width, 128), lambda t: (jnp.minimum(t, early - 1), 0, 0)),
            pl.BlockSpec((4, width, 128), lambda t: (jnp.maximum(t - early, 0), 0, 0)),
            pl.BlockSpec((2, 3 * chunks, deal, 128), lambda t: (0, 0, t, 0)),
            pl.BlockSpec((1, patches, width), turn), pl.BlockSpec((1, patches, width), turn),
            pl.BlockSpec((1, patches, width), turn), pl.BlockSpec((1, patches, width), turn),
            whole((count, patches)), whole((8, 2 * width)),
        ],
        out_specs=(
            pl.BlockSpec((1, patches, width), turn), pl.BlockSpec((1, patches, width), turn),
            pl.BlockSpec((deal, 3 * width), lambda t: (t, 0)), pl.BlockSpec((deal, width), lambda t: (t, 0)),
            pl.BlockSpec((width, chunk), lambda t: (0, t)), pl.BlockSpec((chunk, width), lambda t: (t, 0)),
            whole((shard,)), whole((3,)),
        ) + 8 * (whole((width,)),),
        compiler_params=pltpu.CompilerParams(vmem_limit_bytes=limit),
        name="results",
    )(first, second, attn, low, put, images, cotangent, keep_mask, vec)
    gain2, shift2, b_two, b_project, b_query, b_value, gain1, shift1 = small
    return (
        layer_out, grad_images, gain1, shift1, s_wq, b_query, b_value, s_wp, b_project, gain2, shift2,
        s_w1, s_b1, s_w2, b_two, root_means,
    )


def solution(mesh):
    rows, line = P(("img", "mlp"), None, None), P(("img", "mlp"), None)
    deep = mesh.shape["img"] // 4
    staged = mesh.shape["img"] == 4 * deep and mesh.shape["mlp"] == 2 and 1 < deep <= 4
    return jax.shard_map(
        functools.partial(staged_device, deep) if staged else plain_device,
        mesh=mesh,
        in_specs=(
            rows, line, P(), P(), P(), P(), P(), P(), P(), P(), P(),
            P(None, "mlp"), P("mlp"), P("mlp", None), P(), rows,
        ),
        out_specs=(
            rows, rows, P(), P(), P(), P(), P(), P(), P(), P(), P(),
            P(None, "mlp"), P("mlp"), P("mlp", None), P(), P(),
        ),
        check_vma=False,
    )
```

```python
import functools

import jax
import jax.numpy as jnp
from jax import lax
from jax.experimental import pallas as pl
from jax.experimental.pallas import tpu as pltpu
from jax.sharding import PartitionSpec as P

HEAD_DIM = 64
NORM_EPS = 1e-06
F32 = jnp.float32
BF16 = jnp.bfloat16
MESH = pl.DeviceIdType.MESH
ERFC_POLY = (
    -0.05792342897865154,
    0.27982426175045266,
    -0.47905523971588865,
    0.27061712140601424,
    -0.022718349995155727,
    0.2015184791612061,
    0.24328701077158832,
    0.2823637910445855,
    0.2820864086305586,
)


def dot(a, b):
    return jnp.dot(a, b, preferred_element_type=F32)


def dot_t(a, b):
    return lax.dot_general(a, b, (((1,), (1,)), ((), ())), preferred_element_type=F32)


def t_dot(a, b):
    return lax.dot_general(a, b, (((0,), (0,)), ((), ())), preferred_element_type=F32)


def slots_of(patches):
    most = 4 * patches // 5
    return -(-most // 16) * 16


def norm_rows(rows):
    center = rows - jnp.mean(rows, axis=1, keepdims=True)
    inverse = lax.rsqrt(jnp.mean(center * center, axis=1, keepdims=True) + NORM_EPS)
    return center * inverse, inverse


def norm_back(weighted, scaled, inverse):
    return inverse * (
        weighted
        - jnp.mean(weighted, axis=1, keepdims=True)
        - scaled * jnp.mean(weighted * scaled, axis=1, keepdims=True)
    )


def gelu_pair(values):
    reach = jnp.abs(values) * 0.7071067811865476
    inv = 1.0 / (1.0 + 0.5 * reach)
    decay = jnp.exp(-0.5 * (values * values))
    poly = jnp.full_like(values, ERFC_POLY[0])
    for coefficient in ERFC_POLY[1:]:
        poly = poly * inv + coefficient
    tail = (0.5 * inv) * poly * decay
    share = jnp.where(values > 0, 1.0 - tail, tail)
    return values * share, share + values * (decay * 0.3989422804014327)


def swap_weights(ours, theirs, send_sem, recv_sem):
    other = {"mlp": 1 - lax.axis_index("mlp")}
    copies = [
        pltpu.make_async_remote_copy(
            src_ref=ours[j], dst_ref=theirs[j], send_sem=send_sem.at[j], recv_sem=recv_sem.at[j],
            device_id=other, device_id_type=MESH,
        )
        for j in range(len(ours))
    ]

    def trade(begin):
        @pl.when(pl.program_id(0) == (0 if begin else pl.num_programs(0) - 1))
        def _():
            if begin:
                barrier = pltpu.get_barrier_semaphore()
                pl.semaphore_signal(barrier, inc=1, device_id=other, device_id_type=MESH)
                pl.semaphore_wait(barrier, 1)
            for copy in copies:
                if begin:
                    copy.start()
                else:
                    copy.wait()

    return trade


def as_row(ref):
    return ref[...].astype(F32).reshape(1, -1)


def forward_kernel(
    slots,
    keep_ref, img_ref, cot_ref, g1_ref, b1_ref, wqkv_ref, bq_ref, bv_ref, wproj_ref, bproj_ref, g2_ref, b2_ref,
    sel_ref, x_ref, normed_ref, qkv_ref, probs_ref, att_ref, mid_ref, hid_ref, gm_ref, sums_ref,
):
    patches, width = img_ref.shape[1:]
    heads = width // HEAD_DIM
    keep = keep_ref[pl.ds(pl.program_id(0), 1)].astype(F32)
    upto = lax.broadcasted_iota(jnp.int32, (patches, patches), 0) <= lax.broadcasted_iota(
        jnp.int32, (patches, patches), 1
    )
    keep8 = jnp.broadcast_to(keep, (8, patches)).astype(BF16)
    rank = dot(keep8, upto.astype(F32).astype(BF16))[0:1]
    count = jnp.sum(keep, axis=1, keepdims=True)
    slot = lax.broadcasted_iota(jnp.int32, (slots, patches), 0).astype(F32)
    sel = jnp.where((slot == rank - 1.0) & (keep > 0), 1.0, 0.0).astype(BF16)
    sel_ref[0] = sel
    gm_ref[...] = dot(sel, cot_ref[0]).astype(BF16)
    rows = dot(sel, img_ref[0])
    x_ref[...] = rows.astype(BF16)
    scaled, _ = norm_rows(rows)
    normed = (scaled * as_row(g1_ref) + as_row(b1_ref)).astype(BF16)
    normed_ref[...] = normed
    for part in range(3):
        cols = slice(part * width, (part + 1) * width)
        block = dot(normed, wqkv_ref[:, cols])
        if part == 0:
            block = block + as_row(bq_ref)
        if part == 2:
            block = block + as_row(bv_ref)
        qkv_ref[:, cols] = block.astype(BF16)
    closed = jnp.where(
        lax.broadcasted_iota(jnp.int32, (1, slots), 1).astype(F32) < count, 0.0, -1e30
    )
    first = lax.broadcasted_iota(jnp.int32, (1, 2 * HEAD_DIM), 1) < HEAD_DIM
    zero = jnp.zeros((), BF16)
    for pair in range(heads // 2):
        lanes = slice(pair * 128, pair * 128 + 128)
        query = qkv_ref[:, lanes] * jnp.asarray(HEAD_DIM ** -0.5, BF16)
        key = qkv_ref[:, width + pair * 128 : width + pair * 128 + 128]
        value = qkv_ref[:, 2 * width + pair * 128 : 2 * width + pair * 128 + 128]
        total = None
        for half in range(2):
            mine = first if half == 0 else jnp.logical_not(first)
            scores = dot_t(query, jnp.where(mine, key, zero)) + closed
            raised = jnp.exp(scores - jnp.max(scores, axis=1, keepdims=True))
            probs = (raised * (1.0 / jnp.sum(raised, axis=1, keepdims=True))).astype(BF16)
            probs_ref[0, 2 * pair + half] = probs
            term = dot(probs, jnp.where(mine, value, zero))
            total = term if total is None else total + term
        att_ref[:, lanes] = total.astype(BF16)
    attn_out = dot(att_ref[...], wproj_ref[...]) + as_row(bproj_ref)
    valid = lax.broadcasted_iota(jnp.int32, (slots, 1), 0).astype(F32) < count
    attn_kept = jnp.where(valid, attn_out, 0.0)
    middle = rows + attn_kept
    mid_ref[...] = middle
    sums_ref[0, 0:1] = jnp.sum(attn_kept * attn_kept, axis=0, keepdims=True)
    sums_ref[0, 1:2] = jnp.broadcast_to(count, (1, width))
    scaled, _ = norm_rows(middle)
    hid_ref[...] = (scaled * as_row(g2_ref) + as_row(b2_ref)).astype(BF16)


def forward_staged_kernel(
    slots,
    keep_ref, g1_ref, b1_ref, bq_ref, bv_ref, bproj_ref, g2_ref, b2_ref,
    img_hbm, cot_hbm, wqkv_hbm, wproj_hbm, w1_hbm, bias1_hbm, w2_hbm,
    sums_ref, sel_hbm, x_hbm, normed_hbm, qkv_hbm, probs_hbm, att_hbm, mid_hbm, hid_hbm, gm_hbm,
    far_w1, far_bias1, far_w2,
    img_ref, cot_ref,
    wqkv_ref, wproj_ref, sel_ref, x_ref, normed_ref, qkv_ref, probs_ref, att_ref, mid_ref, hid_ref, gm_ref,
    row_sem, in_sem, out_sem, probs_sem, part_sem, send_sem, recv_sem,
):
    images, patches, width = img_ref.shape
    heads = width // HEAD_DIM
    fetched = [
        pltpu.make_async_copy(wqkv_hbm, wqkv_ref, in_sem.at[0]), pltpu.make_async_copy(wproj_hbm, wproj_ref, in_sem.at[1])
    ]

    def row_copies(i):
        return [
            pltpu.make_async_copy(img_hbm.at[i], img_ref.at[i], row_sem.at[i, 0]),
            pltpu.make_async_copy(cot_hbm.at[i], cot_ref.at[i], row_sem.at[i, 1]),
        ]

    for i in range(images):
        for copy in row_copies(i):
            copy.start()
    for copy in fetched:
        copy.start()
    trade = swap_weights((w1_hbm, bias1_hbm, w2_hbm), (far_w1, far_bias1, far_w2), send_sem, recv_sem)
    trade(True)
    upto = lax.broadcasted_iota(jnp.int32, (patches, patches), 0) <= lax.broadcasted_iota(
        jnp.int32, (patches, patches), 1
    )
    upto = upto.astype(F32).astype(BF16)
    slot = lax.broadcasted_iota(jnp.int32, (slots, patches), 0).astype(F32)
    g1, b1, g2, b2 = (as_row(ref) for ref in (g1_ref, b1_ref, g2_ref, b2_ref))

    def rows_of(i):
        return pl.ds(pl.multiple_of(i * slots, 16), slots)

    def count_of(i):
        return jnp.sum(keep_ref[pl.ds(i, 1)].astype(F32), axis=1, keepdims=True)

    @pl.loop(0, images)
    def _(i):
        for copy in row_copies(i):
            copy.wait()
        here = rows_of(i)
        keep = keep_ref[pl.ds(i, 1)].astype(F32)
        keep8 = jnp.broadcast_to(keep, (8, patches)).astype(BF16)
        rank = dot(keep8, upto)[0:1]
        sel = jnp.where((slot == rank - 1.0) & (keep > 0), 1.0, 0.0).astype(BF16)
        sel_ref[i] = sel
        gm_ref[here] = dot(sel, cot_ref[i]).astype(BF16)
        rows = dot(sel, img_ref[i])
        x_ref[here] = rows.astype(BF16)
        scaled, _ = norm_rows(rows)
        normed_ref[here] = (scaled * g1 + b1).astype(BF16)

    sent = [
        pltpu.make_async_copy(source, target, out_sem.at[j])
        for j, (source, target) in enumerate(
            (
                (sel_ref, sel_hbm), (x_ref, x_hbm), (normed_ref, normed_hbm), (gm_ref, gm_hbm), (qkv_ref, qkv_hbm),
                (att_ref, att_hbm),
            )
        )
    ]
    for copy in sent[:4]:
        copy.start()
    fetched[0].wait()
    wide = width // 3
    for j in range(9):
        cols = slice(j * wide, j * wide + wide)
        block = dot(normed_ref[...], wqkv_ref[:, cols])
        own = slice(j % 3 * wide, j % 3 * wide + wide)
        if j < 3:
            block = block + as_row(bq_ref)[:, own]
        if j >= 6:
            block = block + as_row(bv_ref)[:, own]
        qkv_ref[:, cols] = block.astype(BF16)
    sent[4].start()
    first = lax.broadcasted_iota(jnp.int32, (1, 2 * HEAD_DIM), 1) < HEAD_DIM
    zero = jnp.zeros((), BF16)

    def probs_copy(i):
        return pltpu.make_async_copy(probs_ref.at[i], probs_hbm.at[i], probs_sem.at[i])

    @pl.loop(0, images)
    def _(i):
        here = rows_of(i)
        closed = jnp.where(
            lax.broadcasted_iota(jnp.int32, (1, slots), 1).astype(F32) < count_of(i), 0.0, -1e30
        )
        for pair in range(heads // 2):
            lanes = slice(pair * 128, pair * 128 + 128)
            query = qkv_ref[here, lanes] * jnp.asarray(HEAD_DIM ** -0.5, BF16)
            key = qkv_ref[here, width + pair * 128 : width + pair * 128 + 128]
            value = qkv_ref[here, 2 * width + pair * 128 : 2 * width + pair * 128 + 128]
            total = None
            for half in range(2):
                mine = first if half == 0 else jnp.logical_not(first)
                scores = dot_t(query, jnp.where(mine, key, zero)) + closed
                raised = jnp.exp(scores - jnp.max(scores, axis=1, keepdims=True))
                probs = (raised * (1.0 / jnp.sum(raised, axis=1, keepdims=True))).astype(BF16)
                probs_ref[i, 2 * pair + half] = probs
                term = dot(probs, jnp.where(mine, value, zero))
                total = term if total is None else total + term
            att_ref[here, lanes] = total.astype(BF16)
        probs_copy(i).start()

    sent[5].start()
    fetched[1].wait()
    mid_ref[...] = dot(att_ref[...], wproj_ref[...]) + as_row(bproj_ref)

    def part_copies(i):
        here = rows_of(i)
        return [
            pltpu.make_async_copy(mid_ref.at[here], mid_hbm.at[here], part_sem.at[i, 0]),
            pltpu.make_async_copy(hid_ref.at[here], hid_hbm.at[here], part_sem.at[i, 1]),
        ]

    @pl.loop(0, images)
    def _(i):
        here = rows_of(i)
        count = count_of(i)
        valid = lax.broadcasted_iota(jnp.int32, (slots, 1), 0).astype(F32) < count
        attn_kept = jnp.where(valid, mid_ref[here], 0.0)
        middle = x_ref[here].astype(F32) + attn_kept
        mid_ref[here] = middle
        sums_ref[i, 0:1] = jnp.sum(attn_kept * attn_kept, axis=0, keepdims=True)
        sums_ref[i, 1:2] = jnp.broadcast_to(count, (1, width))
        scaled, _ = norm_rows(middle)
        hid_ref[here] = (scaled * g2 + b2).astype(BF16)
        for copy in part_copies(i):
            copy.start()

    for copy in sent:
        copy.wait()

    @pl.loop(0, images)
    def _(i):
        probs_copy(i).wait()
        for copy in part_copies(i):
            copy.wait()

    trade(False)


def mlp_kernel(hid_ref, gm_ref, w1_ref, b1_ref, w2_ref, out_ref, gh_ref, dw1_ref, dw2_ref, db1_ref):
    step = pl.program_id(0)
    hid, gm = hid_ref[...], gm_ref[...]
    w1, w2 = w1_ref[0], w2_ref[0]
    pre = dot(hid, w1) + b1_ref[0].astype(F32)
    act, slope = gelu_pair(pre)
    act = act.astype(BF16)
    grad_act = dot_t(gm, w2).astype(BF16).astype(F32)
    grad_pre_f = grad_act * slope
    grad_pre = grad_pre_f.astype(BF16)
    dw2_ref[0] = t_dot(act, gm).astype(BF16)
    dw1_ref[0] = t_dot(hid, grad_pre).astype(BF16)
    db1_ref[0] = jnp.sum(grad_pre.astype(F32), axis=0, keepdims=True)

    @pl.when(step == 0)
    def _():
        out_ref[...] = dot(act, w2)
        gh_ref[...] = dot_t(grad_pre, w1)

    @pl.when(step > 0)
    def _():
        out_ref[...] += dot(act, w2)
        gh_ref[...] += dot_t(grad_pre, w1)


def backward_kernel(
    images, slots, groups,
    sel_ref, x_ref, normed_ref, qkv_ref, probs_ref, att_ref, mid_ref, gm_ref, gh_ref, mlp_ref, valid_ref,
    g1_ref, g2_ref, bfc2_ref, wqkv_ref, wproj_ref, img_ref, cot_ref,
    lo_ref, gi_ref, dwp_ref, dwq_ref, vec_ref,
    gmid_ref, gatt_ref, gq_ref, gk_ref, gv_ref, gn_ref,
):
    step = pl.program_id(0)
    rows, width = x_ref.shape

    @pl.when(step == 0)
    def _():
        middle = mid_ref[...]
        valid = valid_ref[...] > 0
        mlp_out = jnp.where(valid, mlp_ref[...] + bfc2_ref[...].astype(F32), 0.0)
        block = middle + mlp_out
        kept = jnp.where(valid, block, 0.0)
        vec_ref[8:9] = jnp.sum(kept * kept, axis=0, keepdims=True)
        vec_ref[9:10] = jnp.sum(mlp_out * mlp_out, axis=0, keepdims=True)
        low = block.astype(BF16)
        for i in range(images):
            put = t_dot(sel_ref[i], low[i * slots : (i + 1) * slots])
            here = jnp.sum(sel_ref[i].astype(F32), axis=0, keepdims=True)
            lo_ref[i] = put.astype(BF16)
        scaled, inverse = norm_rows(middle)
        grad_hidden = gh_ref[...]
        vec_ref[0:1] = jnp.sum(grad_hidden * scaled, axis=0, keepdims=True)
        vec_ref[1:2] = jnp.sum(grad_hidden, axis=0, keepdims=True)
        gm = gm_ref[...].astype(F32)
        vec_ref[2:3] = jnp.sum(gm, axis=0, keepdims=True)
        grad_middle = gm + norm_back(grad_hidden * g2_ref[...], scaled, inverse)
        gmid_ref[...] = grad_middle
        grad_attn = grad_middle.astype(BF16)
        vec_ref[3:4] = jnp.sum(grad_attn.astype(F32), axis=0, keepdims=True)
        dwp_ref[...] = t_dot(att_ref[...], grad_attn).astype(BF16)
        gatt_ref[...] = dot_t(grad_attn, wproj_ref[...]).astype(BF16)
        gn_ref[...] = jnp.zeros_like(gn_ref)

    first = lax.broadcasted_iota(jnp.int32, (1, 2 * HEAD_DIM), 1) < HEAD_DIM
    zero = jnp.zeros((), BF16)
    scale = jnp.asarray(HEAD_DIM ** -0.5, BF16)
    pairs = width // 128 // groups
    for group in range(groups):

        @pl.when(step == group + 1)
        def _():
            base = group * pairs * 128

            @pl.loop(0, images)
            def _(i):
                here = pl.ds(pl.multiple_of(i * slots, 16), slots)
                for pair in range(pairs):
                    at = base + pair * 128
                    own = slice(pair * 128, pair * 128 + 128)
                    query = qkv_ref[here, at : at + 128]
                    key = qkv_ref[here, width + at : width + at + 128]
                    value = qkv_ref[here, 2 * width + at : 2 * width + at + 128]
                    grad_att = gatt_ref[here, at : at + 128]
                    gq = gk = gv = None
                    for half in range(2):
                        mine = first if half == 0 else jnp.logical_not(first)
                        low = probs_ref[i, 2 * (base // 128 + pair) + half]
                        probs = low.astype(F32)
                        g_mine = jnp.where(mine, grad_att, zero)
                        grad_probs = dot_t(g_mine, value).astype(BF16).astype(F32)
                        inner = jnp.sum(probs * grad_probs, axis=1, keepdims=True)
                        grad_scores = (probs * (grad_probs - inner)).astype(BF16) * scale
                        tv = t_dot(low, g_mine)
                        tq = dot(grad_scores, jnp.where(mine, key, zero))
                        tk = t_dot(grad_scores, jnp.where(mine, query, zero))
                        gq = tq if gq is None else gq + tq
                        gk = tk if gk is None else gk + tk
                        gv = tv if gv is None else gv + tv
                    gq_ref[here, own] = gq.astype(BF16)
                    gk_ref[here, own] = gk.astype(BF16)
                    gv_ref[here, own] = gv.astype(BF16)

            span = pairs * 128
            vec_ref[4:5, base : base + span] = jnp.sum(gq_ref[...].astype(F32), axis=0, keepdims=True)
            vec_ref[5:6, base : base + span] = jnp.sum(gv_ref[...].astype(F32), axis=0, keepdims=True)
            for part, ref in enumerate((gq_ref, gk_ref, gv_ref)):
                cols = slice(part * width + base, part * width + base + span)
                dwq_ref[:, cols] = t_dot(normed_ref[...], ref[...]).astype(BF16)
                gn_ref[...] += dot_t(ref[...], wqkv_ref[:, cols])

    @pl.when(step == groups + 1)
    def _():
        scaled, inverse = norm_rows(x_ref[...].astype(F32))
        grad_normed = gn_ref[...]
        vec_ref[6:7] = jnp.sum(grad_normed * scaled, axis=0, keepdims=True)
        vec_ref[7:8] = jnp.sum(grad_normed, axis=0, keepdims=True)
        change = gmid_ref[...] + norm_back(grad_normed * g1_ref[...], scaled, inverse)
        high = change.astype(BF16)
        rest = (change - high.astype(F32)).astype(BF16)
        for i in range(images):
            here = slice(i * slots, (i + 1) * slots)
            gi_ref[i] = t_dot(sel_ref[i], high[here]) + t_dot(sel_ref[i], rest[here])


def whole(shape):
    return pl.BlockSpec(shape, lambda *_: (0,) * len(shape), pipeline_mode=pl.Buffered(1))


def plain_device(
    images, keep_mask, ln1_gain, ln1_bias, w_qkv, bias_q, bias_v, w_proj, b_proj,
    ln2_gain, ln2_bias, w_fc1, b_fc1, w_fc2, b_fc2, cotangent,
):
    count, patches, width = images.shape
    slots = slots_of(patches)
    rows = count * slots
    heads = width // HEAD_DIM
    shard = w_fc1.shape[1]
    row = lambda v: v.reshape(1, -1)
    whole_w1 = lax.all_gather(w_fc1, "mlp")
    whole_w2 = lax.all_gather(w_fc2, "mlp")
    whole_b1 = lax.all_gather(b_fc1, "mlp").reshape(2, 1, shard)
    shape = jax.ShapeDtypeStruct
    limit = pltpu.CompilerParams(vmem_limit_bytes=60 * 2**20)
    per_image = lambda *tail: pl.BlockSpec((1,) + tail, lambda i: (i,) + (0,) * len(tail))
    per_rows = lambda cols: pl.BlockSpec((slots, cols), lambda i: (i, 0))
    sel, x, normed, qkv, probs, att, mid, hid, gm, sums = pl.pallas_call(
        functools.partial(forward_kernel, slots),
        grid=(count,),
        out_shape=(
            shape((count, slots, patches), BF16),
            shape((rows, width), BF16),
            shape((rows, width), BF16),
            shape((rows, 3 * width), BF16),
            shape((count, heads, slots, slots), BF16),
            shape((rows, width), BF16),
            shape((rows, width), F32),
            shape((rows, width), BF16),
            shape((rows, width), BF16),
            shape((count, 8, width), F32),
        ),
        in_specs=[
            whole((count, patches)), per_image(patches, width), per_image(patches, width),
            whole((width,)), whole((width,)), whole((width, 3 * width)), whole((width,)), whole((width,)),
            whole((width, width)), whole((width,)), whole((width,)), whole((width,)),
        ],
        out_specs=(
            per_image(slots, patches), per_rows(width), per_rows(width), per_rows(3 * width),
            per_image(heads, slots, slots), per_rows(width), per_rows(width), per_rows(width), per_rows(width),
            per_image(8, width),
        ),
        compiler_params=limit,
        name="attention_forward",
    )(
        keep_mask, images, cotangent, ln1_gain, ln1_bias, w_qkv, bias_q, bias_v, w_proj, b_proj, ln2_gain, ln2_bias,
    )
    chunk = 512 if shard % 512 == 0 else 256
    each = shard // chunk
    mlp_out, grad_hidden, dw1, dw2, db1 = pl.pallas_call(
        mlp_kernel,
        grid=(2 * each,),
        out_shape=(
            shape((rows, width), F32), shape((rows, width), F32),
            shape((2, width, shard), BF16), shape((2, shard, width), BF16), shape((2, 1, shard), F32),
        ),
        in_specs=[
            whole((rows, width)), whole((rows, width)),
            pl.BlockSpec((1, width, chunk), lambda c: (c // each, 0, c % each)),
            pl.BlockSpec((1, 1, chunk), lambda c: (c // each, 0, c % each)),
            pl.BlockSpec((1, chunk, width), lambda c: (c // each, c % each, 0)),
        ],
        out_specs=(
            whole((rows, width)), whole((rows, width)),
            pl.BlockSpec((1, width, chunk), lambda c: (c // each, 0, c % each)),
            pl.BlockSpec((1, chunk, width), lambda c: (c // each, c % each, 0)),
            pl.BlockSpec((1, 1, chunk), lambda c: (c // each, 0, c % each)),
        ),
        compiler_params=limit,
        name="mlp_both_ways",
    )(hid, gm, whole_w1, whole_b1, whole_w2)
    kept = jnp.sum(keep_mask, axis=1, keepdims=True)
    valid = (jnp.arange(slots, dtype=jnp.int32)[None, :] < kept).astype(F32).reshape(rows, 1)
    groups = 3
    span = width // groups
    low, put, dwp, dwq, vec = pl.pallas_call(
        functools.partial(backward_kernel, count, slots, groups),
        grid=(groups + 2,),
        out_shape=(
            shape((count, patches, width), BF16), shape((count, patches, width), F32),
            shape((width, width), BF16), shape((width, 3 * width), BF16), shape((16, width), F32),
        ),
        in_specs=[
            whole((count, slots, patches)), whole((rows, width)), whole((rows, width)), whole((rows, 3 * width)),
            whole((count, heads, slots, slots)), whole((rows, width)), whole((rows, width)), whole((rows, width)),
            whole((rows, width)), whole((rows, width)), whole((rows, 1)),
            whole((1, width)), whole((1, width)), whole((1, width)), whole((width, 3 * width)), whole((width, width)),
            pl.BlockSpec(memory_space=pl.ANY), pl.BlockSpec(memory_space=pl.ANY),
        ],
        out_specs=(
            whole((count, patches, width)), whole((count, patches, width)),
            whole((width, width)), whole((width, 3 * width)), whole((16, width)),
        ),
        scratch_shapes=[
            pltpu.VMEM((rows, width), F32), pltpu.VMEM((rows, width), BF16),
            pltpu.VMEM((rows, span), BF16), pltpu.VMEM((rows, span), BF16), pltpu.VMEM((rows, span), BF16),
            pltpu.VMEM((rows, width), F32),
        ],
        compiler_params=limit,
        name="attention_backward",
    )(
        sel, x, normed, qkv, probs, att, mid, gm, grad_hidden, mlp_out, valid,
        row(ln1_gain), row(ln2_gain), row(b_fc2), w_qkv, w_proj, images, cotangent,
    )
    kept_at = (keep_mask > 0)[:, :, None]
    layer_out = jnp.where(kept_at, low, images)
    grad_images = jnp.where(kept_at, put, cotangent.astype(F32))
    both = ("img", "mlp")
    place = lax.axis_index("mlp")
    dw1s = lax.psum_scatter(dw1.reshape(2 * width, shard), "mlp", scatter_dimension=0, tiled=True)
    dw2s = lax.psum_scatter(dw2.reshape(2 * shard, width), "mlp", scatter_dimension=0, tiled=True)
    s_w1, s_w2 = lax.psum((dw1s, dw2s), "img")
    s_wq, s_wp = lax.psum((dwq, dwp), both)
    vec, sums, s_b1 = lax.psum((vec, jnp.sum(sums, axis=0), db1.reshape(2, shard)), both)
    s_b1 = lax.dynamic_index_in_dim(s_b1, place, 0, keepdims=False)
    stream_sq, mlp_sq, attn_sq = jnp.sum(vec[8]), jnp.sum(vec[9]), jnp.sum(sums[0])
    root_means = jnp.sqrt(jnp.stack([stream_sq, attn_sq, mlp_sq]) / (sums[1, 0] * width))
    f = lambda v: v.astype(F32)
    return (
        layer_out, grad_images, vec[6], vec[7], f(s_wq), vec[4], vec[5], f(s_wp), vec[3], vec[0], vec[1],
        f(s_w1), s_b1, f(s_w2), vec[2], root_means,
    )


class Place:
    def __init__(self, deep, width):
        spot, self.core = lax.axis_index("img"), lax.axis_index("mlp")
        x, y, self.z = spot % 2, (spot // 2) % 2, spot // 4
        core = self.core
        self.bit1 = x * (1 - core) + y * core
        self.bit2 = y * (1 - core) + x * core
        step_x, step_y = 1 - 2 * x, 2 - 4 * y
        self.deep = deep
        self.other = {"mlp": 1 - core}
        self.peer1 = {"img": spot + step_x * (1 - core) + step_y * core}
        self.peer2 = {"img": spot + step_y * (1 - core) + step_x * core}
        self.peer_z = [{"img": ((self.z + k) % deep) * 4 + spot % 4} for k in range(1, deep)]
        self.half, self.quarter = width // 2, width // 4
        self.piece = width // 4 // deep
        self.half_at = self.bit1 * self.half
        self.half_off = (1 - self.bit1) * self.half
        self.quarter_at = self.half_at + self.bit2 * self.quarter
        self.quarter_off = self.half_at + (1 - self.bit2) * self.quarter

    def piece_at(self, z):
        return self.quarter_at + z * self.piece

    def everyone(self):
        return [self.other, self.peer1, self.peer2] + self.peer_z

    def greet(self):
        for peer in self.everyone():
            pl.semaphore_signal(pltpu.get_barrier_semaphore(), inc=1, device_id=peer, device_id_type=MESH)

    def all_here(self):
        pl.semaphore_wait(pltpu.get_barrier_semaphore(), len(self.everyone()))


def span(start, size):
    return pl.ds(pl.multiple_of(start, 16), size)


def remote(source, target, send_sem, recv_sem, peer):
    return pltpu.make_async_remote_copy(
        src_ref=source, dst_ref=target, send_sem=send_sem, recv_sem=recv_sem, device_id=peer, device_id_type=MESH
    )


def added(left, right):
    return (left.astype(F32) + right.astype(F32)).astype(BF16)


class Reduce:
    def __init__(self, place, partial, sending, total, got_core, got1, got2, got_z, send, recv, send_z, recv_z):
        self.place, self.partial, self.sending, self.total = place, partial, sending, total
        self.got_core, self.got1, self.got2, self.got_z = got_core, got1, got2, got_z
        self.send, self.recv, self.send_z, self.recv_z = send, recv, send_z, recv_z

    def copies(self, c, stage):
        p = self.place
        if stage == 0:
            return [remote(self.sending(c), self.got_core.at[c], self.send.at[c, 0], self.recv.at[c, 0], p.other)]
        total = self.total(c)
        if stage == 1:
            part = total.at[:, span(p.half_off, p.half), :]
            return [remote(part, self.got1.at[c], self.send.at[c, 1], self.recv.at[c, 1], p.peer1)]
        if stage == 2:
            part = total.at[:, span(p.quarter_off, p.quarter), :]
            return [remote(part, self.got2.at[c], self.send.at[c, 2], self.recv.at[c, 2], p.peer2)]
        made = []
        for k, peer in enumerate(p.peer_z):
            part = total.at[:, span(p.piece_at((p.z + k + 1) % p.deep), p.piece), :]
            made.append(remote(part, self.got_z.at[c, k], self.send_z.at[c, k], self.recv_z.at[c, k], peer))
        return made

    def begin(self, c, stage):
        for copy in self.copies(c, stage):
            copy.start()

    def arrive(self, c, stage):
        for copy in self.copies(c, stage):
            copy.wait_recv()

    def sent(self, c):
        for stage in range(4):
            for copy in self.copies(c, stage):
                copy.wait_send()

    def plane1(self, c):
        self.arrive(c, 0)
        total, partial, got = self.total(c), self.partial(c), self.got_core.at[c]
        total[...] = added(partial[...], got[...])
        self.begin(c, 1)

    def plane2(self, c):
        p = self.place
        self.arrive(c, 1)
        rows = span(p.half_at, p.half)
        total = self.total(c)
        total[:, rows, :] = added(total[:, rows, :], self.got1[c])
        self.begin(c, 2)

    def along_z(self, c):
        p = self.place
        self.arrive(c, 2)
        rows = span(p.quarter_at, p.quarter)
        total = self.total(c)
        total[:, rows, :] = added(total[:, rows, :], self.got2[c])
        self.begin(c, 3)

    def finish(self, c):
        p = self.place
        self.arrive(c, 3)
        rows = span(p.piece_at(p.z), p.piece)
        value = self.total(c)[:, rows, :].astype(F32)
        for k in range(p.deep - 1):
            value = value + self.got_z[c, k].astype(F32)
        return value.astype(BF16)


class Gather:
    def __init__(self, place, piece, result, mirror, local, send, recv, send_z, recv_z):
        self.place, self.piece, self.result, self.mirror, self.local = place, piece, result, mirror, local
        self.send, self.recv, self.send_z, self.recv_z = send, recv, send_z, recv_z

    def kept(self, c):
        p = self.place
        return pltpu.make_async_copy(
            self.piece(c), self.result(c).at[:, span(p.piece_at(p.z), p.piece), :], self.local.at[c]
        )

    def copies(self, c, stage, landing=False):
        p, result = self.place, self.result(c)
        if stage == 0:
            made = []
            for k, peer in enumerate(p.peer_z):
                z = (p.z - k - 1 + p.deep) % p.deep if landing else p.z
                target = result.at[:, span(p.piece_at(z), p.piece), :]
                made.append(remote(self.piece(c), target, self.send_z.at[c, k], self.recv_z.at[c, k], peer))
            return made
        if stage == 1:
            source = result.at[:, span(p.quarter_at, p.quarter), :]
            target = result.at[:, span(p.quarter_off if landing else p.quarter_at, p.quarter), :]
            return [remote(source, target, self.send.at[c, 0], self.recv.at[c, 0], p.peer2)]
        if stage == 2:
            source = result.at[:, span(p.half_at, p.half), :]
            target = result.at[:, span(p.half_off if landing else p.half_at, p.half), :]
            return [remote(source, target, self.send.at[c, 1], self.recv.at[c, 1], p.peer1)]
        return [remote(result, self.mirror(c) if landing else result, self.send.at[c, 2], self.recv.at[c, 2], p.other)]

    def begin(self, c, stage):
        for copy in self.copies(c, stage):
            copy.start()

    def arrive(self, c, stage):
        for copy in self.copies(c, stage, landing=True):
            copy.wait_recv()

    def along_z(self, c):
        self.kept(c).start()
        self.begin(c, 0)

    def plane2(self, c):
        self.kept(c).wait()
        self.arrive(c, 0)
        self.begin(c, 1)

    def plane1(self, c):
        self.arrive(c, 1)
        self.begin(c, 2)

    def across(self, c):
        self.arrive(c, 2)
        self.begin(c, 3)

    def sent(self, c):
        for stage in range(3 if self.mirror is None else 4):
            for copy in self.copies(c, stage):
                copy.wait_send()


def vec_slot(slot, width):
    return slice(slot // 2, slot // 2 + 1), slice(slot % 2 * width, slot % 2 * width + width)


def head_back(slots, i, q_ref, k_ref, v_ref, probs_ref, gatt_ref, gq_ref, gk_ref, gv_ref):
    first = lax.broadcasted_iota(jnp.int32, (1, 2 * HEAD_DIM), 1) < HEAD_DIM
    zero = jnp.zeros((), BF16)
    scale = jnp.asarray(HEAD_DIM ** -0.5, BF16)
    pairs = q_ref.shape[1] // 128
    here = pl.ds(pl.multiple_of(i * slots, 16), slots)
    for pair in range(pairs):
        own = slice(pair * 128, pair * 128 + 128)
        query, key, value = q_ref[here, own], k_ref[here, own], v_ref[here, own]
        grad_att = gatt_ref[here, own]
        gq = gk = gv = None
        for half in range(2):
            mine = first if half == 0 else jnp.logical_not(first)
            low = probs_ref[i, 2 * pair + half]
            probs = low.astype(F32)
            g_mine = jnp.where(mine, grad_att, zero)
            grad_probs = dot_t(g_mine, value).astype(BF16).astype(F32)
            inner = jnp.sum(probs * grad_probs, axis=1, keepdims=True)
            grad_scores = (probs * (grad_probs - inner)).astype(BF16) * scale
            tv = t_dot(low, g_mine)
            tq = dot(grad_scores, jnp.where(mine, key, zero))
            tk = t_dot(grad_scores, jnp.where(mine, query, zero))
            gq = tq if gq is None else gq + tq
            gk = tk if gk is None else gk + tk
            gv = tv if gv is None else gv + tv
        gq_ref[here, own] = gq.astype(BF16)
        gk_ref[here, own] = gk.astype(BF16)
        gv_ref[here, own] = gv.astype(BF16)


def mlp_staged_kernel(
    deep, images, slots, ticks,
    hid_ref, gm_ref, sums_ref, w1a_ref, w1b_ref, b1a_ref, b1b_ref, w2a_ref, w2b_ref, g2_ref, bfc2_ref,
    att_hbm, mid_hbm, sel_hbm, wproj_hbm, normed_hbm, qkv_hbm, probs_hbm, wqkv_hbm,
    red_ref, gmid_hbm, gatt_hbm, dwp_hbm, lo_hbm, vec_ref, early_ref, dwh_ref, gn_hbm,
    gmid_ref, gatt_ref, dwp_ref, lo_ref, give_sem,
    att_ref, mid_ref, sel_ref, wproj_ref, normed_ref, q_ref, k_ref, v_ref, probs_ref, wq_ref, wk_ref, wv_ref,
    gq_ref, gk_ref, gv_ref, fetch_sem,
    out_ref, gh_ref, bias_ref, give_ref, own_ref, got_core, got1, got2, got_z, send, recv, send_z, recv_z,
    b_local, b_send, b_recv, b_send_z, b_recv_z,
):
    step = pl.program_id(0)
    rows, width = hid_ref.shape
    place = Place(deep, width)
    panels = 4
    chunk = w1a_ref.shape[1]
    reduce = Reduce(
        place, lambda c: own_ref.at[c], lambda c: give_ref.at[c], lambda c: own_ref.at[c],
        got_core, got1, got2, got_z, send, recv, send_z, recv_z,
    )

    back = Gather(
        place, lambda c: red_ref.at[pl.ds(c * panels, panels)], lambda c: early_ref.at[pl.ds(c * panels, panels)],
        None, b_local, b_send, b_recv, b_send_z, b_recv_z,
    )
    early = early_ref.shape[0] // panels

    wide = q_ref.shape[1]
    thirds = [slice(part * width, part * width + wide) for part in range(3)]
    sources = [att_hbm, mid_hbm, sel_hbm, wproj_hbm, normed_hbm] + [qkv_hbm.at[:, cols] for cols in thirds]
    sources += [probs_hbm.at[:, 0 : probs_ref.shape[1]]] + [wqkv_hbm.at[:, cols] for cols in thirds]
    held = [att_ref, mid_ref, sel_ref, wproj_ref, normed_ref, q_ref, k_ref, v_ref, probs_ref, wq_ref, wk_ref, wv_ref]
    fetched = [
        pltpu.make_async_copy(source, target, fetch_sem.at[j]) for j, (source, target) in enumerate(zip(sources, held))
    ]

    def put_red(c):
        red_ref[pl.ds(c * panels, panels)] = reduce.finish(c)

    def half(w1_ref, b1, w2_ref, target, db_row):
        hid, gm = hid_ref[...], gm_ref[...]
        w1, w2 = w1_ref[...], w2_ref[...]
        pre = dot(hid, w1) + bias_ref[b1, pl.ds(step, 1)]
        act, slope = gelu_pair(pre)
        act = act.astype(BF16)
        grad_act = dot_t(gm, w2).astype(BF16).astype(F32)
        grad_pre = (grad_act * slope).astype(BF16)
        d2 = t_dot(act, gm).astype(BF16)
        for j in range(width // 128):
            at = j % 3 * chunk
            target[2 + j // 3, at : at + chunk, :] = d2[:, j * 128 : j * 128 + 128]
        d1 = t_dot(hid, grad_pre).astype(BF16)
        target[0] = d1[:, :128]
        target[1] = d1[:, 128:]
        cols = pl.ds(pl.multiple_of(step * chunk, chunk), chunk)
        vec_ref[pl.ds(db_row, 1), cols] = jnp.sum(grad_pre.astype(F32), axis=0, keepdims=True)
        out_ref[...] += dot(act, w2)
        gh_ref[...] += dot_t(grad_pre, w1)

    @pl.when(step == 0)
    def _():
        for copy in fetched:
            copy.start()
        place.greet()
        out_ref[...] = jnp.zeros_like(out_ref)
        gh_ref[...] = jnp.zeros_like(gh_ref)
        for side, ref in enumerate((b1a_ref, b1b_ref)):
            line = as_row(ref)
            for c in range(ticks):
                bias_ref[side, c : c + 1] = line[:, c * chunk : (c + 1) * chunk]
        place.all_here()

    @pl.when((step >= 1) & (step <= ticks))
    def _():
        reduce.plane1(step - 1)

    @pl.when(step == ticks)
    def _():
        back.plane1(0)

    @pl.when((step >= 2) & (step <= ticks))
    def _():
        reduce.plane2(step - 2)

    @pl.when((step >= 3) & (step <= ticks))
    def _():
        reduce.along_z(step - 3)

    @pl.when((step >= 4) & (step <= ticks))
    def _():
        put_red(step - 4)
        back.along_z(step - 4)

    @pl.when(step < ticks)
    def _():
        half(w1b_ref, 1, w2b_ref, give_ref.at[step], 7 - place.core)

    @pl.when(step == ticks - 1)
    def _():
        back.plane2(0)

    @pl.when(step < ticks)
    def _():
        reduce.begin(step, 0)
        half(w1a_ref, 0, w2a_ref, own_ref.at[step], 6 + place.core)

    def note(slot, value):
        at_row, at_col = vec_slot(slot, width)
        vec_ref[at_row, at_col] = value

    def column_sum(value):
        return jnp.sum(value, axis=0, keepdims=True)

    @pl.when(step == ticks)
    def _():
        for copy in fetched:
            copy.wait()
        stream = mlp_sq = jnp.zeros((1, width), F32)
        gain = shift = b_two = b_proj = jnp.zeros((1, width), F32)
        for i in range(images):
            here = slice(i * slots, i * slots + slots)
            sel = sel_ref[i]
            middle = mid_ref[here]
            valid = jnp.sum(sel.astype(F32), axis=1, keepdims=True) > 0
            mlp_out = jnp.where(valid, out_ref[here] + as_row(bfc2_ref), 0.0)
            block = middle + mlp_out
            kept = jnp.where(valid, block, 0.0)
            stream = stream + column_sum(kept * kept)
            mlp_sq = mlp_sq + column_sum(mlp_out * mlp_out)
            lo_ref[i] = t_dot(sel, block.astype(BF16)).astype(BF16)
            scaled, inverse = norm_rows(middle)
            grad_hidden = gh_ref[here]
            gain = gain + column_sum(grad_hidden * scaled)
            shift = shift + column_sum(grad_hidden)
            gm = gm_ref[here].astype(F32)
            b_two = b_two + column_sum(gm)
            grad_middle = gm + norm_back(grad_hidden * as_row(g2_ref), scaled, inverse)
            gmid_ref[here] = grad_middle
            grad_attn = grad_middle.astype(BF16)
            b_proj = b_proj + column_sum(grad_attn.astype(F32))
            gatt_ref[here] = grad_attn
            if i == 2:
                back.plane2(1)
        for slot, value in enumerate((gain, shift, b_two, b_proj)):
            note(slot, value)
        note(8, stream)
        note(9, mlp_sq)
        note(10, sum(sums_ref[i, 0:1] for i in range(images)))
        note(11, sum(sums_ref[i, 1:2] for i in range(images)))
        reduce.plane2(ticks - 1)
        reduce.along_z(ticks - 2)
        put_red(ticks - 3)
        back.plane1(1)
        back.plane2(2)
        grad_attn = gatt_ref[...]
        for part in range(3):
            cols = slice(part * width // 3, (part + 1) * width // 3)
            d = t_dot(att_ref[...], grad_attn[:, cols]).astype(BF16)
            dwp_ref[0, part] = d[:, :128]
            dwp_ref[1, part] = d[:, 128:]
        gatt_ref[...] = dot_t(grad_attn, wproj_ref[...]).astype(BF16)
        handed = [
            pltpu.make_async_copy(source, target, give_sem.at[j])
            for j, (source, target) in enumerate(
                ((gmid_ref, gmid_hbm), (lo_ref, lo_hbm), (dwp_ref, dwp_hbm), (gatt_ref, gatt_hbm))
            )
        ]
        for copy in handed:
            copy.start()

        @pl.loop(0, images)
        def _(i):
            @pl.when(i == 2)
            def _():
                reduce.along_z(ticks - 1)
                back.plane1(2)

            @pl.when(i == 4)
            def _():
                put_red(ticks - 2)

            head_back(slots, i, q_ref, k_ref, v_ref, probs_ref, gatt_ref, gq_ref, gk_ref, gv_ref)

        vec_ref[2:3, 0:wide] = column_sum(gq_ref[...].astype(F32))
        vec_ref[2:3, width : width + wide] = column_sum(gv_ref[...].astype(F32))
        total = None
        for part, (ref, w_ref) in enumerate(((gq_ref, wq_ref), (gk_ref, wk_ref), (gv_ref, wv_ref))):
            d = t_dot(normed_ref[...], ref[...]).astype(BF16)
            dwh_ref[0, part] = d[:, :128]
            dwh_ref[1, part] = d[:, 128:]
            term = dot_t(ref[...], w_ref[...])
            total = term if total is None else total + term
        gh_ref[...] = total
        keep_gn = pltpu.make_async_copy(gh_ref, gn_hbm, fetch_sem.at[0])
        keep_gn.start()
        put_red(ticks - 1)
        keep_gn.wait()
        for copy in handed:
            copy.wait()

        @pl.loop(0, ticks)
        def _(c):
            reduce.sent(c)

        @pl.loop(0, early)
        def _(c):
            back.arrive(c, 2)
            back.sent(c)


def attention_staged_kernel(
    deep, images, slots, groups, ticks,
    q_ref, k_ref, v_ref, probs_ref, gatt_ref, wq_ref, wk_ref, wv_ref, g1_ref, dwp_ref, dwh_ref, red_ref, vecin_ref,
    normed_hbm, x_hbm, gmid_hbm, sel_hbm, gn_hbm,
    mlp_ref, attn_ref, gi_hbm, vec_ref,
    gq_ref, gk_ref, gv_ref, gn_ref, stage_ref, total_ref, piece_ref, got_core, got1, got2, got_z,
    vsum_ref, vgot_ref, vz_ref,
    send, recv, send_z, recv_z, m_local, m_send, m_recv, m_send_z, m_recv_z,
    a_local, a_send, a_recv, a_send_z, a_recv_z, v_send, v_recv, v_send_z, v_recv_z,
    normed_ref, x_ref, gmid_ref, sel_ref, fetch_sem, gi_ref, gi_sem,
):
    step = pl.program_id(0)
    rows, width = x_ref.shape
    fetched = [
        pltpu.make_async_copy(source, target, fetch_sem.at[j])
        for j, (source, target) in enumerate(
            ((normed_hbm, normed_ref), (gn_hbm, gn_ref), (x_hbm, x_ref), (gmid_hbm, gmid_ref), (sel_hbm, sel_ref))
        )
    ]
    place = Place(deep, width)
    core = place.core
    polls = images + 2

    def partial_of(owner):
        def pick(c):
            if isinstance(c, int) and c < 2:
                return (dwp_ref, dwh_ref)[c].at[owner]
            return stage_ref.at[c - 2, owner]

        return pick

    reduce = Reduce(
        place, partial_of(core), partial_of(1 - core), lambda c: total_ref.at[c],
        got_core, got1, got2, got_z, send, recv, send_z, recv_z,
    )
    back = Gather(
        place, lambda c: piece_ref.at[c], lambda c: attn_ref.at[core, pl.ds(3 * c, 3)],
        lambda c: attn_ref.at[1 - core, pl.ds(3 * c, 3)], a_local, a_send, a_recv, a_send_z, a_recv_z,
    )
    late = mlp_ref.shape[0] // 4
    mlp = Gather(
        place, lambda c: red_ref.at[pl.ds(4 * (ticks - late + c), 4)], lambda c: mlp_ref.at[pl.ds(4 * c, 4)], None,
        m_local, m_send, m_recv, m_send_z, m_recv_z,
    )

    def turn(c):
        piece_ref[c] = reduce.finish(c)
        back.along_z(c)

    def do(name, c):
        return {
            "X": reduce.plane1, "Y": reduce.plane2, "Z": reduce.along_z, "R": turn,
            "ay": back.plane2, "ax": back.plane1, "ac": back.across,
            "my": mlp.plane2, "mx": mlp.plane1,
        }[name](c - (ticks - late) if name[0] == "m" else c)

    plan = {}
    for at, name, c in (
        (2, "X", 0), (2, "X", 1), (6, "Y", 0), (8, "my", 3), (9, "X", 2), (9, "Y", 1), (10, "Z", 0), (12, "my", 5),
        (13, "mx", 3), (15, "Z", 1), (16, "Y", 2), (16, "X", 3), (16, "R", 0), (18, "my", 4),
    ):
        plan.setdefault(at, []).append((name, c))
    tail = (
        ("Z", 2), ("R", 1), ("ay", 0), ("mx", 5), ("Y", 3), ("R", 2), ("ax", 0), ("ay", 1), ("Z", 3), ("ay", 2),
        ("ax", 1), ("ac", 0), ("R", 3), ("mx", 4), ("ax", 2), ("ac", 1), ("ay", 3), ("ac", 2), ("ax", 3),
        ("ac", 3),
    )

    def run(at, now):
        for moment, jobs in sorted(plan.items()):
            if moment < groups * polls and at(moment % polls):

                @pl.when(now == moment)
                def _(jobs=jobs):
                    for name, c in jobs:
                        do(name, c)

    wide = width // (groups + 1)

    @pl.when(step == 0)
    def _():
        for copy in fetched:
            copy.start()
        place.greet()
        vsum_ref[0] = vecin_ref[...]
        place.all_here()
        reduce.begin(0, 0)
        reduce.begin(1, 0)
        for c in range(late):
            mlp.along_z(c)

    @pl.when(step < groups)
    def _():
        @pl.loop(0, images)
        def _(i):
            run(lambda at: at < images, step * polls + i)
            head_back(slots, i, q_ref, k_ref, v_ref, probs_ref, gatt_ref, gq_ref, gk_ref, gv_ref)

        run(lambda at: at == images, step * polls + images)

        @pl.when(step == 0)
        def _():
            for copy in fetched[:2]:
                copy.wait()

        cols = pl.ds(pl.multiple_of((step + 1) * wide, wide), wide)
        shifted = pl.ds(pl.multiple_of(width + (step + 1) * wide, wide), wide)
        vsum_ref[0, 2:3, cols] = jnp.sum(gq_ref[...].astype(F32), axis=0, keepdims=True)
        vsum_ref[0, 2:3, shifted] = jnp.sum(gv_ref[...].astype(F32), axis=0, keepdims=True)
        for part, ref in enumerate((gq_ref, gk_ref, gv_ref)):
            d = t_dot(normed_ref[...], ref[...]).astype(BF16)
            stage_ref[step, 0, part] = d[:, :128]
            stage_ref[step, 1, part] = d[:, 128:]
        reduce.begin(step + 2, 0)
        for ref, w_ref in ((gq_ref, wq_ref), (gk_ref, wk_ref), (gv_ref, wv_ref)):
            gn_ref[...] += dot_t(ref[...], w_ref[...])
        run(lambda at: at == images + 1, step * polls + images + 1)

    def vec_copies(stage):
        if stage < 3:
            peer = (place.other, place.peer1, place.peer2)[stage]
            return [remote(vsum_ref.at[stage], vgot_ref.at[stage], v_send.at[stage], v_recv.at[stage], peer)]
        return [
            remote(vsum_ref.at[3], vz_ref.at[k], v_send_z.at[k], v_recv_z.at[k], peer)
            for k, peer in enumerate(place.peer_z)
        ]

    def vec_begin(stage):
        for copy in vec_copies(stage):
            copy.start()

    def vec_next(stage):
        for copy in vec_copies(stage):
            copy.wait_recv()
        if stage < 3:
            vsum_ref[stage + 1] = vsum_ref[stage] + vgot_ref[stage]
            vec_begin(stage + 1)

    @pl.when(step == groups)
    def _():
        for copy in fetched[2:]:
            copy.wait()
        g1 = as_row(g1_ref)
        gain = shift = jnp.zeros((1, width), F32)
        for i in range(images):
            for name, c in plan.get(groups * polls + i, ()):
                do(name, c)
            here = slice(i * slots, i * slots + slots)
            sel = sel_ref[i]
            scaled, inverse = norm_rows(x_ref[here].astype(F32))
            grad_normed = gn_ref[here]
            gain = gain + jnp.sum(grad_normed * scaled, axis=0, keepdims=True)
            shift = shift + jnp.sum(grad_normed, axis=0, keepdims=True)
            change = gmid_ref[here] + norm_back(grad_normed * g1, scaled, inverse)
            high = change.astype(BF16)
            rest = (change - high.astype(F32)).astype(BF16)
            gi_ref[i] = t_dot(sel, high) + t_dot(sel, rest)
        at_row, at_col = vec_slot(6, width)
        vsum_ref[0, at_row, at_col] = gain
        at_row, at_col = vec_slot(7, width)
        vsum_ref[0, at_row, at_col] = shift
        leave = pltpu.make_async_copy(gi_ref, gi_hbm, gi_sem.at[0])
        leave.start()
        vec_begin(0)
        for at, (name, c) in enumerate(tail):
            do(name, c)
            if at % 3 == 2 and at // 3 < 4:
                vec_next(at // 3)
        value = None
        for z in range(deep):
            mine = vsum_ref[3]
            from_k = [vz_ref[k] for k in range(deep - 1)]
            term = mine
            for k in range(deep - 1):
                term = jnp.where((place.z - k - 1 + deep) % deep == z, from_k[k], term)
            value = term if value is None else value + term
        vec_ref[...] = value
        leave.wait()
        for c in range(late):
            mlp.arrive(c, 2)
            mlp.sent(c)
        for c in range(groups + 2):
            back.arrive(c, 3)
            back.sent(c)
            reduce.sent(c)
        for stage in range(4):
            for copy in vec_copies(stage):
                copy.wait_send()


def finish_kernel(
    groups, early,
    first_ref, second_ref, attn_ref, low_ref, put_ref, img_ref, cot_ref, keep_ref, vec_ref,
    lo_ref, gi_ref, wq_ref, wp_ref, w1_ref, w2_ref, b1_ref, root_ref, *small_refs,
):
    step = pl.program_id(0)
    width = low_ref.shape[2]
    chunk = w1_ref.shape[1]
    for big_ref, mine in ((first_ref, step < early), (second_ref, step >= early)):

        @pl.when(mine)
        def _(big_ref=big_ref):
            for j in range(chunk // 128):
                w1_ref[:, j * 128 : j * 128 + 128] = big_ref[j].astype(F32)
            for j in range(width // 128):
                at = j % 3 * chunk
                w2_ref[:, j * 128 : j * 128 + 128] = big_ref[2 + j // 3, at : at + chunk].astype(F32)

    for owner in range(2):
        for j in range(3):
            at = (2 * j + owner) * 128
            wp_ref[:, at : at + 128] = attn_ref[owner, j].astype(F32)
            for group in range(groups):
                at = j * width + (2 * group + owner) * 128
                wq_ref[:, at : at + 128] = attn_ref[owner, 3 + 3 * group + j].astype(F32)

    @pl.when(step < keep_ref.shape[0])
    def _():
        keep = keep_ref[pl.ds(step, 1)].astype(F32)
        eight = jnp.broadcast_to(keep, (8, keep.shape[1])).astype(BF16)
        once = jnp.where(lax.broadcasted_iota(jnp.int32, (8, 128), 0) == 0, 1.0, 0.0).astype(BF16)
        kept = t_dot(eight, once)[:, 0:1] > 0.5
        lo_ref[0] = jnp.where(kept, low_ref[0], img_ref[0])
        gi_ref[0] = jnp.where(kept, put_ref[0], cot_ref[0].astype(F32))

    @pl.when(step == 0)
    def _():
        def line(slot):
            at_row, at_col = vec_slot(slot, width)
            return vec_ref[at_row, at_col]

        for slot, ref in enumerate(small_refs):
            ref[...] = line(slot).reshape(width)
        b1_ref[...] = vec_ref[pl.ds(6 + lax.axis_index("mlp"), 1)].reshape(2 * width)
        count = line(11)[:, 0:1]
        lane = lax.broadcasted_iota(jnp.int32, (1, 128), 1)
        sums = jnp.where(lane == 0, jnp.sum(line(8)), jnp.where(lane == 1, jnp.sum(line(10)), jnp.sum(line(9))))
        root_ref[...] = jnp.sqrt(sums / (count * width)).reshape(128)[:3]


def staged_device(
    deep, images, keep_mask, ln1_gain, ln1_bias, w_qkv, bias_q, bias_v, w_proj, b_proj,
    ln2_gain, ln2_bias, w_fc1, b_fc1, w_fc2, b_fc2, cotangent,
):
    count, patches, width = images.shape
    slots = slots_of(patches)
    rows = count * slots
    heads = width // HEAD_DIM
    shard = w_fc1.shape[1]
    row = lambda v: v.reshape(1, -1)
    shape = jax.ShapeDtypeStruct
    limit = 62 * 2**20
    any_space = pl.BlockSpec(memory_space=pl.ANY)
    per_image = lambda *tail: pl.BlockSpec((1,) + tail, lambda i: (i,) + (0,) * len(tail))
    per_rows = lambda cols: pl.BlockSpec((slots, cols), lambda i: (i, 0))
    dma = pltpu.SemaphoreType.DMA
    vmem = pltpu.VMEM
    stored = (
        shape((count, slots, patches), BF16), shape((rows, width), BF16), shape((rows, width), BF16),
        shape((rows, 3 * width), BF16), shape((count, heads, slots, slots), BF16), shape((rows, width), BF16),
        shape((rows, width), F32), shape((rows, width), BF16), shape((rows, width), BF16),
    )
    sums, sel, x, normed, qkv, probs, att, mid, hid, gm, far_w1, far_b1, far_w2 = pl.pallas_call(
        functools.partial(forward_staged_kernel, slots),
        grid=(1,),
        out_shape=(shape((count, 8, width), F32),) + stored + (
            shape((width, shard), BF16), shape((shard,), BF16), shape((shard, width), BF16),
        ),
        in_specs=[
            whole((count, patches)),
        ] + 7 * [whole((width,))] + 7 * [any_space],
        out_specs=(whole((count, 8, width)),) + 12 * (any_space,),
        scratch_shapes=[
            vmem((count, patches, width), BF16), vmem((count, patches, width), BF16),
            vmem((width, 3 * width), BF16), vmem((width, width), BF16),
        ]
        + [vmem(s.shape, s.dtype) for s in stored]
        + [dma((count, 2)), dma((2,)), dma((6,)), dma((count,)), dma((count, 2)), dma((3,)), dma((3,))],
        compiler_params=pltpu.CompilerParams(vmem_limit_bytes=limit, collective_id=0, has_side_effects=True),
        name="attention_forward",
    )(
        keep_mask, ln1_gain, ln1_bias, bias_q, bias_v, b_proj, ln2_gain, ln2_bias,
        images, cotangent, w_qkv, w_proj, w_fc1, b_fc1, w_fc2,
    )
    chunk = 256
    ticks = shard // chunk
    groups = 3
    piece = width // 4 // deep
    by_cols = lambda *lead: pl.BlockSpec(lead + (chunk,), lambda c: (0, c - c // ticks))
    by_rows = pl.BlockSpec((chunk, width), lambda c: (c - c // ticks, 0))
    early = ticks // 2
    wide = width // groups
    red, gmid, gatt, dwp, low, vec, first, dwh, gn = pl.pallas_call(
        functools.partial(mlp_staged_kernel, deep, count, slots, ticks),
        grid=(ticks + 1,),
        out_shape=(
            shape((4 * ticks, piece, 128), BF16), shape((rows, width), F32), shape((rows, width), BF16),
            shape((2, 3, width, 128), BF16), shape((count, patches, width), BF16), shape((8, 2 * width), F32),
            shape((4 * early, width, 128), BF16), shape((2, 3, width, 128), BF16), shape((rows, width), F32),
        ),
        in_specs=[
            whole((rows, width)), whole((rows, width)), whole((count, 8, width)),
            by_cols(width), by_cols(width), whole((shard,)), whole((shard,)), by_rows, by_rows,
            whole((width,)), whole((width,)),
        ] + 8 * [any_space],
        out_specs=(
            whole((4 * ticks, piece, 128)), any_space, any_space, any_space, any_space, whole((8, 2 * width)), any_space,
            whole((2, 3, width, 128)), any_space,
        ),
        scratch_shapes=[
            vmem((rows, width), F32), vmem((rows, width), BF16), vmem((2, 3, width, 128), BF16),
            vmem((count, patches, width), BF16), dma((4,)),
            pltpu.VMEM((rows, width), BF16), pltpu.VMEM((rows, width), F32), pltpu.VMEM((count, slots, patches), BF16),
            pltpu.VMEM((width, width), BF16), pltpu.VMEM((rows, width), BF16),
            pltpu.VMEM((rows, wide), BF16), pltpu.VMEM((rows, wide), BF16), pltpu.VMEM((rows, wide), BF16),
            pltpu.VMEM((count, heads // groups, slots, slots), BF16),
            pltpu.VMEM((width, wide), BF16), pltpu.VMEM((width, wide), BF16), pltpu.VMEM((width, wide), BF16),
            pltpu.VMEM((rows, wide), BF16), pltpu.VMEM((rows, wide), BF16), pltpu.VMEM((rows, wide), BF16), dma((12,)),
            pltpu.VMEM((rows, width), F32), pltpu.VMEM((rows, width), F32), pltpu.VMEM((2, 8, chunk), F32),
            pltpu.VMEM((ticks, 4, width, 128), BF16), pltpu.VMEM((ticks, 4, width, 128), BF16),
            pltpu.VMEM((ticks, 4, width, 128), BF16), pltpu.VMEM((ticks, 4, width // 2, 128), BF16),
            pltpu.VMEM((ticks, 4, width // 4, 128), BF16), pltpu.VMEM((ticks, deep - 1, 4, piece, 128), BF16),
            dma((ticks, 3)), dma((ticks, 3)), dma((ticks, deep - 1)), dma((ticks, deep - 1)),
            dma((early,)), dma((early, 2)), dma((early, 2)), dma((early, deep - 1)), dma((early, deep - 1)),
        ],
        compiler_params=pltpu.CompilerParams(vmem_limit_bytes=limit, collective_id=1, has_side_effects=True),
        name="mlp_both_ways",
    )(
        hid, gm, sums, w_fc1, far_w1, b_fc1, far_b1, w_fc2, far_w2, ln2_gain, b_fc2,
        att, mid, sel, w_proj, normed, qkv, probs, w_qkv,
    )
    chunks = groups + 1
    left = groups - 1
    now = lambda g: 1 + g - g // left
    third = lambda lead, part: pl.BlockSpec((lead, wide), lambda g: (0, part * groups + now(g)))
    late = ticks - early
    second, attn, put, vec = pl.pallas_call(
        functools.partial(attention_staged_kernel, deep, count, slots, left, ticks),
        grid=(left + 1,),
        out_shape=(
            shape((4 * late, width, 128), BF16), shape((2, 3 * chunks, width, 128), BF16),
            shape((count, patches, width), F32), shape((8, 2 * width), F32),
        ),
        in_specs=[
            third(rows, 0), third(rows, 1), third(rows, 2),
            pl.BlockSpec((count, heads // groups, slots, slots), lambda g: (0, now(g), 0, 0)),
            third(rows, 0), third(width, 0), third(width, 1), third(width, 2),
            whole((width,)), whole((2, 3, width, 128)), whole((2, 3, width, 128)), whole((4 * ticks, piece, 128)),
            whole((8, 2 * width)),
        ] + 5 * [any_space],
        out_specs=(any_space, any_space, any_space, whole((8, 2 * width))),
        scratch_shapes=[
            pltpu.VMEM((rows, wide), BF16), pltpu.VMEM((rows, wide), BF16), pltpu.VMEM((rows, wide), BF16),
            pltpu.VMEM((rows, width), F32),
            pltpu.VMEM((left, 2, 3, width, 128), BF16), pltpu.VMEM((chunks, 3, width, 128), BF16),
            pltpu.VMEM((chunks, 3, piece, 128), BF16), pltpu.VMEM((chunks, 3, width, 128), BF16),
            pltpu.VMEM((chunks, 3, width // 2, 128), BF16), pltpu.VMEM((chunks, 3, width // 4, 128), BF16),
            pltpu.VMEM((chunks, deep - 1, 3, piece, 128), BF16),
            pltpu.VMEM((4, 8, 2 * width), F32), pltpu.VMEM((3, 8, 2 * width), F32),
            pltpu.VMEM((deep - 1, 8, 2 * width), F32),
            dma((chunks, 3)), dma((chunks, 3)), dma((chunks, deep - 1)), dma((chunks, deep - 1)),
            dma((late,)), dma((late, 2)), dma((late, 2)), dma((late, deep - 1)), dma((late, deep - 1)),
            dma((chunks,)), dma((chunks, 3)), dma((chunks, 3)), dma((chunks, deep - 1)), dma((chunks, deep - 1)),
            dma((3,)), dma((3,)), dma((deep - 1,)), dma((deep - 1,)),
            pltpu.VMEM((rows, width), BF16), pltpu.VMEM((rows, width), BF16), pltpu.VMEM((rows, width), F32),
            pltpu.VMEM((count, slots, patches), BF16), dma((5,)), vmem((count, patches, width), F32), dma((1,)),
        ],
        compiler_params=pltpu.CompilerParams(vmem_limit_bytes=limit, collective_id=2, has_side_effects=True),
        name="attention_backward",
    )(
        qkv, qkv, qkv, probs, gatt, w_qkv, w_qkv, w_qkv, ln1_gain, dwp, dwh, red, vec, normed, x, gmid, sel, gn,
    )
    deal = width // ticks
    turn = lambda t: (t - t // count, 0, 0)
    layer_out, grad_images, s_wq, s_wp, s_w1, s_w2, s_b1, root_means, *small = pl.pallas_call(
        functools.partial(finish_kernel, groups, early),
        grid=(ticks,),
        out_shape=(
            shape((count, patches, width), BF16), shape((count, patches, width), F32),
            shape((width, 3 * width), F32), shape((width, width), F32), shape((width, shard), F32),
            shape((shard, width), F32), shape((shard,), F32), shape((3,), F32),
        ) + 8 * (shape((width,), F32),),
        in_specs=[
            pl.BlockSpec((4, width, 128), lambda t: (jnp.minimum(t, early - 1), 0, 0)),
            pl.BlockSpec((4, width, 128), lambda t: (jnp.maximum(t - early, 0), 0, 0)),
            pl.BlockSpec((2, 3 * chunks, deal, 128), lambda t: (0, 0, t, 0)),
            pl.BlockSpec((1, patches, width), turn), pl.BlockSpec((1, patches, width), turn),
            pl.BlockSpec((1, patches, width), turn), pl.BlockSpec((1, patches, width), turn),
            whole((count, patches)), whole((8, 2 * width)),
        ],
        out_specs=(
            pl.BlockSpec((1, patches, width), turn), pl.BlockSpec((1, patches, width), turn),
            pl.BlockSpec((deal, 3 * width), lambda t: (t, 0)), pl.BlockSpec((deal, width), lambda t: (t, 0)),
            pl.BlockSpec((width, chunk), lambda t: (0, t)), pl.BlockSpec((chunk, width), lambda t: (t, 0)),
            whole((shard,)), whole((3,)),
        ) + 8 * (whole((width,)),),
        compiler_params=pltpu.CompilerParams(vmem_limit_bytes=limit),
        name="results",
    )(first, second, attn, low, put, images, cotangent, keep_mask, vec)
    gain2, shift2, b_two, b_project, b_query, b_value, gain1, shift1 = small
    return (
        layer_out, grad_images, gain1, shift1, s_wq, b_query, b_value, s_wp, b_project, gain2, shift2,
        s_w1, s_b1, s_w2, b_two, root_means,
    )


def solution(mesh):
    rows, line = P(("img", "mlp"), None, None), P(("img", "mlp"), None)
    deep = mesh.shape["img"] // 4
    staged = mesh.shape["img"] == 4 * deep and mesh.shape["mlp"] == 2 and 1 < deep <= 4
    return jax.shard_map(
        functools.partial(staged_device, deep) if staged else plain_device,
        mesh=mesh,
        in_specs=(
            rows, line, P(), P(), P(), P(), P(), P(), P(), P(), P(),
            P(None, "mlp"), P("mlp"), P("mlp", None), P(), rows,
        ),
        out_specs=(
            rows, rows, P(), P(), P(), P(), P(), P(), P(), P(), P(),
            P(None, "mlp"), P("mlp"), P("mlp", None), P(), P(),
        ),
        check_vma=False,
    )
```
